32 devices in a mesh: grp: 8 (over z, core), dev: 4 (over y, x).
Axes of the slice: x: 2, y: 2, z: 4, core: 2. Of those that a mesh axis runs over, the one named last changes fastest.
Arguments:
- voxel_features: float32 [128, 64, 512], P(('grp', 'dev')), may hold values from -6 to 6
- fine_links: int32 [128, 26], P(('grp', 'dev')), may hold values from -1 to 127, as said below
- parent_codes: int32 [128], P(('grp', 'dev')), may hold values from 0 to 63, as said below
- coarse_links: int32 [64, 26], P(('grp', 'dev')), may hold values from -1 to 63, as said below
- fine_in_weight: float32 [64, 1728], replicated, may hold values from -0.15625 to 0.15625
- fine_in_bias: float32 [64], replicated, may hold values from -3 to 3
- down_weight: float32 [128, 64], replicated, may hold values from -0.75 to 0.75
- coarse_first_weight: float32 [128, 3456], replicated, may hold values from -0.109375 to 0.109375
- coarse_first_bias: float32 [128], replicated, may hold values from -3 to 3
- coarse_second_weight: float32 [128, 3456], replicated, may hold values from -0.109375 to 0.109375
- coarse_second_bias: float32 [128], replicated, may hold values from -3 to 3
- up_weight: float32 [64, 128], replicated, may hold values from -0.5 to 0.5
- fine_out_weight: float32 [64, 1728], replicated, may hold values from -0.15625 to 0.15625
- fine_out_bias: float32 [64], replicated, may hold values from -3 to 3
Outputs:
- refined: float32 [128, 64, 512], P(('grp', 'dev'))
The draws below stay inside these ranges and needn't reach their ends.
Inputs may be any that keep to these rules, and one draw needn't show every extreme that they name: `fine_links`: devices are numbered along grp then dev, device d holding bricks d * 4 to (d + 1) * 4 - 1. An entry is -1 or a brick from d * 4 - 2 to (d + 1) * 4 + 1 for a brick of device d, with 2 = 2. parent_codes[i] = 8 * 2 * owner + 8 * slot + octant: owner is the dev index, within the brick's group of 4 devices, of the device that holds the parent, slot the parent's slot there (0 to 1), and octant = 4 * a + 2 * b + c the child's octant. Within a group all codes differ; the number of slots in use differs from device to device, and some device of every group uses all 2. `coarse_links`: device d holds slots d * 2 to (d + 1) * 2 - 1. An entry is -1 or a slot from (d - 1) * 2 to (d + 2) * 2 - 1 for a slot of device d.
All inputs are finite; a program needn't handle non-finite values.
Results may differ from the reference program's by a relative error of at most 0.0001.
Values sent between devices are 32-bit elements; how exact they have to be, the bound alone decides.
A program may use at most 128 MiB of HBM per device.

```python
import jax
import jax.numpy as jnp
from jax import lax

CF = 64
CC = 128
BR = 4
CMAX = 2
HALO = 2
NB = 128
NCS = 64
N_GRP = 8
N_DEV = 4


def nearby_links(key, row_total, run_length, reach_low, reach_high):
    positions = jnp.arange(row_total, dtype=jnp.int32)
    first_slot = positions // run_length * run_length
    key_offset, key_keep = jax.random.split(key)
    offsets = jax.random.randint(key_offset, (row_total, 26), -reach_low, run_length + reach_high, dtype=jnp.int32)
    targets = jnp.clip(first_slot[:, None] + offsets, 0, row_total - 1)
    kept_mask = jax.random.randint(key_keep, (row_total, 26), 0, 10, dtype=jnp.int32) < 7
    return jnp.where(kept_mask, targets, -1).astype(jnp.int32)


def draw_fine_links(key, part):
    return nearby_links(jax.random.fold_in(key, 11), NB, BR, HALO, HALO)


def draw_coarse_links(key, part):
    return nearby_links(jax.random.fold_in(key, 12), NCS, CMAX, CMAX, CMAX)


def draw_parent_codes(key, part):
    key_live, key_pick, key_score = jax.random.split(jax.random.fold_in(key, 13), 3)
    fewest = (BR + 7) // 8
    live_slots = jax.random.randint(key_live, (N_GRP, N_DEV), fewest, CMAX + 1, dtype=jnp.int32)
    chosen = jax.random.randint(key_pick, (N_GRP, 1), 0, N_DEV, dtype=jnp.int32)
    live_slots = jnp.where(jnp.arange(N_DEV, dtype=jnp.int32)[None, :] == chosen, CMAX, live_slots)
    code_total = N_DEV * CMAX * 8
    code_ids = jnp.arange(code_total, dtype=jnp.int32)
    owners = code_ids // (CMAX * 8)
    slot_ids = code_ids // 8 % CMAX
    alive_codes = slot_ids[None, :] < live_slots[:, owners]
    scores = jax.random.randint(key_score, (N_GRP, code_total), 0, 2 ** 20, dtype=jnp.int32)
    scores = scores + jnp.where(alive_codes, 0, 2 ** 21)
    ranked = jnp.argsort(scores * code_total + code_ids[None, :], axis=1)
    return ranked[:, :N_DEV * BR].reshape(-1).astype(jnp.int32)


def levels(stream_key, dims, cuts, low, largest):
    loudness = 1.0
    for axis_at, blocks in cuts:
        steps = jax.random.uniform(jax.random.fold_in(jax.random.fold_in(stream_key, 6), axis_at), (blocks,), jnp.float32, low / len(cuts), largest / len(cuts))
        loudness = loudness * jnp.repeat(jnp.exp(steps), dims[axis_at] // blocks).reshape((-1,) + (1,) * (len(dims) - 1 - axis_at))
    return loudness


def scatter_about(rng, shape, spread, reach, cuts=(), kind=jnp.bfloat16):
    array = jax.random.normal(rng, shape, jnp.float32) * spread
    if len(cuts) > 0:
        array = levels(rng, shape, cuts, -0.22, 0.18) * array
    return jnp.clip(array, min=-reach, max=reach).astype(kind)


def setup_inputs(seed: int = 0) -> dict:
    key_list = jax.random.split(jax.random.key(seed), 15)
    voxel_features = scatter_about(key_list[0], (NB, CF, 512), 1.0, 6.0, ((0, 32),), jnp.float32)
    fine_links = draw_fine_links(jax.random.fold_in(key_list[14], 71), 0)
    parent_codes = draw_parent_codes(jax.random.fold_in(key_list[14], 71), 0)
    coarse_links = draw_coarse_links(jax.random.fold_in(key_list[14], 71), 0)
    fine_in_weight = scatter_about(key_list[4], (CF, 27 * CF), (27 * CF) ** -0.5, 0.15625, (), jnp.float32)
    fine_in_bias = scatter_about(key_list[5], (CF,), 0.5, 3.0, (), jnp.float32)
    down_weight = scatter_about(key_list[6], (CC, CF), CF ** -0.5, 0.75, (), jnp.float32)
    coarse_first_weight = scatter_about(key_list[7], (CC, 27 * CC), (27 * CC) ** -0.5, 0.109375, (), jnp.float32)
    coarse_first_bias = scatter_about(key_list[8], (CC,), 0.5, 3.0, (), jnp.float32)
    coarse_second_weight = scatter_about(key_list[9], (CC, 27 * CC), (27 * CC) ** -0.5, 0.109375, (), jnp.float32)
    coarse_second_bias = scatter_about(key_list[10], (CC,), 0.5, 3.0, (), jnp.float32)
    up_weight = scatter_about(key_list[11], (CF, CC), CC ** -0.5, 0.5, (), jnp.float32)
    fine_out_weight = scatter_about(key_list[12], (CF, 27 * CF), (27 * CF) ** -0.5, 0.15625, (), jnp.float32)
    fine_out_bias = scatter_about(key_list[13], (CF,), 0.5, 3.0, (), jnp.float32)
    return {"voxel_features": voxel_features, "fine_links": fine_links, "parent_codes": parent_codes, "coarse_links": coarse_links, "fine_in_weight": fine_in_weight, "fine_in_bias": fine_in_bias, "down_weight": down_weight, "coarse_first_weight": coarse_first_weight, "coarse_first_bias": coarse_first_bias, "coarse_second_weight": coarse_second_weight, "coarse_second_bias": coarse_second_bias, "up_weight": up_weight, "fine_out_weight": fine_out_weight, "fine_out_bias": fine_out_bias}


neighbour_offsets = [(step_x, step_y, step_z) for step_x in (-1, 0, 1) for step_y in (-1, 0, 1) for step_z in (-1, 0, 1) if (step_x, step_y, step_z) != (0, 0, 0)]
source_planes = {-1: slice(7, 8), 0: slice(0, 8), 1: slice(0, 1)}


def assemble(source, center, links):
    extent = source.shape[0]
    bricks = center.shape[0]
    channels = center.shape[1]
    bricks_ext = jnp.concatenate([source, jnp.zeros((1,) + source.shape[1:], source.dtype)], 0)
    bricks_ext = bricks_ext.reshape(extent + 1, channels, 8, 8, 8)
    picked = jnp.where(links < 0, extent, links).astype(jnp.int32)
    middle = center.reshape(bricks, channels, 8, 8, 8)
    slabs = []
    for step_x in (-1, 0, 1):
        rows = []
        for step_y in (-1, 0, 1):
            cells = []
            for step_z in (-1, 0, 1):
                if (step_x, step_y, step_z) == (0, 0, 0):
                    cells.append(middle)
                else:
                    column = neighbour_offsets.index((step_x, step_y, step_z))
                    planes = bricks_ext[:, :, source_planes[step_x], source_planes[step_y], source_planes[step_z]]
                    cells.append(planes[picked[:, column]])
            rows.append(jnp.concatenate(cells, axis=4))
        slabs.append(jnp.concatenate(rows, axis=3))
    return jnp.concatenate(slabs, axis=2)


def convolve(source, center, links, weight, biases):
    padded = assemble(source, center, links)
    bricks = center.shape[0]
    channels = center.shape[1]
    summed = jnp.zeros((bricks, weight.shape[0], 512), jnp.float32)
    for offset_x in range(3):
        windows = []
        for offset_y in range(3):
            for offset_z in range(3):
                windows.append(padded[:, :, offset_x:offset_x + 8, offset_y:offset_y + 8, offset_z:offset_z + 8].reshape(bricks, channels, 512))
        stacked = jnp.concatenate(windows, axis=1)
        kernel = weight[:, 9 * offset_x * channels:(9 * offset_x + 9) * channels]
        summed = summed + jnp.einsum("oc,bcv->bov", kernel, stacked, precision=lax.Precision.HIGHEST)
    return summed + biases[None, :, None]


def pooling(hidden):
    bricks = hidden.shape[0]
    channels = hidden.shape[1]
    return hidden.reshape(bricks, channels, 4, 2, 4, 2, 4, 2).sum(axis=(3, 5, 7)).reshape(bricks, channels * 64) * 0.125


def octants_to_bricks(pieces, channels):
    slots = pieces.shape[0] // 8
    return pieces.reshape(slots, 2, 2, 2, channels, 4, 4, 4).transpose(0, 4, 1, 5, 2, 6, 3, 7).reshape(slots, channels, 512)


def bricks_to_octants(cubes, channels):
    slots = cubes.shape[0]
    return cubes.reshape(slots, channels, 2, 4, 2, 4, 2, 4).transpose(0, 2, 4, 6, 1, 3, 5, 7).reshape(slots * 8, channels * 64)


def upsample(octants, channels):
    bricks = octants.shape[0]
    grown = jnp.broadcast_to(octants.reshape(bricks, channels, 4, 1, 4, 1, 4, 1), (bricks, channels, 4, 2, 4, 2, 4, 2))
    return grown.reshape(bricks, channels, 512)


def reference(voxel_features, fine_links, parent_codes, coarse_links, fine_in_weight, fine_in_bias, down_weight, coarse_first_weight, coarse_first_bias, coarse_second_weight, coarse_second_bias, up_weight, fine_out_weight, fine_out_bias):
    bricks = voxel_features.shape[0]
    channels = voxel_features.shape[1]
    hidden = jax.nn.silu(convolve(voxel_features, voxel_features, fine_links, fine_in_weight, fine_in_bias))
    pooled = pooling(hidden)
    groups = jnp.arange(bricks, dtype=jnp.int32) // (N_DEV * BR)
    parent_rows = (groups * (N_DEV * CMAX * 8) + parent_codes.astype(jnp.int32)).astype(jnp.int32)
    slot_total = coarse_links.shape[0]
    pieces = jnp.zeros((slot_total * 8, channels * 64), jnp.float32).at[parent_rows].set(pooled)
    coarse_in = octants_to_bricks(pieces, channels)
    coarse_base = jnp.einsum("oc,bcv->bov", down_weight, coarse_in, precision=lax.Precision.HIGHEST)
    coarse_first = jax.nn.silu(convolve(coarse_base, coarse_base, coarse_links, coarse_first_weight, coarse_first_bias))
    coarse_second = jax.nn.silu(convolve(coarse_first, coarse_first, coarse_links, coarse_second_weight, coarse_second_bias))
    lifted = jnp.einsum("oc,bcv->bov", up_weight, coarse_second, precision=lax.Precision.HIGHEST)
    upward = bricks_to_octants(lifted, channels)
    rising = upsample(upward[parent_rows], channels)
    blended = jax.nn.silu(hidden + rising)
    return voxel_features + convolve(blended, blended, fine_links, fine_out_weight, fine_out_bias)
```

```python
import functools

import jax
import jax.numpy as jnp
from jax import lax
from jax.experimental import pallas as pl
from jax.experimental.pallas import tpu as pltpu
from jax.sharding import PartitionSpec as P

F32 = jnp.float32
BF16 = jnp.bfloat16
MESH = pl.DeviceIdType.MESH
SIDE = 8
VOX = SIDE * SIDE * SIDE
HALO = 2
SURFACE = VOX - 6 * 6 * 6
LINE = 24
LIMIT = 62 * 1024 * 1024
CHUNKS = ((0, 96), (96, 96), (192, 104))

offsets = [(x, y, z) for x in (-1, 0, 1) for y in (-1, 0, 1) for z in (-1, 0, 1)]
columns = {o: k for k, o in enumerate(o for o in offsets if o != (0, 0, 0))}


def high_of(v):
    return v.astype(BF16).astype(F32)


def silu(v):
    return v / (1.0 + jnp.exp(-v))


def dot(a, b):
    return lax.dot_general(a, b, (((1,), (0,)), ((), ())), preferred_element_type=F32)


def first_half(v):
    return lax.broadcasted_iota(jnp.int32, v.shape, 1) < v.shape[1] // 2


def merged(a, b):
    return jnp.where(first_half(a), a, b)


def doubled(v):
    turned = pltpu.roll(v, v.shape[1] // 2, 1)
    return merged(v, turned), merged(turned, v)


def parted(v):
    high = high_of(v)
    return merged(high, v - high)


def fill(load, link, put, rims, put_rim):
    found = {o: link(o) for o in columns}

    def get(o, start, size=SIDE, stride=1):
        row, keep = found[o]
        return load(row, start, size, stride) * keep

    for px in range(SIDE + 2):
        dx = -1 if px == 0 else (1 if px == SIDE + 1 else 0)
        x = {-1: SIDE - 1, 0: px - 1, 1: 0}[dx]
        low = get((dx, -1, 0), 64 * x + 56)
        high = get((dx, 1, 0), 64 * x)
        middle = get((dx, 0, 0), 64 * x, 64) if dx else load(None, 64 * x, 64, 1)
        put(px, jnp.concatenate([low, middle, high], axis=0))
    for plane, dz in enumerate((-1, 1)):
        z = SIDE - 1 if dz < 0 else 0
        for px in range(SIDE + 2):
            dx = -1 if px == 0 else (1 if px == SIDE + 1 else 0)
            x = {-1: SIDE - 1, 0: px - 1, 1: 0}[dx]
            rims[plane, px * LINE + 8 : px * LINE + 16] = get((dx, 0, dz), 64 * x + z, SIDE, 8)
            if dx:
                for dy in (-1, 1):
                    y = SIDE - 1 if dy < 0 else 0
                    at = px * LINE + (7 if dy < 0 else 16)
                    rims[plane, at : at + 1] = get((dx, dy, dz), 64 * x + 8 * y + z, 1)
        for dy in (-1, 1):
            y = SIDE - 1 if dy < 0 else 0
            at = LINE + (7 if dy < 0 else 16)
            rims[plane, pl.ds(at, SIDE, stride=LINE)] = get((0, dy, dz), 8 * y + z, SIDE, 64)
    for j in range(3):
        for px in range(SIDE + 2):
            at = px * LINE + 7 + j
            put_rim(j, px, jnp.concatenate([rims[0, at : at + 8], rims[1, at : at + 8]], axis=0))


def stacked(even, odd, edge):
    taps = []
    for i in range(3):
        for j in range(3):
            main = odd[i : i + 8] if j == 1 else even[i : i + 8, 8 * j : 8 * j + 64]
            rim = edge[j, i : i + 8]
            taps.append(jnp.concatenate([main.reshape(VOX, 128), rim.reshape(128, 128)], axis=0))
    return jnp.concatenate(taps, axis=1)


def shifted_sum(blocks, down, up):
    before, here, after = blocks
    down[8 : VOX + 8] = before[:VOX]
    up[8 : VOX + 8] = after[:VOX]
    for x in range(SIDE):
        rim = VOX + 16 * x
        down[pl.ds(7 + 64 * x, SIDE, stride=8)] = before[rim : rim + 8]
        up[pl.ds(16 + 64 * x, SIDE, stride=8)] = after[rim + 8 : rim + 16]
    return down[7 : VOX + 7] + here[:VOX] + up[9 : VOX + 9]


def fine_matrix(weight, matrix):
    w = weight[...]
    high = high_of(w)
    both = jnp.concatenate([high, w - high], axis=0).T.astype(BF16)
    for tap in range(27):
        rows, cols = tap // 3 * 128, tap % 3 * 128
        block = both[64 * tap : 64 * tap + 64]
        matrix[rows : rows + 64, cols : cols + 128] = block
        matrix[rows + 64 : rows + 128, cols : cols + 128] = block


def coarse_matrix(weight, matrix):
    for tap in range(27):
        rows, cols = tap // 3 * 128, tap % 3 * 128
        block = weight[:, 128 * tap : 128 * tap + 128].T
        high = high_of(block)
        matrix[rows : rows + 128, cols : cols + 128] = high.astype(BF16)
        matrix[rows : rows + 128, 384 + cols : 384 + cols + 128] = (block - high).astype(BF16)


def linker(links, brick, start, own, rows):
    def link(o):
        there = links[brick, columns[o]]
        there_is = there >= 0
        row = jnp.where(there_is, jnp.clip(there - start, 0, rows - 1), own)
        return row, jnp.where(there_is, 1.0, 0.0).astype(F32)

    return link


def loader(parts, own):
    def load(row, start, size, stride):
        row = own if row is None else row
        if stride == 1:
            return parts[row, start : start + size]
        return parts[row, pl.ds(start, size, stride=stride)]

    return load


def fine_conv(parts, own, start, links, brick, scratch, matrix):
    even, odd, edge, rims, down, up = scratch

    def put(px, v):
        even[px] = v.astype(BF16)
        odd[px] = v[8:72].astype(BF16)

    def put_rim(j, px, v):
        edge[j, px] = v.astype(BF16)

    fill(loader(parts, own), linker(links, brick, start, own, parts.shape[0]), put, rims, put_rim)
    sums = dot(stacked(even, odd, edge), matrix[...])
    out = shifted_sum([sums[:, 128 * k : 128 * k + 128] for k in range(3)], down, up)
    return out + pltpu.roll(out, 64, 1)


def coarse_conv(parts, own, start, links, brick, scratch, matrix):
    even, odd, edge, rims, down, up = scratch

    def put(px, v):
        high = v.astype(BF16)
        low = (v - high.astype(F32)).astype(BF16)
        for part, value in enumerate((high, low)):
            even[part, px] = value
        middle = v[8:72]
        high = middle.astype(BF16)
        odd[0, px] = high
        odd[1, px] = (middle - high.astype(F32)).astype(BF16)

    def put_rim(j, px, v):
        high = v.astype(BF16)
        edge[0, j, px] = high
        edge[1, j, px] = (v - high.astype(F32)).astype(BF16)

    fill(loader(parts, own), linker(links, brick, start, own, parts.shape[0]), put, rims, put_rim)
    tops = dot(stacked(even.at[0], odd.at[0], edge.at[0]), matrix[...])
    rests = dot(stacked(even.at[1], odd.at[1], edge.at[1]), matrix[:, 0:384])
    cut = lambda v, at: v[:, 128 * at : 128 * at + 128]
    blocks = [cut(tops, k) + cut(tops, 3 + k) + cut(rests, k) for k in range(3)]
    return shifted_sum(blocks, down, up)


def surface_spots():
    spots = [(0, 0, 64, 1), (64, 448, 64, 1)]
    for x in range(1, 7):
        at = 128 + (x - 1) * 16
        spots += [(at, 64 * x, 8, 1), (at + 8, 64 * x + 56, 8, 1)]
    for x in range(1, 7):
        at = 224 + (x - 1) * 12
        spots += [(at, 64 * x + 8, 6, 8), (at + 6, 64 * x + 15, 6, 8)]
    return spots


def pack(get, wire):
    for at, start, size, stride in surface_spots():
        wire[at : at + size] = get(pl.ds(start, size, stride=stride) if stride > 1 else pl.ds(start, size))


def unpack(wire, brick):
    for at, start, size, stride in surface_spots():
        spot = pl.ds(start, size, stride=stride) if stride > 1 else pl.ds(start, size)
        brick[spot] = wire[at : at + size]


def unpack_pair(wire, scratch, first, second):
    a, b = doubled(wire)
    scratch[0] = parted(a)
    scratch[1] = parted(b)
    unpack(scratch.at[0], first)
    unpack(scratch.at[1], second)


def pool(v, scratch):
    lines = v.reshape(4, 2, 4, 2, SIDE, 128)
    sums = (lines[:, 0, :, 0] + lines[:, 0, :, 1]) + (lines[:, 1, :, 0] + lines[:, 1, :, 1])
    scratch[...] = sums.reshape(128, 128)
    total = scratch[pl.ds(0, 64, stride=2)] + scratch[pl.ds(1, 64, stride=2)]
    return total * 0.125


def place_piece(wire, octant, brick):
    a, b, c = octant // 4, octant // 2 % 2, octant % 2
    for half, v in enumerate(doubled(wire)):
        v = parted(v)
        for xx in range(2):
            for y in range(4):
                at = (4 * a + xx + 2 * half) * 64 + (4 * b + y) * 8 + 4 * c
                rows = xx * 16 + y * 4
                brick[at : at + 4] = v[rows : rows + 4]


def take_pieces(v, pieces):
    for a in range(2):
        for b in range(2):
            for xx in range(2):
                for y in range(4):
                    at = (4 * a + xx) * 64 + (4 * b + y) * 8
                    line = merged(v[at : at + 8], v[at + 128 : at + 136])
                    rows = xx * 16 + y * 4
                    for c in range(2):
                        pieces[4 * a + 2 * b + c, rows : rows + 4] = line[4 * c : 4 * c + 4]


def grow(piece, scratch):
    for half, v in enumerate(doubled(piece)):
        for xx in range(2):
            for y in range(2):
                rows = v[xx * 16 + y * 8 : xx * 16 + y * 8 + 8]
                at = ((2 * half + xx) * 2 + y) * 16
                scratch[pl.ds(at, 8, stride=2)] = rows
                scratch[pl.ds(at + 1, 8, stride=2)] = rows
    lines = scratch[...].reshape(4, 1, 4, 1, SIDE, 128)
    return jnp.broadcast_to(lines, (4, 2, 4, 2, SIDE, 128)).reshape(VOX, 128)


def step_kernel(
    x_any, fine_links, own_codes, coarse_links, in_any, in_bias, down_weight, one_any, one_bias, two_any, two_bias,
    up_weight, out_any, out_bias,
    out,
    x, in_weight, one_weight, two_weight, out_weight, loads,
    matrix, last_matrix, one_matrix, two_matrix,
    even, odd, edge, wide_even, wide_odd, wide_edge, rims, shift_down, shift_up,
    parts, turned, hidden, halves, small, grown,
    x_send, x_halo, hidden_send, hidden_halo,
    code_block, codes, code_table, table, code_scalars, table_scalars,
    pooled, placed, base, first,
    first_send, first_halo, lifted, wanted, window, low_window, high_window,
    local_sems, send_x, recv_x, send_hidden, recv_hidden, send_codes, recv_codes, send_pooled, recv_pooled,
    send_first, recv_first, send_relay, recv_relay, send_wanted, recv_wanted,
):
    group, member = lax.axis_index("grp"), lax.axis_index("dev")
    groups, members = lax.axis_size("grp"), lax.axis_size("dev")
    position = group * members + member
    whole = groups * members
    count, slots = fine_links.shape[0], coarse_links.shape[0]
    pairs = count // 2
    relayed = members == 4
    has_left, has_right = position > 0, position < whole - 1
    has_low, has_high = group > 0, group < groups - 1
    is_first, is_last = member == 0, member == members - 1
    left_at = (jnp.maximum(position - 1, 0) // members, (position + members - 1) % members)
    right_at = (jnp.minimum(position + 1, whole - 1) // members, (position + 1) % members)
    low_at = (jnp.maximum(group - 1, 0), members - 1)
    high_at = (jnp.minimum(group + 1, groups - 1), 0)
    always = position >= 0

    def fetch(k, source, target):
        return pltpu.make_async_copy(source, target, loads.at[k])

    fetches = [
        fetch(0, x_any, x), fetch(1, in_any, in_weight), fetch(2, one_any, one_weight),
        fetch(3, two_any, two_weight), fetch(4, out_any, out_weight),
    ]
    for copy in fetches:
        copy.start()

    barrier = pltpu.get_barrier_semaphore()

    def greet(where):
        pl.semaphore_signal(barrier, inc=1, device_id=where, device_id_type=MESH)

    pl.when(has_left)(lambda: greet(left_at))
    pl.when(has_right)(lambda: greet(right_at))
    for k in range(1, members):
        greet((group, (member + k) % members))
    for k in range(members):
        pl.when(is_first & has_low)(lambda k=k: greet((low_at[0], k)))
        pl.when(is_last & has_high)(lambda k=k: greet((high_at[0], k)))

    def remote(src, dst, send, recv, where):
        return pltpu.make_async_remote_copy(
            src_ref=src, dst_ref=dst, send_sem=send, recv_sem=recv, device_id=where, device_id_type=MESH
        )

    row = lax.broadcasted_iota(jnp.int32, (SIDE, 128), 0)
    block = jnp.full((SIDE, 128), -1, jnp.int32)
    for i in range(count):
        block = jnp.where(row == i, own_codes[i], block)
    code_block[...] = block
    codes[members + member] = block
    fetches[0].wait()
    for pair in range(pairs):
        turned[pair] = x[2 * pair : 2 * pair + 2].reshape(128, VOX).T
    pack(lambda spot: turned[0, spot], x_send.at[0])
    pack(lambda spot: turned[pairs - 1, spot], x_send.at[1])
    pl.semaphore_wait(
        barrier,
        jnp.where(has_left, 1, 0) + jnp.where(has_right, 1, 0) + (members - 1)
        + jnp.where(has_low, 1, 0) + jnp.where(has_high, 1, 0),
    )

    def halo_copies(source, halo, send, recv):
        to_left = remote(source.at[0], halo.at[1], send.at[0], recv.at[1], left_at)
        to_right = remote(source.at[1], halo.at[0], send.at[1], recv.at[0], right_at)
        return to_left, to_right

    def start_halo(copies):
        pl.when(has_left)(copies[0].start)
        pl.when(has_right)(copies[1].start)

    def end_halo(copies):
        pl.when(has_left)(copies[1].wait_recv)
        pl.when(has_right)(copies[0].wait_recv)

    def end_halo_sends(copies):
        pl.when(has_left)(copies[0].wait_send)
        pl.when(has_right)(copies[1].wait_send)

    def shared_copies(source, at, send, recv):
        near = [
            remote(source, at(members + member), send.at[k], recv.at[members + member], (group, (member + k) % members))
            for k in range(1, members)
        ]
        to_high = remote(source, at(member), send.at[0], recv.at[member], high_at)
        to_low = remote(source, at(2 * members + member), send.at[members], recv.at[2 * members + member], low_at)
        return near, to_high, to_low

    def start_shared(copies):
        near, to_high, to_low = copies
        for copy in near:
            copy.start()
        pl.when(has_high)(to_high.start)
        pl.when(has_low)(to_low.start)

    def end_shared(source, at, send, recv):
        for k in range(1, members):
            other = (member + k) % members
            remote(source, at(members + other), send.at[k], recv.at[members + other], (group, other)).wait_recv()
        for k in range(members):
            from_low = remote(source, at(k), send.at[0], recv.at[k], low_at)
            from_high = remote(source, at(2 * members + k), send.at[0], recv.at[2 * members + k], high_at)
            pl.when(is_first & has_low)(from_low.wait_recv)
            pl.when(is_last & has_high)(from_high.wait_recv)

    def end_shared_sends(copies):
        near, to_high, to_low = copies
        for copy in near:
            copy.wait_send()
        pl.when(has_high)(to_high.wait_send)
        pl.when(has_low)(to_low.wait_send)

    x_copies = halo_copies(x_send, x_halo, send_x, recv_x)
    start_halo(x_copies)
    code_at = lambda k: codes.at[k]
    code_copies = shared_copies(code_block, code_at, send_codes, recv_codes)
    start_shared(code_copies)

    fetches[1].wait()
    fine_matrix(in_weight, matrix)
    for pair in range(pairs):
        for one, v in enumerate(doubled(turned[pair])):
            parts[HALO + 2 * pair + one] = parted(v)
    end_shared(code_block, code_at, send_codes, recv_codes)
    lane = lax.broadcasted_iota(jnp.int32, (SIDE, 128), 1)
    table_rows = jnp.full((SIDE, 128), -1, jnp.int32)
    for near in range(3):
        there = position + near - 1
        valid = (there >= 0) & (there < whole)
        there = jnp.where(valid, there, position)
        there_group = there // members
        there_member = there - there_group * members
        band = there_group - group + 1
        spot = jnp.where(valid, lane, -1000) + there_member * slots * 8
        best = jnp.full((SIDE, 128), -1, jnp.int32)
        for k in range(members):
            match = (codes[band * members + k] == spot) & (row < count) & (lane < slots * 8)
            best = jnp.maximum(best, jnp.where(match, (band * members + k) * count + row, -1))
        top = jnp.max(best, axis=0, keepdims=True)
        table_rows = jnp.where(row == near, top, table_rows)
    code_table[...] = codes[pl.ds(members, members)]
    table[...] = table_rows
    to_table = pltpu.make_async_copy(table, table_scalars, local_sems.at[0])
    to_codes = pltpu.make_async_copy(code_table, code_scalars, local_sems.at[1])
    to_table.start()
    to_codes.start()
    fetches[2].wait()
    coarse_matrix(one_weight, one_matrix)
    fetches[3].wait()
    coarse_matrix(two_weight, two_matrix)
    fetches[4].wait()
    fine_matrix(out_weight, last_matrix)
    to_table.wait()
    to_codes.wait()

    fine_start = position * count - HALO
    end_halo(x_copies)
    for side, at in ((0, 0), (1, HALO + count)):
        unpack_pair(x_halo[side], halves, parts.at[at], parts.at[at + 1])
    fine_scratch = (even, odd, edge, rims, shift_down, shift_up)
    two = lambda bias: jnp.concatenate([bias[...], bias[...]], axis=1)
    in_both = two(in_bias)

    def pooled_at(i):
        return lambda k: pooled.at[k, i]

    def pooled_copies(i):
        return shared_copies(pooled.at[members + member, i], pooled_at(i), send_pooled.at[i], recv_pooled.at[i])

    def first_step(i, carry):
        v = silu(fine_conv(parts, HALO + i, fine_start, fine_links, i, fine_scratch, matrix) + in_both)
        means = pool(v, small)
        pooled[members + member, i] = merged(means[0:32], means[32:64])
        hidden[i] = v
        start_shared(pooled_copies(i))
        return carry

    lax.fori_loop(0, count, first_step, 0)
    pack(lambda spot: merged(hidden[0, spot], hidden[1, spot]), hidden_send.at[0])
    pack(lambda spot: merged(hidden[count - 2, spot], hidden[count - 1, spot]), hidden_send.at[1])
    hidden_copies = halo_copies(hidden_send, hidden_halo, send_hidden, recv_hidden)
    start_halo(hidden_copies)

    turned_down = down_weight[...].T
    down_high = high_of(turned_down)
    down_both = jnp.concatenate([down_high, turned_down - down_high], axis=1)
    down_matrix = jnp.concatenate([down_both, down_both], axis=0).astype(BF16)
    for i in range(count):
        end_shared(pooled.at[members + member, i], pooled_at(i), send_pooled.at[i], recv_pooled.at[i])

    def base_step(slot, carry):
        for octant in range(8):
            which = table_scalars[slot // slots, slot % slots * 8 + octant]
            there_is = which >= 0
            which = jnp.where(there_is, jnp.minimum(which, 3 * members * count - 1), (members + member) * count)
            keep = jnp.where(there_is, 1.0, 0.0).astype(F32)
            place_piece(pooled[which // count, which % count] * keep, octant, placed)
        sums = dot(placed[...].astype(BF16), down_matrix)
        base[slot] = sums[:, 0:128] + sums[:, 128:256]
        return carry

    lax.fori_loop(0, 3 * slots, base_step, 0)
    coarse_start = (position - 1) * slots
    wide_scratch = (wide_even, wide_odd, wide_edge, rims, shift_down, shift_up)

    if relayed:
        parity = member % 2
        x_at = (group, member + 1 - 2 * parity)
        relay_group = group + jnp.where(member == 1, -1, 0) + jnp.where(member == 2, 1, 0)
        relays_out = (relay_group >= 0) & (relay_group < groups)
        relays_in = jnp.where(is_first, has_low, True) & jnp.where(is_last, has_high, True)
        relay_at = (jnp.clip(relay_group, 0, groups - 1), (member + 2) % members)

        def direct(i, c):
            at, rows = CHUNKS[c]
            return remote(
                first_send.at[i, pl.ds(at, rows)], first_halo.at[parity, i, pl.ds(at, rows)],
                send_first.at[i, c], recv_first.at[i, c], x_at,
            )

        def came(i, c):
            at, rows = CHUNKS[c]
            return remote(
                first_send.at[i, pl.ds(at, rows)], first_halo.at[1 - parity, i, pl.ds(at, rows)],
                send_first.at[i, c], recv_first.at[i, c], x_at,
            )

        def relay(i, c):
            at, rows = CHUNKS[c]
            return remote(
                first_halo.at[1 - parity, i, pl.ds(at, rows)], first_halo.at[parity, i, pl.ds(at, rows)],
                send_relay.at[i, c], recv_relay.at[i, c], relay_at,
            )

        def start_first(i):
            for c in range(len(CHUNKS)):
                direct(i, c).start()

        def end_first():
            for i in range(slots):
                for c in range(len(CHUNKS)):
                    came(i, c).wait_recv()
                    pl.when(relays_out)(relay(i, c).start)
            for i in range(slots):
                for c in range(len(CHUNKS)):
                    pl.when(relays_in)(relay(i, c).wait_recv)

        def end_first_sends():
            for i in range(slots):
                for c in range(len(CHUNKS)):
                    direct(i, c).wait_send()
                    pl.when(relays_out)(relay(i, c).wait_send)
    else:

        def sides(i):
            to_left = remote(first_send.at[i], first_halo.at[1, i], send_first.at[i, 0], recv_first.at[i, 1], left_at)
            to_right = remote(first_send.at[i], first_halo.at[0, i], send_first.at[i, 1], recv_first.at[i, 0], right_at)
            return to_left, to_right

        def start_first(i):
            start_halo(sides(i))

        def end_first():
            for i in range(slots):
                end_halo(sides(i))

        def end_first_sends():
            for i in range(slots):
                end_halo_sends(sides(i))

    def second_step(i, carry):
        v = silu(coarse_conv(base, slots + i, coarse_start, coarse_links, i, wide_scratch, one_matrix) + one_bias[...])
        first[slots + i] = v
        pack(lambda spot: first[slots + i, spot], first_send.at[i])
        start_first(i)
        return carry

    lax.fori_loop(0, slots, second_step, 0)
    turned_up = up_weight[...].T
    up_high = high_of(turned_up)
    up_both = jnp.concatenate([up_high, turned_up - up_high], axis=1)
    up_matrix = jnp.concatenate([up_both, up_both], axis=0).astype(BF16)
    end_first()
    for side, at in ((0, 0), (1, 2 * slots)):
        for i in range(slots):
            unpack(first_halo.at[side, i], first.at[at + i])

    def third_step(i, carry):
        v = silu(coarse_conv(first, slots + i, coarse_start, coarse_links, i, wide_scratch, two_matrix) + two_bias[...])
        high = v.astype(BF16)
        low = (v - high.astype(F32)).astype(BF16)
        sums = dot(jnp.concatenate([high, low], axis=1), up_matrix)
        take_pieces(sums + pltpu.roll(sums, 64, 1), lifted.at[pl.ds(i * 8, 8)])
        return carry

    lax.fori_loop(0, slots, third_step, 0)
    bricks = members * count
    zeros = jnp.zeros((HALO,) + wanted.shape[1:], F32)
    wanted[0:HALO] = zeros
    wanted[HALO + bricks :] = zeros

    def choose(j, carry):
        code = code_scalars[j // count, j % count, 0] - member * slots * 8
        mine = (code >= 0) & (code < slots * 8)
        keep = jnp.where(mine, 1.0, 0.0).astype(F32)
        wanted[HALO + j] = lifted[jnp.where(mine, code, 0)] * keep
        return carry

    lax.fori_loop(0, bricks, choose, 0)
    span = count + 2 * HALO

    def to_member(k):
        other = (member + k) % members
        return remote(
            wanted.at[pl.ds(other * count, span)], window.at[member], send_wanted.at[k],
            recv_wanted.at[members + member], (group, other),
        )

    to_high = remote(
        wanted.at[pl.ds(bricks, HALO)], low_window.at[member], send_wanted.at[0], recv_wanted.at[member], high_at
    )
    to_low = remote(
        wanted.at[pl.ds(HALO, HALO)], high_window.at[member], send_wanted.at[members],
        recv_wanted.at[2 * members + member], low_at,
    )
    for k in range(1, members):
        to_member(k).start()
    pl.when(has_high)(to_high.start)
    pl.when(has_low)(to_low.start)
    window[member] = wanted[pl.ds(member * count, span)]
    end_halo(hidden_copies)
    for k in range(1, members):
        other = (member + k) % members
        remote(
            wanted.at[pl.ds(0, span)], window.at[other], send_wanted.at[k], recv_wanted.at[members + other],
            (group, other),
        ).wait_recv()
    for k in range(members):
        from_low = remote(wanted.at[pl.ds(0, HALO)], low_window.at[k], send_wanted.at[0], recv_wanted.at[k], low_at)
        from_high = remote(
            wanted.at[pl.ds(0, HALO)], high_window.at[k], send_wanted.at[0], recv_wanted.at[2 * members + k], high_at
        )
        pl.when(is_first & has_low)(from_low.wait_recv)
        pl.when(is_last & has_high)(from_high.wait_recv)

    def total(source, i):
        piece = source[0, i]
        for owner in range(1, members):
            piece = piece + source[owner, i]
        return piece

    def own_blend(i, carry):
        rising = grow(total(window, HALO + i), small)
        parts[HALO + i] = parted(silu(hidden[i] + rising))
        return carry

    lax.fori_loop(0, count, own_blend, 0)
    for side, at, edge_window, beyond in (
        (0, 0, low_window, is_first), (1, HALO + count, high_window, is_last),
    ):
        for one in range(HALO):
            piece = jnp.where(beyond, total(edge_window, one), total(window, at + one))
            grown[one] = grow(piece, small)
        pack(lambda spot: merged(grown[0, spot], grown[1, spot]), halves.at[0])
        wire = silu(hidden_halo[side] + halves[0])
        unpack_pair(wire, halves, parts.at[at], parts.at[at + 1])
    out_both = two(out_bias)

    def last_step(i, carry):
        hidden[i] = fine_conv(parts, HALO + i, fine_start, fine_links, i, fine_scratch, last_matrix) + out_both
        return carry

    lax.fori_loop(0, count, last_step, 0)
    for pair in range(pairs):
        flat = merged(hidden[2 * pair], hidden[2 * pair + 1]).T
        out[2 * pair : 2 * pair + 2] = x[2 * pair : 2 * pair + 2] + flat.reshape(2, 64, VOX)

    end_halo_sends(x_copies)
    end_shared_sends(code_copies)
    for i in range(count):
        end_shared_sends(pooled_copies(i))
    end_halo_sends(hidden_copies)
    end_first_sends()
    for k in range(1, members):
        to_member(k).wait_send()
    pl.when(has_high)(to_high.wait_send)
    pl.when(has_low)(to_low.wait_send)


def per_device(
    x, fine_links, parent_codes, coarse_links,
    in_weight, in_bias, down, one_weight, one_bias, two_weight, two_bias, up, out_weight, out_bias,
):
    count, channels = x.shape[0], x.shape[1]
    slots, wide = coarse_links.shape[0], one_bias.shape[0]
    members = lax.axis_size("dev")
    row = lambda bias: bias.reshape(1, -1)
    vmem = pl.BlockSpec(memory_space=pltpu.VMEM)
    smem = pl.BlockSpec(memory_space=pltpu.SMEM)
    anywhere = pl.BlockSpec(memory_space=pl.ANY)
    floats = lambda *shape: pltpu.VMEM(shape, F32)
    halfs = lambda *shape: pltpu.VMEM(shape, BF16)
    ints = lambda *shape: pltpu.VMEM(shape, jnp.int32)
    sems = lambda *shape: pltpu.SemaphoreType.DMA(shape)
    span = count + 2 * HALO
    wire = (32, 128)
    scratch = [
        floats(*x.shape), floats(*in_weight.shape), floats(*one_weight.shape), floats(*two_weight.shape),
        floats(*out_weight.shape), sems(5),
        halfs(1152, 384), halfs(1152, 384), halfs(1152, 768), halfs(1152, 768),
        halfs(10, 80, 128), halfs(10, 64, 128), halfs(3, 10, 16, 128),
        halfs(2, 10, 80, 128), halfs(2, 10, 64, 128), halfs(2, 3, 10, 16, 128),
        floats(2, 10 * LINE, 128), floats(VOX + 16, 128), floats(VOX + 16, 128),
        floats(span, VOX, 128), floats(count // 2, VOX, 128), floats(count, VOX, 128),
        floats(2, SURFACE, 128), floats(128, 128), floats(HALO, VOX, 128),
        floats(2, SURFACE, 128), floats(2, SURFACE, 128), floats(2, SURFACE, 128), floats(2, SURFACE, 128),
        ints(8, 128), ints(3 * members, 8, 128), ints(members, 8, 128), ints(8, 128),
        pltpu.SMEM((members, 8, 128), jnp.int32), pltpu.SMEM((8, 128), jnp.int32),
        floats(3 * members, count, *wire), floats(VOX, 128), floats(3 * slots, VOX, 128), floats(3 * slots, VOX, 128),
        floats(slots, SURFACE, 128), floats(2, slots, SURFACE, 128), floats(slots * 8, *wire),
        floats(members * count + 2 * HALO, *wire), floats(members, span, *wire), floats(members, HALO, *wire),
        floats(members, HALO, *wire),
        sems(2), sems(2), sems(2), sems(2), sems(2), sems(members + 1), sems(3 * members),
        sems(count, members + 1), sems(count, 3 * members),
        sems(slots, 3), sems(slots, 3), sems(slots, 3), sems(slots, 3), sems(members + 1), sems(3 * members),
    ]
    return pl.pallas_call(
        step_kernel,
        out_shape=jax.ShapeDtypeStruct(x.shape, F32),
        in_specs=[anywhere, smem, smem, smem, anywhere, vmem, vmem, anywhere, vmem, anywhere, vmem, vmem, anywhere, vmem],
        out_specs=vmem,
        scratch_shapes=scratch,
        name="step",
        compiler_params=pltpu.CompilerParams(collective_id=1, has_side_effects=True, vmem_limit_bytes=LIMIT),
    )(
        x, fine_links, parent_codes, coarse_links, in_weight, row(in_bias), down, one_weight, row(one_bias),
        two_weight, row(two_bias), up, out_weight, row(out_bias),
    )


def solution(mesh):
    bricks = P(("grp", "dev"), None, None)
    rows = P(("grp", "dev"), None)
    placed = (bricks, rows, P(("grp", "dev")), rows) + (P(),) * 10
    return jax.shard_map(per_device, mesh=mesh, in_specs=placed, out_specs=bricks, check_vma=False)
```

```python
import functools

import jax
import jax.numpy as jnp
from jax import lax
from jax.experimental import pallas as pl
from jax.experimental.pallas import tpu as pltpu
from jax.sharding import PartitionSpec as P

F32 = jnp.float32
BF16 = jnp.bfloat16
MESH = pl.DeviceIdType.MESH
SIDE = 8
VOX = SIDE * SIDE * SIDE
HALO = 2
SURFACE = VOX - 6 * 6 * 6
LINE = 24
LIMIT = 62 * 1024 * 1024
CHUNKS = ((0, 96), (96, 96), (192, 104))

offsets = [(x, y, z) for x in (-1, 0, 1) for y in (-1, 0, 1) for z in (-1, 0, 1)]
columns = {o: k for k, o in enumerate(o for o in offsets if o != (0, 0, 0))}


def high_of(v):
    return v.astype(BF16).astype(F32)


def silu(v):
    return v / (1.0 + jnp.exp(-v))


def dot(a, b):
    return lax.dot_general(a, b, (((1,), (0,)), ((), ())), preferred_element_type=F32)


def first_half(v):
    return lax.broadcasted_iota(jnp.int32, v.shape, 1) < v.shape[1] // 2


def merged(a, b):
    return jnp.where(first_half(a), a, b)


def doubled(v):
    turned = pltpu.roll(v, v.shape[1] // 2, 1)
    return merged(v, turned), merged(turned, v)


def parted(v):
    high = high_of(v)
    return merged(high, v - high)


def fill(load, link, put, rims, put_rim):
    found = {o: link(o) for o in columns}

    def get(o, start, size=SIDE, stride=1):
        row, keep = found[o]
        return load(row, start, size, stride) * keep

    for px in range(SIDE + 2):
        dx = -1 if px == 0 else (1 if px == SIDE + 1 else 0)
        x = {-1: SIDE - 1, 0: px - 1, 1: 0}[dx]
        low = get((dx, -1, 0), 64 * x + 56)
        high = get((dx, 1, 0), 64 * x)
        middle = get((dx, 0, 0), 64 * x, 64) if dx else load(None, 64 * x, 64, 1)
        put(px, jnp.concatenate([low, middle, high], axis=0))
    for plane, dz in enumerate((-1, 1)):
        z = SIDE - 1 if dz < 0 else 0
        for px in range(SIDE + 2):
            dx = -1 if px == 0 else (1 if px == SIDE + 1 else 0)
            x = {-1: SIDE - 1, 0: px - 1, 1: 0}[dx]
            rims[plane, px * LINE + 8 : px * LINE + 16] = get((dx, 0, dz), 64 * x + z, SIDE, 8)
            if dx:
                for dy in (-1, 1):
                    y = SIDE - 1 if dy < 0 else 0
                    at = px * LINE + (7 if dy < 0 else 16)
                    rims[plane, at : at + 1] = get((dx, dy, dz), 64 * x + 8 * y + z, 1)
        for dy in (-1, 1):
            y = SIDE - 1 if dy < 0 else 0
            at = LINE + (7 if dy < 0 else 16)
            rims[plane, pl.ds(at, SIDE, stride=LINE)] = get((0, dy, dz), 8 * y + z, SIDE, 64)
    for j in range(3):
        for px in range(SIDE + 2):
            at = px * LINE + 7 + j
            put_rim(j, px, jnp.concatenate([rims[0, at : at + 8], rims[1, at : at + 8]], axis=0))


def stacked(even, odd, edge):
    taps = []
    for i in range(3):
        for j in range(3):
            main = odd[i : i + 8] if j == 1 else even[i : i + 8, 8 * j : 8 * j + 64]
            rim = edge[j, i : i + 8]
            taps.append(jnp.concatenate([main.reshape(VOX, 128), rim.reshape(128, 128)], axis=0))
    return jnp.concatenate(taps, axis=1)


def shifted_sum(blocks, down, up):
    before, here, after = blocks
    down[8 : VOX + 8] = before[:VOX]
    up[8 : VOX + 8] = after[:VOX]
    for x in range(SIDE):
        rim = VOX + 16 * x
        down[pl.ds(7 + 64 * x, SIDE, stride=8)] = before[rim : rim + 8]
        up[pl.ds(16 + 64 * x, SIDE, stride=8)] = after[rim + 8 : rim + 16]
    return down[7 : VOX + 7] + here[:VOX] + up[9 : VOX + 9]


def fine_matrix(weight, matrix):
    w = weight[...]
    high = high_of(w)
    both = jnp.concatenate([high, w - high], axis=0).T.astype(BF16)
    for tap in range(27):
        rows, cols = tap // 3 * 128, tap % 3 * 128
        block = both[64 * tap : 64 * tap + 64]
        matrix[rows : rows + 64, cols : cols + 128] = block
        matrix[rows + 64 : rows + 128, cols : cols + 128] = block


def coarse_matrix(weight, matrix):
    for tap in range(27):
        rows, cols = tap // 3 * 128, tap % 3 * 128
        block = weight[:, 128 * tap : 128 * tap + 128].T
        high = high_of(block)
        matrix[rows : rows + 128, cols : cols + 128] = high.astype(BF16)
        matrix[rows : rows + 128, 384 + cols : 384 + cols + 128] = (block - high).astype(BF16)


def linker(links, brick, start, own, rows):
    def link(o):
        there = links[brick, columns[o]]
        there_is = there >= 0
        row = jnp.where(there_is, jnp.clip(there - start, 0, rows - 1), own)
        return row, jnp.where(there_is, 1.0, 0.0).astype(F32)

    return link


def loader(parts, own):
    def load(row, start, size, stride):
        row = own if row is None else row
        if stride == 1:
            return parts[row, start : start + size]
        return parts[row, pl.ds(start, size, stride=stride)]

    return load


def fine_conv(parts, own, start, links, brick, scratch, matrix):
    even, odd, edge, rims, down, up = scratch

    def put(px, v):
        even[px] = v.astype(BF16)
        odd[px] = v[8:72].astype(BF16)

    def put_rim(j, px, v):
        edge[j, px] = v.astype(BF16)

    fill(loader(parts, own), linker(links, brick, start, own, parts.shape[0]), put, rims, put_rim)
    sums = dot(stacked(even, odd, edge), matrix[...])
    out = shifted_sum([sums[:, 128 * k : 128 * k + 128] for k in range(3)], down, up)
    return out + pltpu.roll(out, 64, 1)


def coarse_conv(parts, own, start, links, brick, scratch, matrix):
    even, odd, edge, rims, down, up = scratch

    def put(px, v):
        high = v.astype(BF16)
        low = (v - high.astype(F32)).astype(BF16)
        for part, value in enumerate((high, low)):
            even[part, px] = value
        middle = v[8:72]
        high = middle.astype(BF16)
        odd[0, px] = high
        odd[1, px] = (middle - high.astype(F32)).astype(BF16)

    def put_rim(j, px, v):
        high = v.astype(BF16)
        edge[0, j, px] = high
        edge[1, j, px] = (v - high.astype(F32)).astype(BF16)

    fill(loader(parts, own), linker(links, brick, start, own, parts.shape[0]), put, rims, put_rim)
    tops = dot(stacked(even.at[0], odd.at[0], edge.at[0]), matrix[...])
    rests = dot(stacked(even.at[1], odd.at[1], edge.at[1]), matrix[:, 0:384])
    cut = lambda v, at: v[:, 128 * at : 128 * at + 128]
    blocks = [cut(tops, k) + cut(tops, 3 + k) + cut(rests, k) for k in range(3)]
    return shifted_sum(blocks, down, up)


def surface_spots():
    spots = [(0, 0, 64, 1), (64, 448, 64, 1)]
    for x in range(1, 7):
        at = 128 + (x - 1) * 16
        spots += [(at, 64 * x, 8, 1), (at + 8, 64 * x + 56, 8, 1)]
    for x in range(1, 7):
        at = 224 + (x - 1) * 12
        spots += [(at, 64 * x + 8, 6, 8), (at + 6, 64 * x + 15, 6, 8)]
    return spots


def pack(get, wire):
    for at, start, size, stride in surface_spots():
        wire[at : at + size] = get(pl.ds(start, size, stride=stride) if stride > 1 else pl.ds(start, size))


def unpack(wire, brick):
    for at, start, size, stride in surface_spots():
        spot = pl.ds(start, size, stride=stride) if stride > 1 else pl.ds(start, size)
        brick[spot] = wire[at : at + size]


def unpack_pair(wire, scratch, first, second):
    a, b = doubled(wire)
    scratch[0] = parted(a)
    scratch[1] = parted(b)
    unpack(scratch.at[0], first)
    unpack(scratch.at[1], second)


def pool(v, scratch, wire):
    lines = v.reshape(4, 2, 4, 2, SIDE, 128)
    sums = (lines[:, 0, :, 0] + lines[:, 0, :, 1]) + (lines[:, 1, :, 0] + lines[:, 1, :, 1])
    scratch[...] = sums.reshape(128, 128)
    for z in range(4):
        halves = [
            scratch[pl.ds(64 * half + 2 * z, 8, stride=8)] + scratch[pl.ds(64 * half + 2 * z + 1, 8, stride=8)]
            for half in range(2)
        ]
        wire[8 * z : 8 * z + 8] = merged(*halves) * 0.125


def split_spot(octant, half, z):
    a, b, c = octant // 4, octant // 2 % 2, octant % 2
    return pl.ds(256 * b + 32 * (4 * a + 2 * half) + 4 * c + z, 8, stride=8)


def place_piece(wire, octant, brick):
    for half, v in enumerate(doubled(wire)):
        v = parted(v)
        for z in range(4):
            brick[split_spot(octant, half, z)] = v[8 * z : 8 * z + 8]


def take_pieces(brick, pieces):
    for octant in range(8):
        for z in range(4):
            halves = [brick[split_spot(octant, half, z)] for half in range(2)]
            pieces[octant, 8 * z : 8 * z + 8] = merged(*halves)


def swap_halves(v, split):
    first, second = (2, SIDE) if split else (SIDE, 2)
    return v.reshape(first, second, 32, 128).swapaxes(0, 1).reshape(VOX, 128)


def grow(piece, scratch):
    for half, v in enumerate(doubled(piece)):
        for z in range(4):
            rows = v[8 * z : 8 * z + 8]
            scratch[pl.ds(64 * half + 2 * z, 8, stride=8)] = rows
            scratch[pl.ds(64 * half + 2 * z + 1, 8, stride=8)] = rows
    lines = scratch[...].reshape(4, 1, 4, 1, SIDE, 128)
    return jnp.broadcast_to(lines, (4, 2, 4, 2, SIDE, 128)).reshape(VOX, 128)


def step_kernel(
    x_any, fine_links, own_codes, coarse_links, in_any, in_bias, down_weight, one_any, one_bias, two_any, two_bias,
    up_weight, out_any, out_bias,
    out,
    x, in_weight, one_weight, two_weight, out_weight, loads,
    matrix, last_matrix, one_matrix, two_matrix,
    even, odd, edge, wide_even, wide_odd, wide_edge, rims, shift_down, shift_up,
    parts, turned, hidden, halves, small, grown,
    x_send, x_halo, hidden_send, hidden_halo,
    code_block, codes, code_table, table, code_scalars, table_scalars,
    pooled, placed, base, first,
    first_send, first_halo, lifted, wanted, window, low_window, high_window,
    local_sems, send_x, recv_x, send_hidden, recv_hidden, send_codes, recv_codes, send_pooled, recv_pooled,
    send_first, recv_first, send_relay, recv_relay, send_wanted, recv_wanted,
):
    group, member = lax.axis_index("grp"), lax.axis_index("dev")
    groups, members = lax.axis_size("grp"), lax.axis_size("dev")
    position = group * members + member
    whole = groups * members
    count, slots = fine_links.shape[0], coarse_links.shape[0]
    pairs = count // 2
    relayed = members == 4
    has_left, has_right = position > 0, position < whole - 1
    has_low, has_high = group > 0, group < groups - 1
    is_first, is_last = member == 0, member == members - 1
    left_at = (jnp.maximum(position - 1, 0) // members, (position + members - 1) % members)
    right_at = (jnp.minimum(position + 1, whole - 1) // members, (position + 1) % members)
    low_at = (jnp.maximum(group - 1, 0), members - 1)
    high_at = (jnp.minimum(group + 1, groups - 1), 0)
    always = position >= 0

    def fetch(k, source, target):
        return pltpu.make_async_copy(source, target, loads.at[k])

    fetches = [
        fetch(0, x_any, x), fetch(1, in_any, in_weight), fetch(2, one_any, one_weight),
        fetch(3, two_any, two_weight), fetch(4, out_any, out_weight),
    ]
    for copy in fetches:
        copy.start()

    barrier = pltpu.get_barrier_semaphore()

    def greet(where):
        pl.semaphore_signal(barrier, inc=1, device_id=where, device_id_type=MESH)

    pl.when(has_left)(lambda: greet(left_at))
    pl.when(has_right)(lambda: greet(right_at))
    for k in range(1, members):
        greet((group, (member + k) % members))
    for k in range(members):
        pl.when(is_first & has_low)(lambda k=k: greet((low_at[0], k)))
        pl.when(is_last & has_high)(lambda k=k: greet((high_at[0], k)))

    def remote(src, dst, send, recv, where):
        return pltpu.make_async_remote_copy(
            src_ref=src, dst_ref=dst, send_sem=send, recv_sem=recv, device_id=where, device_id_type=MESH
        )

    row = lax.broadcasted_iota(jnp.int32, (SIDE, 128), 0)
    block = jnp.full((SIDE, 128), -1, jnp.int32)
    for i in range(count):
        block = jnp.where(row == i, own_codes[i], block)
    code_block[...] = block
    codes[members + member] = block
    fetches[0].wait()
    for pair in range(pairs):
        turned[pair] = x[2 * pair : 2 * pair + 2].reshape(128, VOX).T
    pack(lambda spot: turned[0, spot], x_send.at[0])
    pack(lambda spot: turned[pairs - 1, spot], x_send.at[1])
    pl.semaphore_wait(
        barrier,
        jnp.where(has_left, 1, 0) + jnp.where(has_right, 1, 0) + (members - 1)
        + jnp.where(has_low, 1, 0) + jnp.where(has_high, 1, 0),
    )

    def halo_copies(source, halo, send, recv):
        to_left = remote(source.at[0], halo.at[1], send.at[0], recv.at[1], left_at)
        to_right = remote(source.at[1], halo.at[0], send.at[1], recv.at[0], right_at)
        return to_left, to_right

    def start_halo(copies):
        pl.when(has_left)(copies[0].start)
        pl.when(has_right)(copies[1].start)

    def end_halo(copies):
        pl.when(has_left)(copies[1].wait_recv)
        pl.when(has_right)(copies[0].wait_recv)

    def end_halo_sends(copies):
        pl.when(has_left)(copies[0].wait_send)
        pl.when(has_right)(copies[1].wait_send)

    def shared_copies(source, at, send, recv):
        near = [
            remote(source, at(members + member), send.at[k], recv.at[members + member], (group, (member + k) % members))
            for k in range(1, members)
        ]
        to_high = remote(source, at(member), send.at[0], recv.at[member], high_at)
        to_low = remote(source, at(2 * members + member), send.at[members], recv.at[2 * members + member], low_at)
        return near, to_high, to_low

    def start_shared(copies):
        near, to_high, to_low = copies
        for copy in near:
            copy.start()
        pl.when(has_high)(to_high.start)
        pl.when(has_low)(to_low.start)

    def end_shared(source, at, send, recv):
        for k in range(1, members):
            other = (member + k) % members
            remote(source, at(members + other), send.at[k], recv.at[members + other], (group, other)).wait_recv()
        for k in range(members):
            from_low = remote(source, at(k), send.at[0], recv.at[k], low_at)
            from_high = remote(source, at(2 * members + k), send.at[0], recv.at[2 * members + k], high_at)
            pl.when(is_first & has_low)(from_low.wait_recv)
            pl.when(is_last & has_high)(from_high.wait_recv)

    def end_shared_sends(copies):
        near, to_high, to_low = copies
        for copy in near:
            copy.wait_send()
        pl.when(has_high)(to_high.wait_send)
        pl.when(has_low)(to_low.wait_send)

    x_copies = halo_copies(x_send, x_halo, send_x, recv_x)
    start_halo(x_copies)
    code_at = lambda k: codes.at[k]
    code_copies = shared_copies(code_block, code_at, send_codes, recv_codes)
    start_shared(code_copies)

    fetches[1].wait()
    fine_matrix(in_weight, matrix)
    for pair in range(pairs):
        for one, v in enumerate(doubled(turned[pair])):
            parts[HALO + 2 * pair + one] = parted(v)
    end_shared(code_block, code_at, send_codes, recv_codes)
    lane = lax.broadcasted_iota(jnp.int32, (SIDE, 128), 1)
    table_rows = jnp.full((SIDE, 128), -1, jnp.int32)
    for near in range(3):
        there = position + near - 1
        valid = (there >= 0) & (there < whole)
        there = jnp.where(valid, there, position)
        there_group = there // members
        there_member = there - there_group * members
        band = there_group - group + 1
        spot = jnp.where(valid, lane, -1000) + there_member * slots * 8
        best = jnp.full((SIDE, 128), -1, jnp.int32)
        for k in range(members):
            match = (codes[band * members + k] == spot) & (row < count) & (lane < slots * 8)
            best = jnp.maximum(best, jnp.where(match, (band * members + k) * count + row, -1))
        top = jnp.max(best, axis=0, keepdims=True)
        table_rows = jnp.where(row == near, top, table_rows)
    code_table[...] = codes[pl.ds(members, members)]
    table[...] = table_rows
    to_table = pltpu.make_async_copy(table, table_scalars, local_sems.at[0])
    to_codes = pltpu.make_async_copy(code_table, code_scalars, local_sems.at[1])
    to_table.start()
    to_codes.start()
    fetches[2].wait()
    coarse_matrix(one_weight, one_matrix)
    fetches[3].wait()
    coarse_matrix(two_weight, two_matrix)
    fetches[4].wait()
    fine_matrix(out_weight, last_matrix)
    to_table.wait()
    to_codes.wait()

    fine_start = position * count - HALO
    end_halo(x_copies)
    for side, at in ((0, 0), (1, HALO + count)):
        unpack_pair(x_halo[side], halves, parts.at[at], parts.at[at + 1])
    fine_scratch = (even, odd, edge, rims, shift_down, shift_up)
    two = lambda bias: jnp.concatenate([bias[...], bias[...]], axis=1)
    in_both = two(in_bias)

    def pooled_at(i):
        return lambda k: pooled.at[k, i]

    def pooled_copies(i):
        return shared_copies(pooled.at[members + member, i], pooled_at(i), send_pooled.at[i], recv_pooled.at[i])

    def first_step(i, carry):
        v = silu(fine_conv(parts, HALO + i, fine_start, fine_links, i, fine_scratch, matrix) + in_both)
        pool(v, small, pooled.at[members + member, i])
        hidden[i] = v
        start_shared(pooled_copies(i))
        return carry

    lax.fori_loop(0, count, first_step, 0)
    pack(lambda spot: merged(hidden[0, spot], hidden[1, spot]), hidden_send.at[0])
    pack(lambda spot: merged(hidden[count - 2, spot], hidden[count - 1, spot]), hidden_send.at[1])
    hidden_copies = halo_copies(hidden_send, hidden_halo, send_hidden, recv_hidden)
    start_halo(hidden_copies)

    turned_down = down_weight[...]
    down_high = high_of(turned_down)
    down_both = jnp.concatenate([down_high, turned_down - down_high], axis=1)
    down_matrix = jnp.concatenate([down_both, down_both], axis=0).astype(BF16)
    for i in range(count):
        end_shared(pooled.at[members + member, i], pooled_at(i), send_pooled.at[i], recv_pooled.at[i])

    def base_step(slot, carry):
        for octant in range(8):
            which = table_scalars[slot // slots, slot % slots * 8 + octant]
            there_is = which >= 0
            which = jnp.where(there_is, jnp.minimum(which, 3 * members * count - 1), (members + member) * count)
            keep = jnp.where(there_is, 1.0, 0.0).astype(F32)
            place_piece(pooled[which // count, which % count] * keep, octant, placed)
        sums = dot(placed[...].astype(BF16), down_matrix)
        base[slot] = swap_halves(sums[:, 0:128] + sums[:, 128:256], True)
        return carry

    lax.fori_loop(0, 3 * slots, base_step, 0)
    coarse_start = (position - 1) * slots
    wide_scratch = (wide_even, wide_odd, wide_edge, rims, shift_down, shift_up)

    if relayed:
        parity = member % 2
        x_at = (group, member + 1 - 2 * parity)
        relay_group = group + jnp.where(member == 1, -1, 0) + jnp.where(member == 2, 1, 0)
        relays_out = (relay_group >= 0) & (relay_group < groups)
        relays_in = jnp.where(is_first, has_low, True) & jnp.where(is_last, has_high, True)
        relay_at = (jnp.clip(relay_group, 0, groups - 1), (member + 2) % members)

        def direct(i, c):
            at, rows = CHUNKS[c]
            return remote(
                first_send.at[i, pl.ds(at, rows)], first_halo.at[parity, i, pl.ds(at, rows)],
                send_first.at[i, c], recv_first.at[i, c], x_at,
            )

        def came(i, c):
            at, rows = CHUNKS[c]
            return remote(
                first_send.at[i, pl.ds(at, rows)], first_halo.at[1 - parity, i, pl.ds(at, rows)],
                send_first.at[i, c], recv_first.at[i, c], x_at,
            )

        def relay(i, c):
            at, rows = CHUNKS[c]
            return remote(
                first_halo.at[1 - parity, i, pl.ds(at, rows)], first_halo.at[parity, i, pl.ds(at, rows)],
                send_relay.at[i, c], recv_relay.at[i, c], relay_at,
            )

        def start_first(i):
            for c in range(len(CHUNKS)):
                direct(i, c).start()

        def end_first():
            for i in range(slots):
                for c in range(len(CHUNKS)):
                    came(i, c).wait_recv()
                    pl.when(relays_out)(relay(i, c).start)
            for i in range(slots):
                for c in range(len(CHUNKS)):
                    pl.when(relays_in)(relay(i, c).wait_recv)

        def end_first_sends():
            for i in range(slots):
                for c in range(len(CHUNKS)):
                    direct(i, c).wait_send()
                    pl.when(relays_out)(relay(i, c).wait_send)
    else:

        def sides(i):
            to_left = remote(first_send.at[i], first_halo.at[1, i], send_first.at[i, 0], recv_first.at[i, 1], left_at)
            to_right = remote(first_send.at[i], first_halo.at[0, i], send_first.at[i, 1], recv_first.at[i, 0], right_at)
            return to_left, to_right

        def start_first(i):
            start_halo(sides(i))

        def end_first():
            for i in range(slots):
                end_halo(sides(i))

        def end_first_sends():
            for i in range(slots):
                end_halo_sends(sides(i))

    def second_step(i, carry):
        v = silu(coarse_conv(base, slots + i, coarse_start, coarse_links, i, wide_scratch, one_matrix) + one_bias[...])
        first[slots + i] = v
        pack(lambda spot: first[slots + i, spot], first_send.at[i])
        start_first(i)
        return carry

    lax.fori_loop(0, slots, second_step, 0)
    turned_up = up_weight[...].T
    up_high = high_of(turned_up)
    up_both = jnp.concatenate([up_high, turned_up - up_high], axis=1)
    up_matrix = jnp.concatenate([up_both, up_both], axis=0).astype(BF16)
    end_first()
    for side, at in ((0, 0), (1, 2 * slots)):
        for i in range(slots):
            unpack(first_halo.at[side, i], first.at[at + i])

    def third_step(i, carry):
        v = silu(coarse_conv(first, slots + i, coarse_start, coarse_links, i, wide_scratch, two_matrix) + two_bias[...])
        high = v.astype(BF16)
        low = (v - high.astype(F32)).astype(BF16)
        sums = dot(jnp.concatenate([high, low], axis=1), up_matrix)
        placed[...] = swap_halves(sums + pltpu.roll(sums, 64, 1), False)
        take_pieces(placed, lifted.at[pl.ds(i * 8, 8)])
        return carry

    lax.fori_loop(0, slots, third_step, 0)
    bricks = members * count
    zeros = jnp.zeros((HALO,) + wanted.shape[1:], F32)
    wanted[0:HALO] = zeros
    wanted[HALO + bricks :] = zeros

    def choose(j, carry):
        code = code_scalars[j // count, j % count, 0] - member * slots * 8
        mine = (code >= 0) & (code < slots * 8)
        keep = jnp.where(mine, 1.0, 0.0).astype(F32)
        wanted[HALO + j] = lifted[jnp.where(mine, code, 0)] * keep
        return carry

    lax.fori_loop(0, bricks, choose, 0)
    parts_of = ((HALO, count, None), (0, HALO, 0), (HALO + count, HALO, members - 1))

    def to_member(k, part):
        other = (member + k) % members
        at, rows, _ = parts_of[part]
        return remote(
            wanted.at[pl.ds(other * count + at, rows)], window.at[member, pl.ds(at, rows)], send_wanted.at[k, part],
            recv_wanted.at[members + member, part], (group, other),
        )

    def from_member(k, part):
        other = (member + k) % members
        at, rows, _ = parts_of[part]
        return remote(
            wanted.at[pl.ds(at, rows)], window.at[other, pl.ds(at, rows)], send_wanted.at[k, part],
            recv_wanted.at[members + other, part], (group, other),
        )

    def when_read(who, part, action):
        none_at = parts_of[part][2]
        if none_at is None:
            action()
        else:
            pl.when(who != none_at)(action)

    to_high = remote(
        wanted.at[pl.ds(bricks, HALO)], low_window.at[member], send_wanted.at[0, 0], recv_wanted.at[member, 0], high_at
    )
    to_low = remote(
        wanted.at[pl.ds(HALO, HALO)], high_window.at[member], send_wanted.at[members, 0],
        recv_wanted.at[2 * members + member, 0], low_at,
    )
    for k in range(1, members):
        to_member(k, 0).start()
    for k in range(1, members):
        for part in (1, 2):
            when_read((member + k) % members, part, to_member(k, part).start)
    pl.when(has_high)(to_high.start)
    pl.when(has_low)(to_low.start)
    window[member] = wanted[pl.ds(member * count, count + 2 * HALO)]
    end_halo(hidden_copies)
    for k in range(1, members):
        from_member(k, 0).wait_recv()

    def total(source, i):
        piece = source[0, i]
        for owner in range(1, members):
            piece = piece + source[owner, i]
        return piece

    def own_blend(i, carry):
        rising = grow(total(window, HALO + i), small)
        parts[HALO + i] = parted(silu(hidden[i] + rising))
        return carry

    lax.fori_loop(0, count, own_blend, 0)
    for k in range(1, members):
        for part in (1, 2):
            when_read(member, part, from_member(k, part).wait_recv)
    for k in range(members):
        spot = wanted.at[pl.ds(0, HALO)]
        from_low = remote(spot, low_window.at[k], send_wanted.at[0, 0], recv_wanted.at[k, 0], low_at)
        from_high = remote(
            spot, high_window.at[k], send_wanted.at[0, 0], recv_wanted.at[2 * members + k, 0], high_at
        )
        pl.when(is_first & has_low)(from_low.wait_recv)
        pl.when(is_last & has_high)(from_high.wait_recv)
    for side, at, edge_window, beyond in (
        (0, 0, low_window, is_first), (1, HALO + count, high_window, is_last),
    ):
        for one in range(HALO):
            piece = jnp.where(beyond, total(edge_window, one), total(window, at + one))
            grown[one] = grow(piece, small)
        pack(lambda spot: merged(grown[0, spot], grown[1, spot]), halves.at[0])
        wire = silu(hidden_halo[side] + halves[0])
        unpack_pair(wire, halves, parts.at[at], parts.at[at + 1])
    out_both = two(out_bias)

    def last_step(i, carry):
        hidden[i] = fine_conv(parts, HALO + i, fine_start, fine_links, i, fine_scratch, last_matrix) + out_both
        return carry

    lax.fori_loop(0, count, last_step, 0)
    for pair in range(pairs):
        flat = merged(hidden[2 * pair], hidden[2 * pair + 1]).T
        out[2 * pair : 2 * pair + 2] = x[2 * pair : 2 * pair + 2] + flat.reshape(2, 64, VOX)

    end_halo_sends(x_copies)
    end_shared_sends(code_copies)
    for i in range(count):
        end_shared_sends(pooled_copies(i))
    end_halo_sends(hidden_copies)
    end_first_sends()
    for k in range(1, members):
        to_member(k, 0).wait_send()
        for part in (1, 2):
            when_read((member + k) % members, part, to_member(k, part).wait_send)
    pl.when(has_high)(to_high.wait_send)
    pl.when(has_low)(to_low.wait_send)


def per_device(
    x, fine_links, parent_codes, coarse_links,
    in_weight, in_bias, down, one_weight, one_bias, two_weight, two_bias, up, out_weight, out_bias,
):
    count, channels = x.shape[0], x.shape[1]
    slots, wide = coarse_links.shape[0], one_bias.shape[0]
    members = lax.axis_size("dev")
    row = lambda bias: bias.reshape(1, -1)
    vmem = pl.BlockSpec(memory_space=pltpu.VMEM)
    smem = pl.BlockSpec(memory_space=pltpu.SMEM)
    anywhere = pl.BlockSpec(memory_space=pl.ANY)
    floats = lambda *shape: pltpu.VMEM(shape, F32)
    halfs = lambda *shape: pltpu.VMEM(shape, BF16)
    ints = lambda *shape: pltpu.VMEM(shape, jnp.int32)
    sems = lambda *shape: pltpu.SemaphoreType.DMA(shape)
    span = count + 2 * HALO
    wire = (32, 128)
    scratch = [
        floats(*x.shape), floats(*in_weight.shape), floats(*one_weight.shape), floats(*two_weight.shape),
        floats(*out_weight.shape), sems(5),
        halfs(1152, 384), halfs(1152, 384), halfs(1152, 768), halfs(1152, 768),
        halfs(10, 80, 128), halfs(10, 64, 128), halfs(3, 10, 16, 128),
        halfs(2, 10, 80, 128), halfs(2, 10, 64, 128), halfs(2, 3, 10, 16, 128),
        floats(2, 10 * LINE, 128), floats(VOX + 16, 128), floats(VOX + 16, 128),
        floats(span, VOX, 128), floats(count // 2, VOX, 128), floats(count, VOX, 128),
        floats(2, SURFACE, 128), floats(128, 128), floats(HALO, VOX, 128),
        floats(2, SURFACE, 128), floats(2, SURFACE, 128), floats(2, SURFACE, 128), floats(2, SURFACE, 128),
        ints(8, 128), ints(3 * members, 8, 128), ints(members, 8, 128), ints(8, 128),
        pltpu.SMEM((members, 8, 128), jnp.int32), pltpu.SMEM((8, 128), jnp.int32),
        floats(3 * members, count, *wire), floats(VOX, 128), floats(3 * slots, VOX, 128), floats(3 * slots, VOX, 128),
        floats(slots, SURFACE, 128), floats(2, slots, SURFACE, 128), floats(slots * 8, *wire),
        floats(members * count + 2 * HALO, *wire), floats(members, span, *wire), floats(members, HALO, *wire),
        floats(members, HALO, *wire),
        sems(2), sems(2), sems(2), sems(2), sems(2), sems(members + 1), sems(3 * members),
        sems(count, members + 1), sems(count, 3 * members),
        sems(slots, 3), sems(slots, 3), sems(slots, 3), sems(slots, 3), sems(members + 1, 3), sems(3 * members, 3),
    ]
    return pl.pallas_call(
        step_kernel,
        out_shape=jax.ShapeDtypeStruct(x.shape, F32),
        in_specs=[anywhere, smem, smem, smem, anywhere, vmem, vmem, anywhere, vmem, anywhere, vmem, vmem, anywhere, vmem],
        out_specs=vmem,
        scratch_shapes=scratch,
        name="step",
        compiler_params=pltpu.CompilerParams(collective_id=1, has_side_effects=True, vmem_limit_bytes=LIMIT),
    )(
        x, fine_links, parent_codes, coarse_links, in_weight, row(in_bias), down.T, one_weight, row(one_bias),
        two_weight, row(two_bias), up, out_weight, row(out_bias),
    )


def solution(mesh):
    bricks = P(("grp", "dev"), None, None)
    rows = P(("grp", "dev"), None)
    placed = (bricks, rows, P(("grp", "dev")), rows) + (P(),) * 10
    return jax.shard_map(per_device, mesh=mesh, in_specs=placed, out_specs=bricks, check_vma=False)
```

```python
import functools

import jax
import jax.numpy as jnp
from jax import lax
from jax.experimental import pallas as pl
from jax.experimental.pallas import tpu as pltpu
from jax.sharding import PartitionSpec as P

F32 = jnp.float32
BF16 = jnp.bfloat16
MESH = pl.DeviceIdType.MESH
SIDE = 8
VOX = SIDE * SIDE * SIDE
HALO = 2
SURFACE = VOX - 6 * 6 * 6
LINE = 24
LIMIT = 62 * 1024 * 1024
CHUNKS = ((0, 96), (96, 96), (192, 104))

offsets = [(x, y, z) for x in (-1, 0, 1) for y in (-1, 0, 1) for z in (-1, 0, 1)]
columns = {o: k for k, o in enumerate(o for o in offsets if o != (0, 0, 0))}


def high_of(v):
    return v.astype(BF16).astype(F32)


def silu(v):
    return v / (1.0 + jnp.exp(-v))


def dot(a, b):
    return lax.dot_general(a, b, (((1,), (0,)), ((), ())), preferred_element_type=F32)


def first_half(v):
    return lax.broadcasted_iota(jnp.int32, v.shape, 1) < v.shape[1] // 2


def merged(a, b):
    return jnp.where(first_half(a), a, b)


def doubled(v):
    turned = pltpu.roll(v, v.shape[1] // 2, 1)
    return merged(v, turned), merged(turned, v)


def parted(v):
    high = high_of(v)
    return merged(high, v - high)


def fill(load, link, put, rims, put_rim):
    found = {o: link(o) for o in columns}

    def get(o, start, size=SIDE, stride=1):
        row, keep = found[o]
        return load(row, start, size, stride) * keep

    for px in range(SIDE + 2):
        dx = -1 if px == 0 else (1 if px == SIDE + 1 else 0)
        x = {-1: SIDE - 1, 0: px - 1, 1: 0}[dx]
        low = get((dx, -1, 0), 64 * x + 56)
        high = get((dx, 1, 0), 64 * x)
        middle = get((dx, 0, 0), 64 * x, 64) if dx else load(None, 64 * x, 64, 1)
        put(px, jnp.concatenate([low, middle, high], axis=0))
    fill_edges(get, rims, put_rim)


def fill_edges(get, rims, put_rim):
    for plane, dz in enumerate((-1, 1)):
        z = SIDE - 1 if dz < 0 else 0
        for px in range(SIDE + 2):
            dx = -1 if px == 0 else (1 if px == SIDE + 1 else 0)
            x = {-1: SIDE - 1, 0: px - 1, 1: 0}[dx]
            rims[plane, px * LINE + 8 : px * LINE + 16] = get((dx, 0, dz), 64 * x + z, SIDE, 8)
            if dx:
                for dy in (-1, 1):
                    y = SIDE - 1 if dy < 0 else 0
                    at = px * LINE + (7 if dy < 0 else 16)
                    rims[plane, at : at + 1] = get((dx, dy, dz), 64 * x + 8 * y + z, 1)
        for dy in (-1, 1):
            y = SIDE - 1 if dy < 0 else 0
            at = LINE + (7 if dy < 0 else 16)
            rims[plane, pl.ds(at, SIDE, stride=LINE)] = get((0, dy, dz), 8 * y + z, SIDE, 64)
    for j in range(3):
        for px in range(SIDE + 2):
            at = px * LINE + 7 + j
            put_rim(j, px, jnp.concatenate([rims[0, at : at + 8], rims[1, at : at + 8]], axis=0))


def stacked(even, odd, edge):
    taps = []
    for i in range(3):
        for j in range(3):
            main = odd[i : i + 8] if j == 1 else even[i : i + 8, 8 * j : 8 * j + 64]
            rim = edge[j, i : i + 8]
            taps.append(jnp.concatenate([main.reshape(VOX, 128), rim.reshape(128, 128)], axis=0))
    return jnp.concatenate(taps, axis=1)


def shifted_sum(blocks, down, up):
    before, here, after = blocks
    down[8 : VOX + 8] = before[:VOX]
    up[8 : VOX + 8] = after[:VOX]
    for x in range(SIDE):
        rim = VOX + 16 * x
        down[pl.ds(7 + 64 * x, SIDE, stride=8)] = before[rim : rim + 8]
        up[pl.ds(16 + 64 * x, SIDE, stride=8)] = after[rim + 8 : rim + 16]
    return down[7 : VOX + 7] + here[:VOX] + up[9 : VOX + 9]


def fine_matrix(weight, matrix):
    w = weight[...]
    high = high_of(w)
    both = jnp.concatenate([high, w - high], axis=0).T.astype(BF16)
    for tap in range(27):
        rows, cols = tap // 3 * 128, tap % 3 * 128
        block = both[64 * tap : 64 * tap + 64]
        matrix[rows : rows + 64, cols : cols + 128] = block
        matrix[rows + 64 : rows + 128, cols : cols + 128] = block


def coarse_matrix(weight, matrix):
    for tap in range(27):
        rows, cols = tap // 3 * 128, tap % 3 * 128
        block = weight[:, 128 * tap : 128 * tap + 128].T
        high = high_of(block)
        matrix[rows : rows + 128, cols : cols + 128] = high.astype(BF16)
        matrix[rows : rows + 128, 384 + cols : 384 + cols + 128] = (block - high).astype(BF16)


def linker(links, brick, start, own, rows):
    def link(o):
        there = links[brick, columns[o]]
        there_is = there >= 0
        row = jnp.where(there_is, jnp.clip(there - start, 0, rows - 1), own)
        return row, jnp.where(there_is, 1.0, 0.0).astype(F32)

    return link


def loader(parts, own):
    def load(row, start, size, stride):
        row = own if row is None else row
        if stride == 1:
            return parts[row, start : start + size]
        return parts[row, pl.ds(start, size, stride=stride)]

    return load


def fine_conv(parts, own, start, links, brick, scratch, matrix):
    even, odd, edge, rims, down, up = scratch

    def put(px, v):
        even[px] = v.astype(BF16)
        odd[px] = v[8:72].astype(BF16)

    def put_rim(j, px, v):
        edge[j, px] = v.astype(BF16)

    fill(loader(parts, own), linker(links, brick, start, own, parts.shape[0]), put, rims, put_rim)
    sums = dot(stacked(even, odd, edge), matrix[...])
    out = shifted_sum([sums[:, 128 * k : 128 * k + 128] for k in range(3)], down, up)
    return out + pltpu.roll(out, 64, 1)


def coarse_conv(parts, own, start, links, brick, scratch, matrix):
    even, odd, edge, rims, down, up = scratch

    def put(px, v):
        high = v.astype(BF16)
        low = (v - high.astype(F32)).astype(BF16)
        for part, value in enumerate((high, low)):
            even[part, px] = value
        middle = v[8:72]
        high = middle.astype(BF16)
        odd[0, px] = high
        odd[1, px] = (middle - high.astype(F32)).astype(BF16)

    def put_rim(j, px, v):
        high = v.astype(BF16)
        edge[0, j, px] = high
        edge[1, j, px] = (v - high.astype(F32)).astype(BF16)

    fill(loader(parts, own), linker(links, brick, start, own, parts.shape[0]), put, rims, put_rim)
    tops = dot(stacked(even.at[0], odd.at[0], edge.at[0]), matrix[...])
    rests = dot(stacked(even.at[1], odd.at[1], edge.at[1]), matrix[:, 0:384])
    cut = lambda v, at: v[:, 128 * at : 128 * at + 128]
    blocks = [cut(tops, k) + cut(tops, 3 + k) + cut(rests, k) for k in range(3)]
    return shifted_sum(blocks, down, up)


def pieces_of(v, wide):
    high = v.astype(BF16)
    return (high, (v - high.astype(F32)).astype(BF16)) if wide else (high,)


def multiplied(lhs, wide, matrix, blocks):
    rows = [matrix.at[pl.ds(128 * at, 128)] for at in blocks]
    take = lambda cols: jnp.concatenate([r[:, cols] for r in rows], axis=0)
    cut = lambda v, at: v[:, 128 * at : 128 * at + 128]
    if not wide:
        sums = dot(lhs[0], take(slice(0, 384)))
        return [cut(sums, k) for k in range(3)]
    tops, rests = dot(lhs[0], take(slice(0, 768))), dot(lhs[1], take(slice(0, 384)))
    return [cut(tops, k) + cut(tops, 3 + k) + cut(rests, k) for k in range(3)]


def line_sum(blocks, down, up):
    rows = blocks[0].shape[0]
    down[8 : rows + 8] = blocks[0]
    up[8 : rows + 8] = blocks[2]
    zeros = jnp.zeros((SIDE, 128), F32)
    for at in range(0, rows, 64):
        down[pl.ds(7 + at, SIDE, stride=8)] = zeros
        up[pl.ds(16 + at, SIDE, stride=8)] = zeros
    return down[7 : rows + 7] + blocks[1] + up[9 : rows + 9]


def clear_center(even, odd, wide):
    for part in range(2 if wide else 1):
        for px in (0, SIDE + 1):
            even[part, px] = jnp.zeros(even.shape[2:], BF16)
            odd[part, px] = jnp.zeros(odd.shape[2:], BF16)


def fill_center(brick, wide, even, odd):
    zeros = jnp.zeros((SIDE, 128), F32)
    for x in range(SIDE):
        middle = brick[64 * x : 64 * x + 64]
        for part, v in enumerate(pieces_of(jnp.concatenate([zeros, middle, zeros], axis=0), wide)):
            even[part, x + 1] = v
        for part, v in enumerate(pieces_of(middle, wide)):
            odd[part, x + 1] = v


def center(wide, even, odd, down, up, matrix, first, last):
    def taps(part):
        windows = []
        for i in range(3):
            for j in range(3):
                xs = slice(first + i, last + i)
                v = odd[part, xs] if j == 1 else even[part, xs, 8 * j : 8 * j + 64]
                windows.append(v.reshape((last - first) * 64, 128))
        return jnp.concatenate(windows, axis=1)

    lhs = [taps(part) for part in range(2 if wide else 1)]
    return line_sum(multiplied(lhs, wide, matrix, range(9)), down, up)


def fill_rims(load, link, wide, at, faces_even, faces_odd, edge, rims):
    found = {o: link(o) for o in columns}
    zeros = jnp.zeros((SIDE, 128), F32)

    def get(o, start, size=SIDE, stride=1):
        row, keep = found[o]
        return load(row, start, size, stride) * keep

    def put_face(face, lines):
        v = jnp.concatenate(lines, axis=0)
        for part, value in enumerate(pieces_of(v, wide)):
            faces_even[part, face, at] = value
        for part, value in enumerate(pieces_of(v[8:72], wide)):
            faces_odd[part, face, at] = value

    def put_rim(j, px, v):
        for part, value in enumerate(pieces_of(v, wide)):
            edge[part, j, at, px] = value

    for face, d in enumerate((-1, 1)):
        spot = SIDE - 1 if d < 0 else 0
        put_face(face, [get((d, -1, 0), 64 * spot + 56), get((d, 0, 0), 64 * spot, 64), get((d, 1, 0), 64 * spot)])
        lines = [get((0, d, 0), 64 * x + 8 * spot) for x in range(SIDE)]
        put_face(2 + face, [zeros] + lines + [zeros])
    fill_edges(get, rims, put_rim)


def add_rims(sums, n, wide, faces_even, faces_odd, edge, down, up, matrix):
    parts = range(2 if wide else 1)
    for face in range(4):
        side = 2 * (face % 2)
        blocks = [3 * side + t for t in range(3)] if face < 2 else [3 * t + side for t in range(3)]
        lhs = []
        for part in parts:
            windows = []
            for t in range(3):
                v = faces_odd[part, face] if t == 1 else faces_even[part, face, :, 8 * t : 8 * t + 64]
                windows.append(v.reshape(n * 64, 128))
            lhs.append(jnp.concatenate(windows, axis=1))
        total = line_sum(multiplied(lhs, wide, matrix, blocks), down, up)
        for b in range(n):
            if face < 2:
                sums[b, 224 * side : 224 * side + 64] += total[64 * b : 64 * b + 64]
            else:
                for x in range(SIDE):
                    at = 64 * x + 28 * side
                    sums[b, at : at + 8] += total[64 * b + 8 * x : 64 * b + 8 * x + 8]
    lhs = []
    for part in parts:
        windows = [edge[part, j, :, i : i + 8].reshape(n * 128, 128) for i in range(3) for j in range(3)]
        lhs.append(jnp.concatenate(windows, axis=1))
    ends = lambda at: jnp.concatenate([matrix[:, at : at + 128], matrix[:, at + 256 : at + 384]], axis=1)
    total = dot(lhs[0], ends(0))
    if wide:
        total = total + dot(lhs[0], ends(384)) + dot(lhs[1], ends(0))
    for b in range(n):
        for x in range(SIDE):
            at = 128 * b + 16 * x
            sums[b, pl.ds(64 * x, SIDE, stride=8)] += total[at : at + 8, 0:128]
            sums[b, pl.ds(64 * x + 7, SIDE, stride=8)] += total[at + 8 : at + 16, 128:256]


def surface_spots():
    spots = [(0, 0, 64, 1), (64, 448, 64, 1)]
    for x in range(1, 7):
        at = 128 + (x - 1) * 16
        spots += [(at, 64 * x, 8, 1), (at + 8, 64 * x + 56, 8, 1)]
    for x in range(1, 7):
        at = 224 + (x - 1) * 12
        spots += [(at, 64 * x + 8, 6, 8), (at + 6, 64 * x + 15, 6, 8)]
    return spots


def pack(get, wire):
    for at, start, size, stride in surface_spots():
        wire[at : at + size] = get(pl.ds(start, size, stride=stride) if stride > 1 else pl.ds(start, size))


def unpack(wire, brick):
    for at, start, size, stride in surface_spots():
        spot = pl.ds(start, size, stride=stride) if stride > 1 else pl.ds(start, size)
        brick[spot] = wire[at : at + size]


def unpack_pair(wire, scratch, first, second):
    a, b = doubled(wire)
    scratch[0] = parted(a)
    scratch[1] = parted(b)
    unpack(scratch.at[0], first)
    unpack(scratch.at[1], second)


def pool(v, scratch, wire):
    lines = v.reshape(4, 2, 4, 2, SIDE, 128)
    sums = (lines[:, 0, :, 0] + lines[:, 0, :, 1]) + (lines[:, 1, :, 0] + lines[:, 1, :, 1])
    scratch[...] = sums.reshape(128, 128)
    for z in range(4):
        halves = [
            scratch[pl.ds(64 * half + 2 * z, 8, stride=8)] + scratch[pl.ds(64 * half + 2 * z + 1, 8, stride=8)]
            for half in range(2)
        ]
        wire[8 * z : 8 * z + 8] = merged(*halves) * 0.125


def split_spot(octant, half, z):
    a, b, c = octant // 4, octant // 2 % 2, octant % 2
    return pl.ds(256 * b + 32 * (4 * a + 2 * half) + 4 * c + z, 8, stride=8)


def place_piece(wire, octant, brick):
    for half, v in enumerate(doubled(wire)):
        v = parted(v)
        for z in range(4):
            brick[split_spot(octant, half, z)] = v[8 * z : 8 * z + 8]


def take_pieces(brick, pieces):
    for octant in range(8):
        for z in range(4):
            halves = [brick[split_spot(octant, half, z)] for half in range(2)]
            pieces[octant, 8 * z : 8 * z + 8] = merged(*halves)


def swap_halves(v, split):
    first, second = (2, SIDE) if split else (SIDE, 2)
    return v.reshape(first, second, 32, 128).swapaxes(0, 1).reshape(VOX, 128)


def grow(piece, scratch):
    for half, v in enumerate(doubled(piece)):
        for z in range(4):
            rows = v[8 * z : 8 * z + 8]
            scratch[pl.ds(64 * half + 2 * z, 8, stride=8)] = rows
            scratch[pl.ds(64 * half + 2 * z + 1, 8, stride=8)] = rows
    lines = scratch[...].reshape(4, 1, 4, 1, SIDE, 128)
    return jnp.broadcast_to(lines, (4, 2, 4, 2, SIDE, 128)).reshape(VOX, 128)


def step_kernel(
    x_any, fine_links, own_codes, coarse_links, in_any, in_bias, down_weight, one_any, one_bias, two_any, two_bias,
    up_weight, out_any, out_bias,
    out,
    x, in_weight, one_weight, two_weight, out_weight, loads,
    matrix, last_matrix, one_matrix, two_matrix,
    even, odd, edge, wide_even, wide_odd, wide_edge, rims, shift_down, shift_up,
    faces_even, faces_odd, face_edge, wide_faces_even, wide_faces_odd, wide_face_edge, wide_sums,
    parts, turned, hidden, halves, small, grown,
    x_send, x_halo, hidden_send, hidden_halo,
    code_block, codes, code_table, table, code_scalars, table_scalars,
    pooled, placed, base, first,
    first_send, first_halo, lifted, wanted, window, low_window, high_window,
    local_sems, send_x, recv_x, send_hidden, recv_hidden, send_codes, recv_codes, send_pooled, recv_pooled,
    send_first, recv_first, send_relay, recv_relay, send_wanted, recv_wanted,
):
    group, member = lax.axis_index("grp"), lax.axis_index("dev")
    groups, members = lax.axis_size("grp"), lax.axis_size("dev")
    position = group * members + member
    whole = groups * members
    count, slots = fine_links.shape[0], coarse_links.shape[0]
    pairs = count // 2
    relayed = members == 4
    has_left, has_right = position > 0, position < whole - 1
    has_low, has_high = group > 0, group < groups - 1
    is_first, is_last = member == 0, member == members - 1
    left_at = (jnp.maximum(position - 1, 0) // members, (position + members - 1) % members)
    right_at = (jnp.minimum(position + 1, whole - 1) // members, (position + 1) % members)
    low_at = (jnp.maximum(group - 1, 0), members - 1)
    high_at = (jnp.minimum(group + 1, groups - 1), 0)
    always = position >= 0

    def fetch(k, source, target):
        return pltpu.make_async_copy(source, target, loads.at[k])

    fetches = [
        fetch(0, x_any, x), fetch(1, in_any, in_weight), fetch(2, one_any, one_weight),
        fetch(3, two_any, two_weight), fetch(4, out_any, out_weight),
    ]
    for copy in fetches:
        copy.start()

    barrier = pltpu.get_barrier_semaphore()

    def greet(where):
        pl.semaphore_signal(barrier, inc=1, device_id=where, device_id_type=MESH)

    pl.when(has_left)(lambda: greet(left_at))
    pl.when(has_right)(lambda: greet(right_at))
    for k in range(1, members):
        greet((group, (member + k) % members))
    for k in range(members):
        pl.when(is_first & has_low)(lambda k=k: greet((low_at[0], k)))
        pl.when(is_last & has_high)(lambda k=k: greet((high_at[0], k)))

    def remote(src, dst, send, recv, where):
        return pltpu.make_async_remote_copy(
            src_ref=src, dst_ref=dst, send_sem=send, recv_sem=recv, device_id=where, device_id_type=MESH
        )

    row = lax.broadcasted_iota(jnp.int32, (SIDE, 128), 0)
    block = jnp.full((SIDE, 128), -1, jnp.int32)
    for i in range(count):
        block = jnp.where(row == i, own_codes[i], block)
    code_block[...] = block
    codes[members + member] = block
    fetches[0].wait()
    for pair in range(pairs):
        turned[pair] = x[2 * pair : 2 * pair + 2].reshape(128, VOX).T
    pack(lambda spot: turned[0, spot], x_send.at[0])
    pack(lambda spot: turned[pairs - 1, spot], x_send.at[1])
    pl.semaphore_wait(
        barrier,
        jnp.where(has_left, 1, 0) + jnp.where(has_right, 1, 0) + (members - 1)
        + jnp.where(has_low, 1, 0) + jnp.where(has_high, 1, 0),
    )

    def halo_copies(source, halo, send, recv):
        to_left = remote(source.at[0], halo.at[1], send.at[0], recv.at[1], left_at)
        to_right = remote(source.at[1], halo.at[0], send.at[1], recv.at[0], right_at)
        return to_left, to_right

    def start_halo(copies):
        pl.when(has_left)(copies[0].start)
        pl.when(has_right)(copies[1].start)

    def end_halo(copies):
        pl.when(has_left)(copies[1].wait_recv)
        pl.when(has_right)(copies[0].wait_recv)

    def end_halo_sends(copies):
        pl.when(has_left)(copies[0].wait_send)
        pl.when(has_right)(copies[1].wait_send)

    def shared_copies(source, at, send, recv):
        near = [
            remote(source, at(members + member), send.at[k], recv.at[members + member], (group, (member + k) % members))
            for k in range(1, members)
        ]
        to_high = remote(source, at(member), send.at[0], recv.at[member], high_at)
        to_low = remote(source, at(2 * members + member), send.at[members], recv.at[2 * members + member], low_at)
        return near, to_high, to_low

    def start_shared(copies):
        near, to_high, to_low = copies
        for copy in near:
            copy.start()
        pl.when(has_high)(to_high.start)
        pl.when(has_low)(to_low.start)

    def end_shared(source, at, send, recv):
        for k in range(1, members):
            other = (member + k) % members
            remote(source, at(members + other), send.at[k], recv.at[members + other], (group, other)).wait_recv()
        for k in range(members):
            from_low = remote(source, at(k), send.at[0], recv.at[k], low_at)
            from_high = remote(source, at(2 * members + k), send.at[0], recv.at[2 * members + k], high_at)
            pl.when(is_first & has_low)(from_low.wait_recv)
            pl.when(is_last & has_high)(from_high.wait_recv)

    def end_shared_sends(copies):
        near, to_high, to_low = copies
        for copy in near:
            copy.wait_send()
        pl.when(has_high)(to_high.wait_send)
        pl.when(has_low)(to_low.wait_send)

    x_copies = halo_copies(x_send, x_halo, send_x, recv_x)
    start_halo(x_copies)
    code_at = lambda k: codes.at[k]
    code_copies = shared_copies(code_block, code_at, send_codes, recv_codes)
    start_shared(code_copies)

    fetches[1].wait()
    fine_matrix(in_weight, matrix)
    for pair in range(pairs):
        for one, v in enumerate(doubled(turned[pair])):
            parts[HALO + 2 * pair + one] = parted(v)

    clear_center(even, odd, False)

    def own_step(i, carry):
        fill_center(parts.at[HALO + i], False, even, odd)
        hidden[i] = center(False, even, odd, shift_down, shift_up, matrix, 0, SIDE)
        return carry

    lax.fori_loop(0, count, own_step, 0)
    end_shared(code_block, code_at, send_codes, recv_codes)
    lane = lax.broadcasted_iota(jnp.int32, (SIDE, 128), 1)
    table_rows = jnp.full((SIDE, 128), -1, jnp.int32)
    for near in range(3):
        there = position + near - 1
        valid = (there >= 0) & (there < whole)
        there = jnp.where(valid, there, position)
        there_group = there // members
        there_member = there - there_group * members
        band = there_group - group + 1
        spot = jnp.where(valid, lane, -1000) + there_member * slots * 8
        best = jnp.full((SIDE, 128), -1, jnp.int32)
        for k in range(members):
            match = (codes[band * members + k] == spot) & (row < count) & (lane < slots * 8)
            best = jnp.maximum(best, jnp.where(match, (band * members + k) * count + row, -1))
        top = jnp.max(best, axis=0, keepdims=True)
        table_rows = jnp.where(row == near, top, table_rows)
    code_table[...] = codes[pl.ds(members, members)]
    table[...] = table_rows
    to_table = pltpu.make_async_copy(table, table_scalars, local_sems.at[0])
    to_codes = pltpu.make_async_copy(code_table, code_scalars, local_sems.at[1])
    to_table.start()
    to_codes.start()
    fetches[2].wait()
    coarse_matrix(one_weight, one_matrix)
    fetches[3].wait()
    coarse_matrix(two_weight, two_matrix)
    fetches[4].wait()
    fine_matrix(out_weight, last_matrix)
    to_table.wait()
    to_codes.wait()

    fine_start = position * count - HALO
    end_halo(x_copies)
    for side, at in ((0, 0), (1, HALO + count)):
        unpack_pair(x_halo[side], halves, parts.at[at], parts.at[at + 1])
    fine_scratch = (even.at[0], odd.at[0], edge, rims, shift_down, shift_up)
    two = lambda bias: jnp.concatenate([bias[...], bias[...]], axis=1)
    in_both = two(in_bias)

    def pooled_at(i):
        return lambda k: pooled.at[k, i]

    def pooled_copies(i):
        return shared_copies(pooled.at[members + member, i], pooled_at(i), send_pooled.at[i], recv_pooled.at[i])

    def rim_step(i, carry):
        fill_rims(
            loader(parts, HALO + i), linker(fine_links, i, fine_start, HALO + i, parts.shape[0]), False, i,
            faces_even, faces_odd, face_edge, rims,
        )
        return carry

    lax.fori_loop(0, count, rim_step, 0)
    add_rims(hidden, count, False, faces_even, faces_odd, face_edge, shift_down, shift_up, matrix)

    def first_step(i, carry):
        v = hidden[i]
        v = silu(v + pltpu.roll(v, 64, 1) + in_both)
        pool(v, small, pooled.at[members + member, i])
        hidden[i] = v
        start_shared(pooled_copies(i))
        return carry

    lax.fori_loop(0, count, first_step, 0)
    pack(lambda spot: merged(hidden[0, spot], hidden[1, spot]), hidden_send.at[0])
    pack(lambda spot: merged(hidden[count - 2, spot], hidden[count - 1, spot]), hidden_send.at[1])
    hidden_copies = halo_copies(hidden_send, hidden_halo, send_hidden, recv_hidden)
    start_halo(hidden_copies)

    turned_down = down_weight[...]
    down_high = high_of(turned_down)
    down_both = jnp.concatenate([down_high, turned_down - down_high], axis=1)
    down_matrix = jnp.concatenate([down_both, down_both], axis=0).astype(BF16)
    for i in range(count):
        end_shared(pooled.at[members + member, i], pooled_at(i), send_pooled.at[i], recv_pooled.at[i])

    def base_step(slot, carry):
        for octant in range(8):
            which = table_scalars[slot // slots, slot % slots * 8 + octant]
            there_is = which >= 0
            which = jnp.where(there_is, jnp.minimum(which, 3 * members * count - 1), (members + member) * count)
            keep = jnp.where(there_is, 1.0, 0.0).astype(F32)
            place_piece(pooled[which // count, which % count] * keep, octant, placed)
        sums = dot(placed[...].astype(BF16), down_matrix)
        base[slot] = swap_halves(sums[:, 0:128] + sums[:, 128:256], True)
        return carry

    lax.fori_loop(0, 3 * slots, base_step, 0)
    coarse_start = (position - 1) * slots
    wide_scratch = (wide_even, wide_odd, wide_edge, rims, shift_down, shift_up)

    if relayed:
        parity = member % 2
        x_at = (group, member + 1 - 2 * parity)
        relay_group = group + jnp.where(member == 1, -1, 0) + jnp.where(member == 2, 1, 0)
        relays_out = (relay_group >= 0) & (relay_group < groups)
        relays_in = jnp.where(is_first, has_low, True) & jnp.where(is_last, has_high, True)
        relay_at = (jnp.clip(relay_group, 0, groups - 1), (member + 2) % members)

        def direct(i, c):
            at, rows = CHUNKS[c]
            return remote(
                first_send.at[i, pl.ds(at, rows)], first_halo.at[parity, i, pl.ds(at, rows)],
                send_first.at[i, c], recv_first.at[i, c], x_at,
            )

        def came(i, c):
            at, rows = CHUNKS[c]
            return remote(
                first_send.at[i, pl.ds(at, rows)], first_halo.at[1 - parity, i, pl.ds(at, rows)],
                send_first.at[i, c], recv_first.at[i, c], x_at,
            )

        def relay(i, c):
            at, rows = CHUNKS[c]
            return remote(
                first_halo.at[1 - parity, i, pl.ds(at, rows)], first_halo.at[parity, i, pl.ds(at, rows)],
                send_relay.at[i, c], recv_relay.at[i, c], relay_at,
            )

        def start_first(i):
            for c in range(len(CHUNKS)):
                direct(i, c).start()

        arrivals = [(i, c) for i in range(slots) for c in range(len(CHUNKS))]

        def pass_on(at):
            i, c = arrivals[at]
            came(i, c).wait_recv()
            pl.when(relays_out)(relay(i, c).start)

        def end_first(passed):
            for at in range(passed, len(arrivals)):
                pass_on(at)
            for i in range(slots):
                for c in range(len(CHUNKS)):
                    pl.when(relays_in)(relay(i, c).wait_recv)

        def end_first_sends():
            for i in range(slots):
                for c in range(len(CHUNKS)):
                    direct(i, c).wait_send()
                    pl.when(relays_out)(relay(i, c).wait_send)
    else:

        def sides(i):
            to_left = remote(first_send.at[i], first_halo.at[1, i], send_first.at[i, 0], recv_first.at[i, 1], left_at)
            to_right = remote(first_send.at[i], first_halo.at[0, i], send_first.at[i, 1], recv_first.at[i, 0], right_at)
            return to_left, to_right

        def start_first(i):
            start_halo(sides(i))

        def pass_on(at):
            pass

        def end_first(passed):
            for i in range(slots):
                end_halo(sides(i))

        def end_first_sends():
            for i in range(slots):
                end_halo_sends(sides(i))

    def second_step(i, carry):
        v = silu(coarse_conv(base, slots + i, coarse_start, coarse_links, i, wide_scratch, one_matrix) + one_bias[...])
        first[slots + i] = v
        pack(lambda spot: first[slots + i, spot], first_send.at[i])
        start_first(i)
        return carry

    lax.fori_loop(0, slots, second_step, 0)
    turned_up = up_weight[...].T
    up_high = high_of(turned_up)
    up_both = jnp.concatenate([up_high, turned_up - up_high], axis=1)
    up_matrix = jnp.concatenate([up_both, up_both], axis=0).astype(BF16)
    clear_center(wide_even, wide_odd, True)
    passed = 0
    for i in range(slots):
        fill_center(first.at[slots + i], True, wide_even, wide_odd)
        for half in range(2):
            pass_on(passed)
            passed += 1
            spot = slice(256 * half, 256 * half + 256)
            wide_sums[i, spot] = center(
                True, wide_even, wide_odd, shift_down, shift_up, two_matrix, 4 * half, 4 * half + 4
            )
    end_first(passed)
    for side, at in ((0, 0), (1, 2 * slots)):
        for i in range(slots):
            unpack(first_halo.at[side, i], first.at[at + i])

    def wide_rim_step(i, carry):
        fill_rims(
            loader(first, slots + i), linker(coarse_links, i, coarse_start, slots + i, first.shape[0]), True, i,
            wide_faces_even, wide_faces_odd, wide_face_edge, rims,
        )
        return carry

    lax.fori_loop(0, slots, wide_rim_step, 0)
    add_rims(
        wide_sums, slots, True, wide_faces_even, wide_faces_odd, wide_face_edge, shift_down, shift_up, two_matrix
    )

    def third_step(i, carry):
        v = silu(wide_sums[i] + two_bias[...])
        high = v.astype(BF16)
        low = (v - high.astype(F32)).astype(BF16)
        sums = dot(jnp.concatenate([high, low], axis=1), up_matrix)
        placed[...] = swap_halves(sums + pltpu.roll(sums, 64, 1), False)
        take_pieces(placed, lifted.at[pl.ds(i * 8, 8)])
        return carry

    lax.fori_loop(0, slots, third_step, 0)
    bricks = members * count
    zeros = jnp.zeros((HALO,) + wanted.shape[1:], F32)
    wanted[0:HALO] = zeros
    wanted[HALO + bricks :] = zeros

    def choose(j, carry):
        code = code_scalars[j // count, j % count, 0] - member * slots * 8
        mine = (code >= 0) & (code < slots * 8)
        keep = jnp.where(mine, 1.0, 0.0).astype(F32)
        wanted[HALO + j] = lifted[jnp.where(mine, code, 0)] * keep
        return carry

    lax.fori_loop(0, bricks, choose, 0)
    parts_of = ((HALO, count, None), (0, HALO, 0), (HALO + count, HALO, members - 1))

    def to_member(k, part):
        other = (member + k) % members
        at, rows, _ = parts_of[part]
        return remote(
            wanted.at[pl.ds(other * count + at, rows)], window.at[member, pl.ds(at, rows)], send_wanted.at[k, part],
            recv_wanted.at[members + member, part], (group, other),
        )

    def from_member(k, part):
        other = (member + k) % members
        at, rows, _ = parts_of[part]
        return remote(
            wanted.at[pl.ds(at, rows)], window.at[other, pl.ds(at, rows)], send_wanted.at[k, part],
            recv_wanted.at[members + other, part], (group, other),
        )

    def when_read(who, part, action):
        none_at = parts_of[part][2]
        if none_at is None:
            action()
        else:
            pl.when(who != none_at)(action)

    to_high = remote(
        wanted.at[pl.ds(bricks, HALO)], low_window.at[member], send_wanted.at[0, 0], recv_wanted.at[member, 0], high_at
    )
    to_low = remote(
        wanted.at[pl.ds(HALO, HALO)], high_window.at[member], send_wanted.at[members, 0],
        recv_wanted.at[2 * members + member, 0], low_at,
    )
    for k in range(1, members):
        to_member(k, 0).start()
    for k in range(1, members):
        for part in (1, 2):
            when_read((member + k) % members, part, to_member(k, part).start)
    pl.when(has_high)(to_high.start)
    pl.when(has_low)(to_low.start)
    window[member] = wanted[pl.ds(member * count, count + 2 * HALO)]
    end_halo(hidden_copies)
    for k in range(1, members):
        from_member(k, 0).wait_recv()

    def total(source, i):
        piece = source[0, i]
        for owner in range(1, members):
            piece = piece + source[owner, i]
        return piece

    def own_blend(i, carry):
        rising = grow(total(window, HALO + i), small)
        parts[HALO + i] = parted(silu(hidden[i] + rising))
        return carry

    lax.fori_loop(0, count, own_blend, 0)
    for k in range(1, members):
        for part in (1, 2):
            when_read(member, part, from_member(k, part).wait_recv)
    for k in range(members):
        spot = wanted.at[pl.ds(0, HALO)]
        from_low = remote(spot, low_window.at[k], send_wanted.at[0, 0], recv_wanted.at[k, 0], low_at)
        from_high = remote(
            spot, high_window.at[k], send_wanted.at[0, 0], recv_wanted.at[2 * members + k, 0], high_at
        )
        pl.when(is_first & has_low)(from_low.wait_recv)
        pl.when(is_last & has_high)(from_high.wait_recv)
    for side, at, edge_window, beyond in (
        (0, 0, low_window, is_first), (1, HALO + count, high_window, is_last),
    ):
        for one in range(HALO):
            piece = jnp.where(beyond, total(edge_window, one), total(window, at + one))
            grown[one] = grow(piece, small)
        pack(lambda spot: merged(grown[0, spot], grown[1, spot]), halves.at[0])
        wire = silu(hidden_halo[side] + halves[0])
        unpack_pair(wire, halves, parts.at[at], parts.at[at + 1])
    out_both = two(out_bias)

    def last_step(i, carry):
        hidden[i] = fine_conv(parts, HALO + i, fine_start, fine_links, i, fine_scratch, last_matrix) + out_both
        return carry

    lax.fori_loop(0, count, last_step, 0)
    for pair in range(pairs):
        flat = merged(hidden[2 * pair], hidden[2 * pair + 1]).T
        out[2 * pair : 2 * pair + 2] = x[2 * pair : 2 * pair + 2] + flat.reshape(2, 64, VOX)

    end_halo_sends(x_copies)
    end_shared_sends(code_copies)
    for i in range(count):
        end_shared_sends(pooled_copies(i))
    end_halo_sends(hidden_copies)
    end_first_sends()
    for k in range(1, members):
        to_member(k, 0).wait_send()
        for part in (1, 2):
            when_read((member + k) % members, part, to_member(k, part).wait_send)
    pl.when(has_high)(to_high.wait_send)
    pl.when(has_low)(to_low.wait_send)


def per_device(
    x, fine_links, parent_codes, coarse_links,
    in_weight, in_bias, down, one_weight, one_bias, two_weight, two_bias, up, out_weight, out_bias,
):
    count, channels = x.shape[0], x.shape[1]
    slots, wide = coarse_links.shape[0], one_bias.shape[0]
    members = lax.axis_size("dev")
    row = lambda bias: bias.reshape(1, -1)
    vmem = pl.BlockSpec(memory_space=pltpu.VMEM)
    smem = pl.BlockSpec(memory_space=pltpu.SMEM)
    anywhere = pl.BlockSpec(memory_space=pl.ANY)
    floats = lambda *shape: pltpu.VMEM(shape, F32)
    halfs = lambda *shape: pltpu.VMEM(shape, BF16)
    ints = lambda *shape: pltpu.VMEM(shape, jnp.int32)
    sems = lambda *shape: pltpu.SemaphoreType.DMA(shape)
    span = count + 2 * HALO
    wire = (32, 128)
    scratch = [
        floats(*x.shape), floats(*in_weight.shape), floats(*one_weight.shape), floats(*two_weight.shape),
        floats(*out_weight.shape), sems(5),
        halfs(1152, 384), halfs(1152, 384), halfs(1152, 768), halfs(1152, 768),
        halfs(1, 10, 80, 128), halfs(1, 10, 64, 128), halfs(3, 10, 16, 128),
        halfs(2, 10, 80, 128), halfs(2, 10, 64, 128), halfs(2, 3, 10, 16, 128),
        floats(2, 10 * LINE, 128), floats(VOX + 16, 128), floats(VOX + 16, 128),
        halfs(1, 4, count, 80, 128), halfs(1, 4, count, 64, 128), halfs(1, 3, count, 10, 16, 128),
        halfs(2, 4, slots, 80, 128), halfs(2, 4, slots, 64, 128), halfs(2, 3, slots, 10, 16, 128),
        floats(slots, VOX, 128),
        floats(span, VOX, 128), floats(count // 2, VOX, 128), floats(count, VOX, 128),
        floats(2, SURFACE, 128), floats(128, 128), floats(HALO, VOX, 128),
        floats(2, SURFACE, 128), floats(2, SURFACE, 128), floats(2, SURFACE, 128), floats(2, SURFACE, 128),
        ints(8, 128), ints(3 * members, 8, 128), ints(members, 8, 128), ints(8, 128),
        pltpu.SMEM((members, 8, 128), jnp.int32), pltpu.SMEM((8, 128), jnp.int32),
        floats(3 * members, count, *wire), floats(VOX, 128), floats(3 * slots, VOX, 128), floats(3 * slots, VOX, 128),
        floats(slots, SURFACE, 128), floats(2, slots, SURFACE, 128), floats(slots * 8, *wire),
        floats(members * count + 2 * HALO, *wire), floats(members, span, *wire), floats(members, HALO, *wire),
        floats(members, HALO, *wire),
        sems(2), sems(2), sems(2), sems(2), sems(2), sems(members + 1), sems(3 * members),
        sems(count, members + 1), sems(count, 3 * members),
        sems(slots, 3), sems(slots, 3), sems(slots, 3), sems(slots, 3), sems(members + 1, 3), sems(3 * members, 3),
    ]
    return pl.pallas_call(
        step_kernel,
        out_shape=jax.ShapeDtypeStruct(x.shape, F32),
        in_specs=[anywhere, smem, smem, smem, anywhere, vmem, vmem, anywhere, vmem, anywhere, vmem, vmem, anywhere, vmem],
        out_specs=vmem,
        scratch_shapes=scratch,
        name="step",
        compiler_params=pltpu.CompilerParams(collective_id=1, has_side_effects=True, vmem_limit_bytes=LIMIT),
    )(
        x, fine_links, parent_codes, coarse_links, in_weight, row(in_bias), down.T, one_weight, row(one_bias),
        two_weight, row(two_bias), up, out_weight, row(out_bias),
    )


def solution(mesh):
    bricks = P(("grp", "dev"), None, None)
    rows = P(("grp", "dev"), None)
    placed = (bricks, rows, P(("grp", "dev")), rows) + (P(),) * 10
    return jax.shard_map(per_device, mesh=mesh, in_specs=placed, out_specs=bricks, check_vma=False)
```

```python
import functools

import jax
import jax.numpy as jnp
from jax import lax
from jax.experimental import pallas as pl
from jax.experimental.pallas import tpu as pltpu
from jax.sharding import PartitionSpec as P

F32 = jnp.float32
BF16 = jnp.bfloat16
MESH = pl.DeviceIdType.MESH
SIDE = 8
VOX = SIDE * SIDE * SIDE
HALO = 2
SURFACE = VOX - 6 * 6 * 6
LINE = 24
LIMIT = 62 * 1024 * 1024
CHUNKS = ((0, 96), (96, 96), (192, 104))

offsets = [(x, y, z) for x in (-1, 0, 1) for y in (-1, 0, 1) for z in (-1, 0, 1)]
columns = {o: k for k, o in enumerate(o for o in offsets if o != (0, 0, 0))}


def high_of(v):
    return v.astype(BF16).astype(F32)


def silu(v):
    return v / (1.0 + jnp.exp(-v))


def dot(a, b):
    return lax.dot_general(a, b, (((1,), (0,)), ((), ())), preferred_element_type=F32)


def first_half(v):
    return lax.broadcasted_iota(jnp.int32, v.shape, 1) < v.shape[1] // 2


def merged(a, b):
    return jnp.where(first_half(a), a, b)


def doubled(v):
    turned = pltpu.roll(v, v.shape[1] // 2, 1)
    return merged(v, turned), merged(turned, v)


def parted(v):
    high = high_of(v)
    return merged(high, v - high)


def fill(load, link, put, rims, put_rim):
    found = {o: link(o) for o in columns}

    def get(o, start, size=SIDE, stride=1):
        row, keep = found[o]
        return load(row, start, size, stride) * keep

    for px in range(SIDE + 2):
        dx = -1 if px == 0 else (1 if px == SIDE + 1 else 0)
        x = {-1: SIDE - 1, 0: px - 1, 1: 0}[dx]
        low = get((dx, -1, 0), 64 * x + 56)
        high = get((dx, 1, 0), 64 * x)
        middle = get((dx, 0, 0), 64 * x, 64) if dx else load(None, 64 * x, 64, 1)
        put(px, jnp.concatenate([low, middle, high], axis=0))
    fill_edges(get, rims, put_rim)


def fill_edges(get, rims, put_rim):
    for plane, dz in enumerate((-1, 1)):
        z = SIDE - 1 if dz < 0 else 0
        for px in range(SIDE + 2):
            dx = -1 if px == 0 else (1 if px == SIDE + 1 else 0)
            x = {-1: SIDE - 1, 0: px - 1, 1: 0}[dx]
            rims[plane, px * LINE + 8 : px * LINE + 16] = get((dx, 0, dz), 64 * x + z, SIDE, 8)
            if dx:
                for dy in (-1, 1):
                    y = SIDE - 1 if dy < 0 else 0
                    at = px * LINE + (7 if dy < 0 else 16)
                    rims[plane, at : at + 1] = get((dx, dy, dz), 64 * x + 8 * y + z, 1)
        for dy in (-1, 1):
            y = SIDE - 1 if dy < 0 else 0
            at = LINE + (7 if dy < 0 else 16)
            rims[plane, pl.ds(at, SIDE, stride=LINE)] = get((0, dy, dz), 8 * y + z, SIDE, 64)
    for j in range(3):
        for px in range(SIDE + 2):
            at = px * LINE + 7 + j
            put_rim(j, px, jnp.concatenate([rims[0, at : at + 8], rims[1, at : at + 8]], axis=0))


def stacked(even, odd, edge):
    mains, rims = [], []
    for i in range(3):
        for j in range(3):
            main = odd[i : i + 8] if j == 1 else even[i : i + 8, 8 * j : 8 * j + 64]
            mains.append(main.reshape(VOX, 128))
            rims.append(edge[j, i : i + 8].reshape(128, 128))
    return jnp.concatenate(mains, axis=1), jnp.concatenate(rims, axis=1)


def shifted_sum(blocks, edges, down, up):
    before, here, after = blocks
    down[8 : VOX + 8] = before
    up[8 : VOX + 8] = after
    for x in range(SIDE):
        down[pl.ds(7 + 64 * x, SIDE, stride=8)] = edges[16 * x : 16 * x + 8, 0:128]
        up[pl.ds(16 + 64 * x, SIDE, stride=8)] = edges[16 * x + 8 : 16 * x + 16, 128:256]
    return down[7 : VOX + 7] + here + up[9 : VOX + 9]


def fine_matrix(weight, matrix):
    w = weight[...]
    high = high_of(w)
    both = jnp.concatenate([high, w - high], axis=0).T.astype(BF16)
    for tap in range(27):
        rows, cols = tap // 3 * 128, tap % 3 * 128
        block = both[64 * tap : 64 * tap + 64]
        matrix[rows : rows + 64, cols : cols + 128] = block
        matrix[rows + 64 : rows + 128, cols : cols + 128] = block


def coarse_matrix(weight, matrix):
    for tap in range(27):
        rows, cols = tap // 3 * 128, tap % 3 * 128
        block = weight[:, 128 * tap : 128 * tap + 128].T
        high = high_of(block)
        matrix[rows : rows + 128, cols : cols + 128] = high.astype(BF16)
        matrix[rows : rows + 128, 384 + cols : 384 + cols + 128] = (block - high).astype(BF16)


def linker(links, brick, start, own, rows):
    def link(o):
        there = links[brick, columns[o]]
        there_is = there >= 0
        row = jnp.where(there_is, jnp.clip(there - start, 0, rows - 1), own)
        return row, jnp.where(there_is, 1.0, 0.0).astype(F32)

    return link


def loader(parts, own):
    def load(row, start, size, stride):
        row = own if row is None else row
        if stride == 1:
            return parts[row, start : start + size]
        return parts[row, pl.ds(start, size, stride=stride)]

    return load


def fine_conv(parts, own, start, links, brick, scratch, matrix):
    even, odd, edge, rims, down, up = scratch

    def put(px, v):
        even[px] = v.astype(BF16)
        odd[px] = v[8:72].astype(BF16)

    def put_rim(j, px, v):
        edge[j, px] = v.astype(BF16)

    fill(loader(parts, own), linker(links, brick, start, own, parts.shape[0]), put, rims, put_rim)
    main, rim = stacked(even, odd, edge)
    sums = dot(main, matrix[...])
    ends = lambda at: jnp.concatenate([matrix[:, at : at + 128], matrix[:, at + 256 : at + 384]], axis=1)
    edges = dot(rim, ends(0))
    out = shifted_sum([sums[:, 128 * k : 128 * k + 128] for k in range(3)], edges, down, up)
    return out + pltpu.roll(out, 64, 1)


def coarse_conv(parts, own, start, links, brick, scratch, matrix):
    even, odd, edge, rims, down, up = scratch

    def put(px, v):
        high = v.astype(BF16)
        low = (v - high.astype(F32)).astype(BF16)
        for part, value in enumerate((high, low)):
            even[part, px] = value
        middle = v[8:72]
        high = middle.astype(BF16)
        odd[0, px] = high
        odd[1, px] = (middle - high.astype(F32)).astype(BF16)

    def put_rim(j, px, v):
        high = v.astype(BF16)
        edge[0, j, px] = high
        edge[1, j, px] = (v - high.astype(F32)).astype(BF16)

    fill(loader(parts, own), linker(links, brick, start, own, parts.shape[0]), put, rims, put_rim)
    (main_0, rim_0), (main_1, rim_1) = (stacked(even.at[p], odd.at[p], edge.at[p]) for p in range(2))
    tops = dot(main_0, matrix[...])
    rests = dot(main_1, matrix[:, 0:384])
    ends = lambda at: jnp.concatenate([matrix[:, at : at + 128], matrix[:, at + 256 : at + 384]], axis=1)
    edges = dot(rim_0, ends(0)) + dot(rim_0, ends(384)) + dot(rim_1, ends(0))
    cut = lambda v, at: v[:, 128 * at : 128 * at + 128]
    blocks = [cut(tops, k) + cut(tops, 3 + k) + cut(rests, k) for k in range(3)]
    return shifted_sum(blocks, edges, down, up)


def pieces_of(v, wide):
    high = v.astype(BF16)
    return (high, (v - high.astype(F32)).astype(BF16)) if wide else (high,)


def multiplied(lhs, wide, matrix, blocks):
    rows = [matrix.at[pl.ds(128 * at, 128)] for at in blocks]
    take = lambda cols: jnp.concatenate([r[:, cols] for r in rows], axis=0)
    cut = lambda v, at: v[:, 128 * at : 128 * at + 128]
    if not wide:
        sums = dot(lhs[0], take(slice(0, 384)))
        return [cut(sums, k) for k in range(3)]
    tops, rests = dot(lhs[0], take(slice(0, 768))), dot(lhs[1], take(slice(0, 384)))
    return [cut(tops, k) + cut(tops, 3 + k) + cut(rests, k) for k in range(3)]


def line_sum(blocks, down, up):
    rows = blocks[0].shape[0]
    down[8 : rows + 8] = blocks[0]
    up[8 : rows + 8] = blocks[2]
    zeros = jnp.zeros((SIDE, 128), F32)
    for at in range(0, rows, 64):
        down[pl.ds(7 + at, SIDE, stride=8)] = zeros
        up[pl.ds(16 + at, SIDE, stride=8)] = zeros
    return down[7 : rows + 7] + blocks[1] + up[9 : rows + 9]


def clear_center(even, odd, wide):
    for part in range(2 if wide else 1):
        for px in (0, SIDE + 1):
            even[part, px] = jnp.zeros(even.shape[2:], BF16)
            odd[part, px] = jnp.zeros(odd.shape[2:], BF16)


def fill_center(brick, wide, even, odd):
    zeros = jnp.zeros((SIDE, 128), F32)
    for x in range(SIDE):
        middle = brick[64 * x : 64 * x + 64]
        for part, v in enumerate(pieces_of(jnp.concatenate([zeros, middle, zeros], axis=0), wide)):
            even[part, x + 1] = v
        for part, v in enumerate(pieces_of(middle, wide)):
            odd[part, x + 1] = v


def center(wide, even, odd, down, up, matrix, first, last):
    def taps(part):
        windows = []
        for i in range(3):
            for j in range(3):
                xs = slice(first + i, last + i)
                v = odd[part, xs] if j == 1 else even[part, xs, 8 * j : 8 * j + 64]
                windows.append(v.reshape((last - first) * 64, 128))
        return jnp.concatenate(windows, axis=1)

    lhs = [taps(part) for part in range(2 if wide else 1)]
    return line_sum(multiplied(lhs, wide, matrix, range(9)), down, up)


def fill_rims(load, link, wide, at, faces_even, faces_odd, edge, rims):
    found = {o: link(o) for o in columns}
    zeros = jnp.zeros((SIDE, 128), F32)

    def get(o, start, size=SIDE, stride=1):
        row, keep = found[o]
        return load(row, start, size, stride) * keep

    def put_face(face, lines):
        v = jnp.concatenate(lines, axis=0)
        for part, value in enumerate(pieces_of(v, wide)):
            faces_even[part, face, at] = value
        for part, value in enumerate(pieces_of(v[8:72], wide)):
            faces_odd[part, face, at] = value

    def put_rim(j, px, v):
        for part, value in enumerate(pieces_of(v, wide)):
            edge[part, j, at, px] = value

    for face, d in enumerate((-1, 1)):
        spot = SIDE - 1 if d < 0 else 0
        put_face(face, [get((d, -1, 0), 64 * spot + 56), get((d, 0, 0), 64 * spot, 64), get((d, 1, 0), 64 * spot)])
        lines = [get((0, d, 0), 64 * x + 8 * spot) for x in range(SIDE)]
        put_face(2 + face, [zeros] + lines + [zeros])
    fill_edges(get, rims, put_rim)


def add_rims(sums, n, wide, faces_even, faces_odd, edge, down, up, matrix):
    parts = range(2 if wide else 1)
    for face in range(4):
        side = 2 * (face % 2)
        blocks = [3 * side + t for t in range(3)] if face < 2 else [3 * t + side for t in range(3)]
        lhs = []
        for part in parts:
            windows = []
            for t in range(3):
                v = faces_odd[part, face] if t == 1 else faces_even[part, face, :, 8 * t : 8 * t + 64]
                windows.append(v.reshape(n * 64, 128))
            lhs.append(jnp.concatenate(windows, axis=1))
        total = line_sum(multiplied(lhs, wide, matrix, blocks), down, up)
        for b in range(n):
            if face < 2:
                sums[b, 224 * side : 224 * side + 64] += total[64 * b : 64 * b + 64]
            else:
                for x in range(SIDE):
                    at = 64 * x + 28 * side
                    sums[b, at : at + 8] += total[64 * b + 8 * x : 64 * b + 8 * x + 8]
    lhs = []
    for part in parts:
        windows = [edge[part, j, :, i : i + 8].reshape(n * 128, 128) for i in range(3) for j in range(3)]
        lhs.append(jnp.concatenate(windows, axis=1))
    ends = lambda at: jnp.concatenate([matrix[:, at : at + 128], matrix[:, at + 256 : at + 384]], axis=1)
    total = dot(lhs[0], ends(0))
    if wide:
        total = total + dot(lhs[0], ends(384)) + dot(lhs[1], ends(0))
    for b in range(n):
        for x in range(SIDE):
            at = 128 * b + 16 * x
            sums[b, pl.ds(64 * x, SIDE, stride=8)] += total[at : at + 8, 0:128]
            sums[b, pl.ds(64 * x + 7, SIDE, stride=8)] += total[at + 8 : at + 16, 128:256]


def surface_spots():
    spots = [(0, 0, 64, 1), (64, 448, 64, 1)]
    for x in range(1, 7):
        at = 128 + (x - 1) * 16
        spots += [(at, 64 * x, 8, 1), (at + 8, 64 * x + 56, 8, 1)]
    for x in range(1, 7):
        at = 224 + (x - 1) * 12
        spots += [(at, 64 * x + 8, 6, 8), (at + 6, 64 * x + 15, 6, 8)]
    return spots


def pack(get, wire):
    for at, start, size, stride in surface_spots():
        wire[at : at + size] = get(pl.ds(start, size, stride=stride) if stride > 1 else pl.ds(start, size))


def unpack(wire, brick):
    for at, start, size, stride in surface_spots():
        spot = pl.ds(start, size, stride=stride) if stride > 1 else pl.ds(start, size)
        brick[spot] = wire[at : at + size]


def unpack_pair(wire, scratch, first, second):
    a, b = doubled(wire)
    scratch[0] = parted(a)
    scratch[1] = parted(b)
    unpack(scratch.at[0], first)
    unpack(scratch.at[1], second)


def pool(v, scratch, wire):
    lines = v.reshape(4, 2, 4, 2, SIDE, 128)
    sums = (lines[:, 0, :, 0] + lines[:, 0, :, 1]) + (lines[:, 1, :, 0] + lines[:, 1, :, 1])
    scratch[...] = sums.reshape(128, 128)
    for z in range(4):
        halves = [
            scratch[pl.ds(64 * half + 2 * z, 8, stride=8)] + scratch[pl.ds(64 * half + 2 * z + 1, 8, stride=8)]
            for half in range(2)
        ]
        wire[8 * z : 8 * z + 8] = merged(*halves) * 0.125


def split_spot(octant, half, z):
    a, b, c = octant // 4, octant // 2 % 2, octant % 2
    return pl.ds(256 * b + 32 * (4 * a + 2 * half) + 4 * c + z, 8, stride=8)


def place_piece(wire, octant, brick):
    for half, v in enumerate(doubled(wire)):
        v = parted(v)
        for z in range(4):
            brick[split_spot(octant, half, z)] = v[8 * z : 8 * z + 8]


def take_pieces(brick, pieces):
    for octant in range(8):
        for z in range(4):
            halves = [brick[split_spot(octant, half, z)] for half in range(2)]
            pieces[octant, 8 * z : 8 * z + 8] = merged(*halves)


def swap_halves(v, split):
    first, second = (2, SIDE) if split else (SIDE, 2)
    return v.reshape(first, second, 32, 128).swapaxes(0, 1).reshape(VOX, 128)


def grow(piece, scratch):
    for half, v in enumerate(doubled(piece)):
        for z in range(4):
            rows = v[8 * z : 8 * z + 8]
            scratch[pl.ds(64 * half + 2 * z, 8, stride=8)] = rows
            scratch[pl.ds(64 * half + 2 * z + 1, 8, stride=8)] = rows
    lines = scratch[...].reshape(4, 1, 4, 1, SIDE, 128)
    return jnp.broadcast_to(lines, (4, 2, 4, 2, SIDE, 128)).reshape(VOX, 128)


def step_kernel(
    x_any, fine_links, own_codes, coarse_links, in_any, in_bias, down_weight, one_any, one_bias, two_any, two_bias,
    up_weight, out_any, out_bias,
    out,
    x, in_weight, one_weight, two_weight, out_weight, loads,
    matrix, last_matrix, one_matrix, two_matrix,
    even, odd, edge, wide_even, wide_odd, wide_edge, rims, shift_down, shift_up,
    faces_even, faces_odd, face_edge, wide_faces_even, wide_faces_odd, wide_face_edge, wide_sums,
    parts, turned, hidden, halves, small, grown,
    x_send, x_halo, hidden_send, hidden_halo,
    code_block, codes, code_table, table, code_scalars, table_scalars,
    pooled, placed, base, first,
    first_send, first_halo, lifted, wanted, window, low_window, high_window,
    local_sems, send_x, recv_x, send_hidden, recv_hidden, send_codes, recv_codes, send_pooled, recv_pooled,
    send_first, recv_first, send_relay, recv_relay, send_wanted, recv_wanted,
):
    group, member = lax.axis_index("grp"), lax.axis_index("dev")
    groups, members = lax.axis_size("grp"), lax.axis_size("dev")
    position = group * members + member
    whole = groups * members
    count, slots = fine_links.shape[0], coarse_links.shape[0]
    pairs = count // 2
    relayed = members == 4
    has_left, has_right = position > 0, position < whole - 1
    has_low, has_high = group > 0, group < groups - 1
    is_first, is_last = member == 0, member == members - 1
    left_at = (jnp.maximum(position - 1, 0) // members, (position + members - 1) % members)
    right_at = (jnp.minimum(position + 1, whole - 1) // members, (position + 1) % members)
    low_at = (jnp.maximum(group - 1, 0), members - 1)
    high_at = (jnp.minimum(group + 1, groups - 1), 0)
    always = position >= 0

    def fetch(k, source, target):
        return pltpu.make_async_copy(source, target, loads.at[k])

    fetches = [
        fetch(0, x_any, x), fetch(1, in_any, in_weight), fetch(2, one_any, one_weight),
        fetch(3, two_any, two_weight), fetch(4, out_any, out_weight),
    ]
    for copy in fetches:
        copy.start()

    barrier = pltpu.get_barrier_semaphore()

    def greet(where):
        pl.semaphore_signal(barrier, inc=1, device_id=where, device_id_type=MESH)

    pl.when(has_left)(lambda: greet(left_at))
    pl.when(has_right)(lambda: greet(right_at))
    for k in range(1, members):
        greet((group, (member + k) % members))
    for k in range(members):
        pl.when(is_first & has_low)(lambda k=k: greet((low_at[0], k)))
        pl.when(is_last & has_high)(lambda k=k: greet((high_at[0], k)))

    def remote(src, dst, send, recv, where):
        return pltpu.make_async_remote_copy(
            src_ref=src, dst_ref=dst, send_sem=send, recv_sem=recv, device_id=where, device_id_type=MESH
        )

    row = lax.broadcasted_iota(jnp.int32, (SIDE, 128), 0)
    block = jnp.full((SIDE, 128), -1, jnp.int32)
    for i in range(count):
        block = jnp.where(row == i, own_codes[i], block)
    code_block[...] = block
    codes[members + member] = block
    fetches[0].wait()
    for pair in range(pairs):
        turned[pair] = x[2 * pair : 2 * pair + 2].reshape(128, VOX).T
    pack(lambda spot: turned[0, spot], x_send.at[0])
    pack(lambda spot: turned[pairs - 1, spot], x_send.at[1])
    pl.semaphore_wait(
        barrier,
        jnp.where(has_left, 1, 0) + jnp.where(has_right, 1, 0) + (members - 1)
        + jnp.where(has_low, 1, 0) + jnp.where(has_high, 1, 0),
    )

    def halo_copies(source, halo, send, recv):
        to_left = remote(source.at[0], halo.at[1], send.at[0], recv.at[1], left_at)
        to_right = remote(source.at[1], halo.at[0], send.at[1], recv.at[0], right_at)
        return to_left, to_right

    def start_halo(copies):
        pl.when(has_left)(copies[0].start)
        pl.when(has_right)(copies[1].start)

    def end_halo(copies):
        pl.when(has_left)(copies[1].wait_recv)
        pl.when(has_right)(copies[0].wait_recv)

    def end_halo_sends(copies):
        pl.when(has_left)(copies[0].wait_send)
        pl.when(has_right)(copies[1].wait_send)

    def shared_copies(source, at, send, recv):
        near = [
            remote(source, at(members + member), send.at[k], recv.at[members + member], (group, (member + k) % members))
            for k in range(1, members)
        ]
        to_high = remote(source, at(member), send.at[0], recv.at[member], high_at)
        to_low = remote(source, at(2 * members + member), send.at[members], recv.at[2 * members + member], low_at)
        return near, to_high, to_low

    def start_shared(copies):
        near, to_high, to_low = copies
        for copy in near:
            copy.start()
        pl.when(has_high)(to_high.start)
        pl.when(has_low)(to_low.start)

    def end_near(source, at, send, recv):
        for k in range(1, members):
            other = (member + k) % members
            remote(source, at(members + other), send.at[k], recv.at[members + other], (group, other)).wait_recv()

    def end_far(source, at, send, recv):
        for k in range(members):
            from_low = remote(source, at(k), send.at[0], recv.at[k], low_at)
            from_high = remote(source, at(2 * members + k), send.at[0], recv.at[2 * members + k], high_at)
            pl.when(is_first & has_low)(from_low.wait_recv)
            pl.when(is_last & has_high)(from_high.wait_recv)

    def end_shared_sends(copies):
        near, to_high, to_low = copies
        for copy in near:
            copy.wait_send()
        pl.when(has_high)(to_high.wait_send)
        pl.when(has_low)(to_low.wait_send)

    x_copies = halo_copies(x_send, x_halo, send_x, recv_x)
    start_halo(x_copies)
    code_at = lambda k: codes.at[k]
    code_copies = shared_copies(code_block, code_at, send_codes, recv_codes)
    start_shared(code_copies)

    fetches[1].wait()
    fine_matrix(in_weight, matrix)
    for pair in range(pairs):
        for one, v in enumerate(doubled(turned[pair])):
            parts[HALO + 2 * pair + one] = parted(v)

    clear_center(even, odd, False)

    def own_step(i, carry):
        fill_center(parts.at[HALO + i], False, even, odd)
        hidden[i] = center(False, even, odd, shift_down, shift_up, matrix, 0, SIDE)
        return carry

    lax.fori_loop(0, count, own_step, 0)
    end_near(code_block, code_at, send_codes, recv_codes)
    end_far(code_block, code_at, send_codes, recv_codes)
    lane = lax.broadcasted_iota(jnp.int32, (SIDE, 128), 1)
    table_rows = jnp.full((SIDE, 128), -1, jnp.int32)
    for near in range(3):
        there = position + near - 1
        valid = (there >= 0) & (there < whole)
        there = jnp.where(valid, there, position)
        there_group = there // members
        there_member = there - there_group * members
        band = there_group - group + 1
        spot = jnp.where(valid, lane, -1000) + there_member * slots * 8
        best = jnp.full((SIDE, 128), -1, jnp.int32)
        for k in range(members):
            match = (codes[band * members + k] == spot) & (row < count) & (lane < slots * 8)
            best = jnp.maximum(best, jnp.where(match, (band * members + k) * count + row, -1))
        top = jnp.max(best, axis=0, keepdims=True)
        table_rows = jnp.where(row == near, top, table_rows)
    code_table[...] = codes[pl.ds(members, members)]
    table[...] = table_rows
    to_table = pltpu.make_async_copy(table, table_scalars, local_sems.at[0])
    to_codes = pltpu.make_async_copy(code_table, code_scalars, local_sems.at[1])
    to_table.start()
    to_codes.start()

    fine_start = position * count - HALO
    end_halo(x_copies)
    for side, at in ((0, 0), (1, HALO + count)):
        unpack_pair(x_halo[side], halves, parts.at[at], parts.at[at + 1])
    fine_scratch = (even.at[0], odd.at[0], edge, rims, shift_down, shift_up)
    two = lambda bias: jnp.concatenate([bias[...], bias[...]], axis=1)
    in_both = two(in_bias)

    def pooled_at(i):
        return lambda k: pooled.at[k, i]

    def pooled_copies(i):
        return shared_copies(pooled.at[members + member, i], pooled_at(i), send_pooled.at[i], recv_pooled.at[i])

    def rim_step(i, carry):
        fill_rims(
            loader(parts, HALO + i), linker(fine_links, i, fine_start, HALO + i, parts.shape[0]), False, i,
            faces_even, faces_odd, face_edge, rims,
        )
        return carry

    lax.fori_loop(0, count, rim_step, 0)
    add_rims(hidden, count, False, faces_even, faces_odd, face_edge, shift_down, shift_up, matrix)

    def first_step(i, carry):
        v = hidden[i]
        v = silu(v + pltpu.roll(v, 64, 1) + in_both)
        pool(v, small, pooled.at[members + member, i])
        hidden[i] = v
        start_shared(pooled_copies(i))
        return carry

    lax.fori_loop(0, count, first_step, 0)
    pack(lambda spot: merged(hidden[0, spot], hidden[1, spot]), hidden_send.at[0])
    pack(lambda spot: merged(hidden[count - 2, spot], hidden[count - 1, spot]), hidden_send.at[1])
    hidden_copies = halo_copies(hidden_send, hidden_halo, send_hidden, recv_hidden)
    pl.when(has_left)(hidden_copies[0].start)
    fetches[2].wait()
    coarse_matrix(one_weight, one_matrix)
    fetches[3].wait()
    coarse_matrix(two_weight, two_matrix)
    fetches[4].wait()
    fine_matrix(out_weight, last_matrix)
    to_table.wait()
    to_codes.wait()

    turned_down = down_weight[...]
    down_high = high_of(turned_down)
    down_both = jnp.concatenate([down_high, turned_down - down_high], axis=1)
    down_matrix = jnp.concatenate([down_both, down_both], axis=0).astype(BF16)
    for i in range(count):
        end_near(pooled.at[members + member, i], pooled_at(i), send_pooled.at[i], recv_pooled.at[i])
    for i in range(count):
        end_far(pooled.at[members + member, i], pooled_at(i), send_pooled.at[i], recv_pooled.at[i])

    def base_of(near):
        for slot in range(slots):
            for octant in range(8):
                which = table_scalars[near, slot * 8 + octant]
                there_is = which >= 0
                which = jnp.where(there_is, jnp.minimum(which, 3 * members * count - 1), (members + member) * count)
                keep = jnp.where(there_is, 1.0, 0.0).astype(F32)
                place_piece(pooled[which // count, which % count] * keep, octant, placed.at[slot])
        sums = dot(placed[...].reshape(slots * VOX, 128).astype(BF16), down_matrix)
        sums = sums[:, 0:128] + sums[:, 128:256]
        for slot in range(slots):
            base[near * slots + slot] = swap_halves(sums[slot * VOX : slot * VOX + VOX], True)

    def base_step(t, carry):
        base_of(t)
        return carry

    lax.fori_loop(0, 3, base_step, 0)
    coarse_start = (position - 1) * slots
    wide_scratch = (wide_even, wide_odd, wide_edge, rims, shift_down, shift_up)

    if relayed:
        parity = member % 2
        x_at = (group, member + 1 - 2 * parity)
        relay_group = group + jnp.where(member == 1, -1, 0) + jnp.where(member == 2, 1, 0)
        relays_out = (relay_group >= 0) & (relay_group < groups)
        relays_in = jnp.where(is_first, has_low, True) & jnp.where(is_last, has_high, True)
        relay_at = (jnp.clip(relay_group, 0, groups - 1), (member + 2) % members)

        def direct(i, c):
            at, rows = CHUNKS[c]
            return remote(
                first_send.at[i, pl.ds(at, rows)], first_halo.at[parity, i, pl.ds(at, rows)],
                send_first.at[i, c], recv_first.at[i, c], x_at,
            )

        def came(i, c):
            at, rows = CHUNKS[c]
            return remote(
                first_send.at[i, pl.ds(at, rows)], first_halo.at[1 - parity, i, pl.ds(at, rows)],
                send_first.at[i, c], recv_first.at[i, c], x_at,
            )

        def relay(i, c):
            at, rows = CHUNKS[c]
            return remote(
                first_halo.at[1 - parity, i, pl.ds(at, rows)], first_halo.at[parity, i, pl.ds(at, rows)],
                send_relay.at[i, c], recv_relay.at[i, c], relay_at,
            )

        def start_first(i):
            for c in range(len(CHUNKS)):
                direct(i, c).start()

        arrivals = [(i, c) for i in range(slots) for c in range(len(CHUNKS))]

        def pass_on(at):
            i, c = arrivals[at]
            came(i, c).wait_recv()
            pl.when(relays_out)(relay(i, c).start)

        def end_first(passed):
            for at in range(passed, len(arrivals)):
                pass_on(at)
            for i in range(slots):
                for c in range(len(CHUNKS)):
                    pl.when(relays_in)(relay(i, c).wait_recv)

        def end_first_sends():
            for i in range(slots):
                for c in range(len(CHUNKS)):
                    direct(i, c).wait_send()
                    pl.when(relays_out)(relay(i, c).wait_send)
    else:

        def sides(i):
            to_left = remote(first_send.at[i], first_halo.at[1, i], send_first.at[i, 0], recv_first.at[i, 1], left_at)
            to_right = remote(first_send.at[i], first_halo.at[0, i], send_first.at[i, 1], recv_first.at[i, 0], right_at)
            return to_left, to_right

        def start_first(i):
            start_halo(sides(i))

        def pass_on(at):
            pass

        def end_first(passed):
            for i in range(slots):
                end_halo(sides(i))

        def end_first_sends():
            for i in range(slots):
                end_halo_sends(sides(i))

    def second_step(i, carry):
        v = silu(coarse_conv(base, slots + i, coarse_start, coarse_links, i, wide_scratch, one_matrix) + one_bias[...])
        first[slots + i] = v
        pack(lambda spot: first[slots + i, spot], first_send.at[i])
        start_first(i)
        return carry

    lax.fori_loop(0, slots, second_step, 0)
    pl.when(has_right)(hidden_copies[1].start)
    turned_up = up_weight[...].T
    up_high = high_of(turned_up)
    up_both = jnp.concatenate([up_high, turned_up - up_high], axis=1)
    up_matrix = jnp.concatenate([up_both, up_both], axis=0).astype(BF16)
    clear_center(wide_even, wide_odd, True)
    passed = 0
    for i in range(slots):
        fill_center(first.at[slots + i], True, wide_even, wide_odd)
        for half in range(2):
            pass_on(passed)
            passed += 1
            spot = slice(256 * half, 256 * half + 256)
            wide_sums[i, spot] = center(
                True, wide_even, wide_odd, shift_down, shift_up, two_matrix, 4 * half, 4 * half + 4
            )
    end_first(passed)
    for side, at in ((0, 0), (1, 2 * slots)):
        for i in range(slots):
            unpack(first_halo.at[side, i], first.at[at + i])

    def wide_rim_step(i, carry):
        fill_rims(
            loader(first, slots + i), linker(coarse_links, i, coarse_start, slots + i, first.shape[0]), True, i,
            wide_faces_even, wide_faces_odd, wide_face_edge, rims,
        )
        return carry

    lax.fori_loop(0, slots, wide_rim_step, 0)
    add_rims(
        wide_sums, slots, True, wide_faces_even, wide_faces_odd, wide_face_edge, shift_down, shift_up, two_matrix
    )

    def third_step(i, carry):
        v = silu(wide_sums[i] + two_bias[...])
        high = v.astype(BF16)
        low = (v - high.astype(F32)).astype(BF16)
        sums = dot(jnp.concatenate([high, low], axis=1), up_matrix)
        placed[0] = swap_halves(sums + pltpu.roll(sums, 64, 1), False)
        take_pieces(placed.at[0], lifted.at[pl.ds(i * 8, 8)])
        return carry

    lax.fori_loop(0, slots, third_step, 0)
    bricks = members * count
    zeros = jnp.zeros((HALO,) + wanted.shape[1:], F32)
    wanted[0:HALO] = zeros
    wanted[HALO + bricks :] = zeros

    def choose(j, carry):
        code = code_scalars[j // count, j % count, 0] - member * slots * 8
        mine = (code >= 0) & (code < slots * 8)
        keep = jnp.where(mine, 1.0, 0.0).astype(F32)
        wanted[HALO + j] = lifted[jnp.where(mine, code, 0)] * keep
        return carry

    lax.fori_loop(0, bricks, choose, 0)
    parts_of = ((HALO, count, None), (0, HALO, 0), (HALO + count, HALO, members - 1))

    def to_member(k, part):
        other = (member + k) % members
        at, rows, _ = parts_of[part]
        return remote(
            wanted.at[pl.ds(other * count + at, rows)], window.at[member, pl.ds(at, rows)], send_wanted.at[k, part],
            recv_wanted.at[members + member, part], (group, other),
        )

    def from_member(k, part):
        other = (member + k) % members
        at, rows, _ = parts_of[part]
        return remote(
            wanted.at[pl.ds(at, rows)], window.at[other, pl.ds(at, rows)], send_wanted.at[k, part],
            recv_wanted.at[members + other, part], (group, other),
        )

    def when_read(who, part, action):
        none_at = parts_of[part][2]
        if none_at is None:
            action()
        else:
            pl.when(who != none_at)(action)

    to_high = remote(
        wanted.at[pl.ds(bricks, HALO)], low_window.at[member], send_wanted.at[0, 0], recv_wanted.at[member, 0], high_at
    )
    to_low = remote(
        wanted.at[pl.ds(HALO, HALO)], high_window.at[member], send_wanted.at[members, 0],
        recv_wanted.at[2 * members + member, 0], low_at,
    )
    for k in range(1, members):
        to_member(k, 0).start()
    for k in range(1, members):
        for part in (1, 2):
            when_read((member + k) % members, part, to_member(k, part).start)
    pl.when(has_high)(to_high.start)
    pl.when(has_low)(to_low.start)
    window[member] = wanted[pl.ds(member * count, count + 2 * HALO)]
    end_halo(hidden_copies)
    for k in range(1, members):
        from_member(k, 0).wait_recv()

    def total(source, i):
        piece = source[0, i]
        for owner in range(1, members):
            piece = piece + source[owner, i]
        return piece

    def own_blend(i, carry):
        rising = grow(total(window, HALO + i), small)
        parts[HALO + i] = parted(silu(hidden[i] + rising))
        return carry

    lax.fori_loop(0, count, own_blend, 0)
    for k in range(1, members):
        for part in (1, 2):
            when_read(member, part, from_member(k, part).wait_recv)
    for k in range(members):
        spot = wanted.at[pl.ds(0, HALO)]
        from_low = remote(spot, low_window.at[k], send_wanted.at[0, 0], recv_wanted.at[k, 0], low_at)
        from_high = remote(
            spot, high_window.at[k], send_wanted.at[0, 0], recv_wanted.at[2 * members + k, 0], high_at
        )
        pl.when(is_first & has_low)(from_low.wait_recv)
        pl.when(is_last & has_high)(from_high.wait_recv)
    for side, at, edge_window, beyond in (
        (0, 0, low_window, is_first), (1, HALO + count, high_window, is_last),
    ):
        for one in range(HALO):
            piece = jnp.where(beyond, total(edge_window, one), total(window, at + one))
            grown[one] = grow(piece, small)
        pack(lambda spot: merged(grown[0, spot], grown[1, spot]), halves.at[0])
        wire = silu(hidden_halo[side] + halves[0])
        unpack_pair(wire, halves, parts.at[at], parts.at[at + 1])
    out_both = two(out_bias)

    def last_step(i, carry):
        hidden[i] = fine_conv(parts, HALO + i, fine_start, fine_links, i, fine_scratch, last_matrix) + out_both
        return carry

    lax.fori_loop(0, count, last_step, 0)
    for pair in range(pairs):
        flat = merged(hidden[2 * pair], hidden[2 * pair + 1]).T
        out[2 * pair : 2 * pair + 2] = x[2 * pair : 2 * pair + 2] + flat.reshape(2, 64, VOX)

    end_halo_sends(x_copies)
    end_shared_sends(code_copies)
    for i in range(count):
        end_shared_sends(pooled_copies(i))
    end_halo_sends(hidden_copies)
    end_first_sends()
    for k in range(1, members):
        to_member(k, 0).wait_send()
        for part in (1, 2):
            when_read((member + k) % members, part, to_member(k, part).wait_send)
    pl.when(has_high)(to_high.wait_send)
    pl.when(has_low)(to_low.wait_send)


def per_device(
    x, fine_links, parent_codes, coarse_links,
    in_weight, in_bias, down, one_weight, one_bias, two_weight, two_bias, up, out_weight, out_bias,
):
    count, channels = x.shape[0], x.shape[1]
    slots, wide = coarse_links.shape[0], one_bias.shape[0]
    members = lax.axis_size("dev")
    row = lambda bias: bias.reshape(1, -1)
    vmem = pl.BlockSpec(memory_space=pltpu.VMEM)
    smem = pl.BlockSpec(memory_space=pltpu.SMEM)
    anywhere = pl.BlockSpec(memory_space=pl.ANY)
    floats = lambda *shape: pltpu.VMEM(shape, F32)
    halfs = lambda *shape: pltpu.VMEM(shape, BF16)
    ints = lambda *shape: pltpu.VMEM(shape, jnp.int32)
    sems = lambda *shape: pltpu.SemaphoreType.DMA(shape)
    span = count + 2 * HALO
    wire = (32, 128)
    scratch = [
        floats(*x.shape), floats(*in_weight.shape), floats(*one_weight.shape), floats(*two_weight.shape),
        floats(*out_weight.shape), sems(5),
        halfs(1152, 384), halfs(1152, 384), halfs(1152, 768), halfs(1152, 768),
        halfs(1, 10, 80, 128), halfs(1, 10, 64, 128), halfs(3, 10, 16, 128),
        halfs(2, 10, 80, 128), halfs(2, 10, 64, 128), halfs(2, 3, 10, 16, 128),
        floats(2, 10 * LINE, 128), floats(VOX + 16, 128), floats(VOX + 16, 128),
        halfs(1, 4, count, 80, 128), halfs(1, 4, count, 64, 128), halfs(1, 3, count, 10, 16, 128),
        halfs(2, 4, slots, 80, 128), halfs(2, 4, slots, 64, 128), halfs(2, 3, slots, 10, 16, 128),
        floats(slots, VOX, 128),
        floats(span, VOX, 128), floats(count // 2, VOX, 128), floats(count, VOX, 128),
        floats(2, SURFACE, 128), floats(128, 128), floats(HALO, VOX, 128),
        floats(2, SURFACE, 128), floats(2, SURFACE, 128), floats(2, SURFACE, 128), floats(2, SURFACE, 128),
        ints(8, 128), ints(3 * members, 8, 128), ints(members, 8, 128), ints(8, 128),
        pltpu.SMEM((members, 8, 128), jnp.int32), pltpu.SMEM((8, 128), jnp.int32),
        floats(3 * members, count, *wire), floats(slots, VOX, 128), floats(3 * slots, VOX, 128), floats(3 * slots, VOX, 128),
        floats(slots, SURFACE, 128), floats(2, slots, SURFACE, 128), floats(slots * 8, *wire),
        floats(members * count + 2 * HALO, *wire), floats(members, span, *wire), floats(members, HALO, *wire),
        floats(members, HALO, *wire),
        sems(2), sems(2), sems(2), sems(2), sems(2), sems(members + 1), sems(3 * members),
        sems(count, members + 1), sems(count, 3 * members),
        sems(slots, 3), sems(slots, 3), sems(slots, 3), sems(slots, 3), sems(members + 1, 3), sems(3 * members, 3),
    ]
    return pl.pallas_call(
        step_kernel,
        out_shape=jax.ShapeDtypeStruct(x.shape, F32),
        in_specs=[anywhere, smem, smem, smem, anywhere, vmem, vmem, anywhere, vmem, anywhere, vmem, vmem, anywhere, vmem],
        out_specs=vmem,
        scratch_shapes=scratch,
        name="step",
        compiler_params=pltpu.CompilerParams(collective_id=1, has_side_effects=True, vmem_limit_bytes=LIMIT),
    )(
        x, fine_links, parent_codes, coarse_links, in_weight, row(in_bias), down.T, one_weight, row(one_bias),
        two_weight, row(two_bias), up, out_weight, row(out_bias),
    )


def solution(mesh):
    bricks = P(("grp", "dev"), None, None)
    rows = P(("grp", "dev"), None)
    placed = (bricks, rows, P(("grp", "dev")), rows) + (P(),) * 10
    return jax.shard_map(per_device, mesh=mesh, in_specs=placed, out_specs=bricks, check_vma=False)
```

```python
import functools

import jax
import jax.numpy as jnp
from jax import lax
from jax.experimental import pallas as pl
from jax.experimental.pallas import tpu as pltpu
from jax.sharding import PartitionSpec as P

F32 = jnp.float32
BF16 = jnp.bfloat16
MESH = pl.DeviceIdType.MESH
SIDE = 8
VOX = SIDE * SIDE * SIDE
HALO = 2
SURFACE = VOX - 6 * 6 * 6
LINE = 24
LIMIT = 62 * 1024 * 1024
EARLY = 160
CHUNKS = ((0, 96), (96, 96), (192, 104))

offsets = [(x, y, z) for x in (-1, 0, 1) for y in (-1, 0, 1) for z in (-1, 0, 1)]
columns = {o: k for k, o in enumerate(o for o in offsets if o != (0, 0, 0))}


def high_of(v):
    return v.astype(BF16).astype(F32)


def silu(v):
    return v / (1.0 + jnp.exp(-v))


def dot(a, b):
    return lax.dot_general(a, b, (((1,), (0,)), ((), ())), preferred_element_type=F32)


def first_half(v):
    return lax.broadcasted_iota(jnp.int32, v.shape, 1) < v.shape[1] // 2


def merged(a, b):
    return jnp.where(first_half(a), a, b)


def doubled(v):
    turned = pltpu.roll(v, v.shape[1] // 2, 1)
    return merged(v, turned), merged(turned, v)


def parted(v):
    high = high_of(v)
    return merged(high, v - high)


def fill(load, link, put, rims, put_rim):
    found = {o: link(o) for o in columns}

    def get(o, start, size=SIDE, stride=1):
        row, keep = found[o]
        return load(row, start, size, stride) * keep

    for px in range(SIDE + 2):
        dx = -1 if px == 0 else (1 if px == SIDE + 1 else 0)
        x = {-1: SIDE - 1, 0: px - 1, 1: 0}[dx]
        low = get((dx, -1, 0), 64 * x + 56)
        high = get((dx, 1, 0), 64 * x)
        middle = get((dx, 0, 0), 64 * x, 64) if dx else load(None, 64 * x, 64, 1)
        put(px, jnp.concatenate([low, middle, high], axis=0))
    fill_edges(get, rims, put_rim)


def fill_edges(get, rims, put_rim):
    for plane, dz in enumerate((-1, 1)):
        z = SIDE - 1 if dz < 0 else 0
        for px in range(SIDE + 2):
            dx = -1 if px == 0 else (1 if px == SIDE + 1 else 0)
            x = {-1: SIDE - 1, 0: px - 1, 1: 0}[dx]
            rims[plane, px * LINE + 8 : px * LINE + 16] = get((dx, 0, dz), 64 * x + z, SIDE, 8)
            if dx:
                for dy in (-1, 1):
                    y = SIDE - 1 if dy < 0 else 0
                    at = px * LINE + (7 if dy < 0 else 16)
                    rims[plane, at : at + 1] = get((dx, dy, dz), 64 * x + 8 * y + z, 1)
        for dy in (-1, 1):
            y = SIDE - 1 if dy < 0 else 0
            at = LINE + (7 if dy < 0 else 16)
            rims[plane, pl.ds(at, SIDE, stride=LINE)] = get((0, dy, dz), 8 * y + z, SIDE, 64)
    for j in range(3):
        for px in range(SIDE + 2):
            at = px * LINE + 7 + j
            put_rim(j, px, jnp.concatenate([rims[0, at : at + 8], rims[1, at : at + 8]], axis=0))


def stacked(even, odd, edge):
    mains, rims = [], []
    for i in range(3):
        for j in range(3):
            main = odd[i : i + 8] if j == 1 else even[i : i + 8, 8 * j : 8 * j + 64]
            mains.append(main.reshape(VOX, 128))
            rims.append(edge[j, i : i + 8].reshape(128, 128))
    return jnp.concatenate(mains, axis=1), jnp.concatenate(rims, axis=1)


def shifted_sum(blocks, edges, down, up):
    before, here, after = blocks
    down[8 : VOX + 8] = before
    up[8 : VOX + 8] = after
    for x in range(SIDE):
        down[pl.ds(7 + 64 * x, SIDE, stride=8)] = edges[16 * x : 16 * x + 8, 0:128]
        up[pl.ds(16 + 64 * x, SIDE, stride=8)] = edges[16 * x + 8 : 16 * x + 16, 128:256]
    return down[7 : VOX + 7] + here + up[9 : VOX + 9]


def fine_matrix(weight, matrix):
    w = weight[...]
    high = high_of(w)
    both = jnp.concatenate([high, w - high], axis=0).T.astype(BF16)
    for tap in range(27):
        rows, cols = tap // 3 * 128, tap % 3 * 128
        block = both[64 * tap : 64 * tap + 64]
        matrix[rows : rows + 64, cols : cols + 128] = block
        matrix[rows + 64 : rows + 128, cols : cols + 128] = block


def coarse_matrix(weight, matrix):
    for tap in range(27):
        rows, cols = tap // 3 * 128, tap % 3 * 128
        block = weight[:, 128 * tap : 128 * tap + 128].T
        high = high_of(block)
        matrix[rows : rows + 128, cols : cols + 128] = high.astype(BF16)
        matrix[rows : rows + 128, 384 + cols : 384 + cols + 128] = (block - high).astype(BF16)


def linker(links, brick, start, own, rows):
    def link(o):
        there = links[brick, columns[o]]
        there_is = there >= 0
        row = jnp.where(there_is, jnp.clip(there - start, 0, rows - 1), own)
        return row, jnp.where(there_is, 1.0, 0.0).astype(F32)

    return link


def loader(parts, own):
    def load(row, start, size, stride):
        row = own if row is None else row
        if stride == 1:
            return parts[row, start : start + size]
        return parts[row, pl.ds(start, size, stride=stride)]

    return load


def fine_conv(parts, own, start, links, brick, scratch, matrix):
    even, odd, edge, rims, down, up = scratch

    def put(px, v):
        even[px] = v.astype(BF16)
        odd[px] = v[8:72].astype(BF16)

    def put_rim(j, px, v):
        edge[j, px] = v.astype(BF16)

    fill(loader(parts, own), linker(links, brick, start, own, parts.shape[0]), put, rims, put_rim)
    main, rim = stacked(even, odd, edge)
    sums = dot(main, matrix[...])
    ends = lambda at: jnp.concatenate([matrix[:, at : at + 128], matrix[:, at + 256 : at + 384]], axis=1)
    edges = dot(rim, ends(0))
    out = shifted_sum([sums[:, 128 * k : 128 * k + 128] for k in range(3)], edges, down, up)
    return out + pltpu.roll(out, 64, 1)


def coarse_conv(parts, own, start, links, brick, scratch, matrix):
    even, odd, edge, rims, down, up = scratch

    def put(px, v):
        high = v.astype(BF16)
        low = (v - high.astype(F32)).astype(BF16)
        for part, value in enumerate((high, low)):
            even[part, px] = value
        middle = v[8:72]
        high = middle.astype(BF16)
        odd[0, px] = high
        odd[1, px] = (middle - high.astype(F32)).astype(BF16)

    def put_rim(j, px, v):
        high = v.astype(BF16)
        edge[0, j, px] = high
        edge[1, j, px] = (v - high.astype(F32)).astype(BF16)

    fill(loader(parts, own), linker(links, brick, start, own, parts.shape[0]), put, rims, put_rim)
    (main_0, rim_0), (main_1, rim_1) = (stacked(even.at[p], odd.at[p], edge.at[p]) for p in range(2))
    tops = dot(main_0, matrix[...])
    rests = dot(main_1, matrix[:, 0:384])
    ends = lambda at: jnp.concatenate([matrix[:, at : at + 128], matrix[:, at + 256 : at + 384]], axis=1)
    edges = dot(rim_0, ends(0)) + dot(rim_0, ends(384)) + dot(rim_1, ends(0))
    cut = lambda v, at: v[:, 128 * at : 128 * at + 128]
    blocks = [cut(tops, k) + cut(tops, 3 + k) + cut(rests, k) for k in range(3)]
    return shifted_sum(blocks, edges, down, up)


def pieces_of(v, wide):
    high = v.astype(BF16)
    return (high, (v - high.astype(F32)).astype(BF16)) if wide else (high,)


def multiplied(lhs, wide, matrix, blocks):
    rows = [matrix.at[pl.ds(128 * at, 128)] for at in blocks]
    take = lambda cols: jnp.concatenate([r[:, cols] for r in rows], axis=0)
    cut = lambda v, at: v[:, 128 * at : 128 * at + 128]
    if not wide:
        sums = dot(lhs[0], take(slice(0, 384)))
        return [cut(sums, k) for k in range(3)]
    tops, rests = dot(lhs[0], take(slice(0, 768))), dot(lhs[1], take(slice(0, 384)))
    return [cut(tops, k) + cut(tops, 3 + k) + cut(rests, k) for k in range(3)]


def line_sum(blocks, down, up):
    rows = blocks[0].shape[0]
    down[8 : rows + 8] = blocks[0]
    up[8 : rows + 8] = blocks[2]
    zeros = jnp.zeros((SIDE, 128), F32)
    for at in range(0, rows, 64):
        down[pl.ds(7 + at, SIDE, stride=8)] = zeros
        up[pl.ds(16 + at, SIDE, stride=8)] = zeros
    return down[7 : rows + 7] + blocks[1] + up[9 : rows + 9]


def clear_center(even, odd, wide):
    for part in range(2 if wide else 1):
        for px in (0, SIDE + 1):
            even[part, px] = jnp.zeros(even.shape[2:], BF16)
            odd[part, px] = jnp.zeros(odd.shape[2:], BF16)


def fill_center(brick, wide, even, odd):
    zeros = jnp.zeros((SIDE, 128), F32)
    for x in range(SIDE):
        middle = brick[64 * x : 64 * x + 64]
        for part, v in enumerate(pieces_of(jnp.concatenate([zeros, middle, zeros], axis=0), wide)):
            even[part, x + 1] = v
        for part, v in enumerate(pieces_of(middle, wide)):
            odd[part, x + 1] = v


def center(wide, even, odd, down, up, matrix, first, last):
    def taps(part):
        windows = []
        for i in range(3):
            for j in range(3):
                xs = slice(first + i, last + i)
                v = odd[part, xs] if j == 1 else even[part, xs, 8 * j : 8 * j + 64]
                windows.append(v.reshape((last - first) * 64, 128))
        return jnp.concatenate(windows, axis=1)

    lhs = [taps(part) for part in range(2 if wide else 1)]
    return line_sum(multiplied(lhs, wide, matrix, range(9)), down, up)


def fill_rims(load, link, wide, at, faces_even, faces_odd, edge, rims):
    found = {o: link(o) for o in columns}
    zeros = jnp.zeros((SIDE, 128), F32)

    def get(o, start, size=SIDE, stride=1):
        row, keep = found[o]
        return load(row, start, size, stride) * keep

    def put_face(face, lines):
        v = jnp.concatenate(lines, axis=0)
        for part, value in enumerate(pieces_of(v, wide)):
            faces_even[part, face, at] = value
        for part, value in enumerate(pieces_of(v[8:72], wide)):
            faces_odd[part, face, at] = value

    def put_rim(j, px, v):
        for part, value in enumerate(pieces_of(v, wide)):
            edge[part, j, at, px] = value

    for face, d in enumerate((-1, 1)):
        spot = SIDE - 1 if d < 0 else 0
        put_face(face, [get((d, -1, 0), 64 * spot + 56), get((d, 0, 0), 64 * spot, 64), get((d, 1, 0), 64 * spot)])
        lines = [get((0, d, 0), 64 * x + 8 * spot) for x in range(SIDE)]
        put_face(2 + face, [zeros] + lines + [zeros])
    fill_edges(get, rims, put_rim)


def add_rims(sums, n, wide, faces_even, faces_odd, edge, down, up, matrix):
    parts = range(2 if wide else 1)
    for face in range(4):
        side = 2 * (face % 2)
        blocks = [3 * side + t for t in range(3)] if face < 2 else [3 * t + side for t in range(3)]
        lhs = []
        for part in parts:
            windows = []
            for t in range(3):
                v = faces_odd[part, face] if t == 1 else faces_even[part, face, :, 8 * t : 8 * t + 64]
                windows.append(v.reshape(n * 64, 128))
            lhs.append(jnp.concatenate(windows, axis=1))
        total = line_sum(multiplied(lhs, wide, matrix, blocks), down, up)
        for b in range(n):
            if face < 2:
                sums[b, 224 * side : 224 * side + 64] += total[64 * b : 64 * b + 64]
            else:
                for x in range(SIDE):
                    at = 64 * x + 28 * side
                    sums[b, at : at + 8] += total[64 * b + 8 * x : 64 * b + 8 * x + 8]
    lhs = []
    for part in parts:
        windows = [edge[part, j, :, i : i + 8].reshape(n * 128, 128) for i in range(3) for j in range(3)]
        lhs.append(jnp.concatenate(windows, axis=1))
    ends = lambda at: jnp.concatenate([matrix[:, at : at + 128], matrix[:, at + 256 : at + 384]], axis=1)
    total = dot(lhs[0], ends(0))
    if wide:
        total = total + dot(lhs[0], ends(384)) + dot(lhs[1], ends(0))
    for b in range(n):
        for x in range(SIDE):
            at = 128 * b + 16 * x
            sums[b, pl.ds(64 * x, SIDE, stride=8)] += total[at : at + 8, 0:128]
            sums[b, pl.ds(64 * x + 7, SIDE, stride=8)] += total[at + 8 : at + 16, 128:256]


def surface_spots():
    spots = [(0, 0, 64, 1), (64, 448, 64, 1)]
    for x in range(1, 7):
        at = 128 + (x - 1) * 16
        spots += [(at, 64 * x, 8, 1), (at + 8, 64 * x + 56, 8, 1)]
    for x in range(1, 7):
        at = 224 + (x - 1) * 12
        spots += [(at, 64 * x + 8, 6, 8), (at + 6, 64 * x + 15, 6, 8)]
    return spots


def pack(get, wire):
    for at, start, size, stride in surface_spots():
        wire[at : at + size] = get(pl.ds(start, size, stride=stride) if stride > 1 else pl.ds(start, size))


def unpack(wire, brick):
    for at, start, size, stride in surface_spots():
        spot = pl.ds(start, size, stride=stride) if stride > 1 else pl.ds(start, size)
        brick[spot] = wire[at : at + size]


def unpack_pair(wire, scratch, first, second):
    a, b = doubled(wire)
    scratch[0] = parted(a)
    scratch[1] = parted(b)
    unpack(scratch.at[0], first)
    unpack(scratch.at[1], second)


def pool(v, scratch, wire):
    lines = v.reshape(4, 2, 4, 2, SIDE, 128)
    sums = (lines[:, 0, :, 0] + lines[:, 0, :, 1]) + (lines[:, 1, :, 0] + lines[:, 1, :, 1])
    scratch[...] = sums.reshape(128, 128)
    for z in range(4):
        halves = [
            scratch[pl.ds(64 * half + 2 * z, 8, stride=8)] + scratch[pl.ds(64 * half + 2 * z + 1, 8, stride=8)]
            for half in range(2)
        ]
        wire[8 * z : 8 * z + 8] = merged(*halves) * 0.125


def split_spot(octant, half, z):
    a, b, c = octant // 4, octant // 2 % 2, octant % 2
    return pl.ds(256 * b + 32 * (4 * a + 2 * half) + 4 * c + z, 8, stride=8)


def place_piece(wire, octant, brick):
    for half, v in enumerate(doubled(wire)):
        v = parted(v)
        for z in range(4):
            brick[split_spot(octant, half, z)] = v[8 * z : 8 * z + 8]


def take_pieces(brick, pieces):
    for octant in range(8):
        for z in range(4):
            halves = [brick[split_spot(octant, half, z)] for half in range(2)]
            pieces[octant, 8 * z : 8 * z + 8] = merged(*halves)


def swap_halves(v, split):
    first, second = (2, SIDE) if split else (SIDE, 2)
    return v.reshape(first, second, 32, 128).swapaxes(0, 1).reshape(VOX, 128)


def grow(piece, scratch):
    for half, v in enumerate(doubled(piece)):
        for z in range(4):
            rows = v[8 * z : 8 * z + 8]
            scratch[pl.ds(64 * half + 2 * z, 8, stride=8)] = rows
            scratch[pl.ds(64 * half + 2 * z + 1, 8, stride=8)] = rows
    lines = scratch[...].reshape(4, 1, 4, 1, SIDE, 128)
    return jnp.broadcast_to(lines, (4, 2, 4, 2, SIDE, 128)).reshape(VOX, 128)


def step_kernel(
    x_any, fine_links, own_codes, coarse_links, in_any, in_bias, down_weight, one_any, one_bias, two_any, two_bias,
    up_weight, out_any, out_bias,
    out,
    x, in_weight, one_weight, two_weight, out_weight, loads,
    matrix, last_matrix, one_matrix, two_matrix,
    even, odd, edge, wide_even, wide_odd, wide_edge, rims, shift_down, shift_up,
    faces_even, faces_odd, face_edge, wide_faces_even, wide_faces_odd, wide_face_edge, wide_sums,
    parts, turned, hidden, halves, small, grown,
    x_send, x_halo, hidden_send, hidden_halo,
    code_block, codes, code_table, table, code_scalars, table_scalars,
    pooled, placed, base, first,
    first_send, first_halo, lifted, wanted, window, low_window, high_window,
    local_sems, send_x, recv_x, send_hidden, recv_hidden, send_codes, recv_codes, send_pooled, recv_pooled,
    send_first, recv_first, send_relay, recv_relay, send_wanted, recv_wanted,
):
    group, member = lax.axis_index("grp"), lax.axis_index("dev")
    groups, members = lax.axis_size("grp"), lax.axis_size("dev")
    position = group * members + member
    whole = groups * members
    count, slots = fine_links.shape[0], coarse_links.shape[0]
    pairs = count // 2
    relayed = members == 4
    has_left, has_right = position > 0, position < whole - 1
    has_low, has_high = group > 0, group < groups - 1
    is_first, is_last = member == 0, member == members - 1
    left_at = (jnp.maximum(position - 1, 0) // members, (position + members - 1) % members)
    right_at = (jnp.minimum(position + 1, whole - 1) // members, (position + 1) % members)
    low_at = (jnp.maximum(group - 1, 0), members - 1)
    high_at = (jnp.minimum(group + 1, groups - 1), 0)
    always = position >= 0

    def fetch(k, source, target):
        return pltpu.make_async_copy(source, target, loads.at[k])

    fetches = [
        fetch(0, x_any, x), fetch(1, in_any, in_weight), fetch(2, one_any, one_weight),
        fetch(3, two_any, two_weight), fetch(4, out_any, out_weight),
    ]
    for copy in fetches:
        copy.start()

    barrier = pltpu.get_barrier_semaphore()

    def greet(where):
        pl.semaphore_signal(barrier, inc=1, device_id=where, device_id_type=MESH)

    pl.when(has_left)(lambda: greet(left_at))
    pl.when(has_right)(lambda: greet(right_at))
    for k in range(1, members):
        greet((group, (member + k) % members))
    for k in range(members):
        pl.when(is_first & has_low)(lambda k=k: greet((low_at[0], k)))
        pl.when(is_last & has_high)(lambda k=k: greet((high_at[0], k)))

    def remote(src, dst, send, recv, where):
        return pltpu.make_async_remote_copy(
            src_ref=src, dst_ref=dst, send_sem=send, recv_sem=recv, device_id=where, device_id_type=MESH
        )

    row = lax.broadcasted_iota(jnp.int32, (SIDE, 128), 0)
    block = jnp.full((SIDE, 128), -1, jnp.int32)
    for i in range(count):
        block = jnp.where(row == i, own_codes[i], block)
    code_block[...] = block
    codes[members + member] = block
    fetches[0].wait()
    for pair in range(pairs):
        turned[pair] = x[2 * pair : 2 * pair + 2].reshape(128, VOX).T
    pack(lambda spot: turned[0, spot], x_send.at[0])
    pack(lambda spot: turned[pairs - 1, spot], x_send.at[1])
    pl.semaphore_wait(
        barrier,
        jnp.where(has_left, 1, 0) + jnp.where(has_right, 1, 0) + (members - 1)
        + jnp.where(has_low, 1, 0) + jnp.where(has_high, 1, 0),
    )

    def halo_copies(source, halo, send, recv, at=0, rows=SURFACE):
        spot = pl.ds(at, rows)
        to_left = remote(source.at[0, spot], halo.at[1, spot], send.at[0], recv.at[1], left_at)
        to_right = remote(source.at[1, spot], halo.at[0, spot], send.at[1], recv.at[0], right_at)
        return to_left, to_right

    def start_halo(copies):
        pl.when(has_left)(copies[0].start)
        pl.when(has_right)(copies[1].start)

    def end_halo(copies):
        pl.when(has_left)(copies[1].wait_recv)
        pl.when(has_right)(copies[0].wait_recv)

    def end_halo_sends(copies):
        pl.when(has_left)(copies[0].wait_send)
        pl.when(has_right)(copies[1].wait_send)

    def shared_copies(source, at, send, recv):
        near = [
            remote(source, at(members + member), send.at[k], recv.at[members + member], (group, (member + k) % members))
            for k in range(1, members)
        ]
        to_high = remote(source, at(member), send.at[0], recv.at[member], high_at)
        to_low = remote(source, at(2 * members + member), send.at[members], recv.at[2 * members + member], low_at)
        return near, to_high, to_low

    def start_shared(copies):
        near, to_high, to_low = copies
        for copy in near:
            copy.start()
        pl.when(has_high)(to_high.start)
        pl.when(has_low)(to_low.start)

    def end_near(source, at, send, recv):
        for k in range(1, members):
            other = (member + k) % members
            remote(source, at(members + other), send.at[k], recv.at[members + other], (group, other)).wait_recv()

    def end_far(source, at, send, recv):
        for k in range(members):
            from_low = remote(source, at(k), send.at[0], recv.at[k], low_at)
            from_high = remote(source, at(2 * members + k), send.at[0], recv.at[2 * members + k], high_at)
            pl.when(is_first & has_low)(from_low.wait_recv)
            pl.when(is_last & has_high)(from_high.wait_recv)

    def end_shared_sends(copies):
        near, to_high, to_low = copies
        for copy in near:
            copy.wait_send()
        pl.when(has_high)(to_high.wait_send)
        pl.when(has_low)(to_low.wait_send)

    x_copies = halo_copies(x_send, x_halo, send_x, recv_x)
    start_halo(x_copies)
    code_at = lambda k: codes.at[k]
    code_copies = shared_copies(code_block, code_at, send_codes, recv_codes)
    start_shared(code_copies)

    fetches[1].wait()
    fine_matrix(in_weight, matrix)
    for pair in range(pairs):
        for one, v in enumerate(doubled(turned[pair])):
            parts[HALO + 2 * pair + one] = parted(v)

    clear_center(even, odd, False)

    def own_step(i, carry):
        fill_center(parts.at[HALO + i], False, even, odd)
        hidden[i] = center(False, even, odd, shift_down, shift_up, matrix, 0, SIDE)
        return carry

    lax.fori_loop(0, count, own_step, 0)
    end_near(code_block, code_at, send_codes, recv_codes)
    end_far(code_block, code_at, send_codes, recv_codes)
    lane = lax.broadcasted_iota(jnp.int32, (SIDE, 128), 1)
    table_rows = jnp.full((SIDE, 128), -1, jnp.int32)
    for near in range(3):
        there = position + near - 1
        valid = (there >= 0) & (there < whole)
        there = jnp.where(valid, there, position)
        there_group = there // members
        there_member = there - there_group * members
        band = there_group - group + 1
        spot = jnp.where(valid, lane, -1000) + there_member * slots * 8
        best = jnp.full((SIDE, 128), -1, jnp.int32)
        for k in range(members):
            match = (codes[band * members + k] == spot) & (row < count) & (lane < slots * 8)
            best = jnp.maximum(best, jnp.where(match, (band * members + k) * count + row, -1))
        top = jnp.max(best, axis=0, keepdims=True)
        table_rows = jnp.where(row == near, top, table_rows)
    code_table[...] = codes[pl.ds(members, members)]
    table[...] = table_rows
    to_table = pltpu.make_async_copy(table, table_scalars, local_sems.at[0])
    to_codes = pltpu.make_async_copy(code_table, code_scalars, local_sems.at[1])
    to_table.start()
    to_codes.start()

    fine_start = position * count - HALO
    end_halo(x_copies)
    for side, at in ((0, 0), (1, HALO + count)):
        unpack_pair(x_halo[side], halves, parts.at[at], parts.at[at + 1])
    fine_scratch = (even.at[0], odd.at[0], edge, rims, shift_down, shift_up)
    two = lambda bias: jnp.concatenate([bias[...], bias[...]], axis=1)
    in_both = two(in_bias)

    def pooled_at(i):
        return lambda k: pooled.at[k, i]

    def pooled_copies(i):
        return shared_copies(pooled.at[members + member, i], pooled_at(i), send_pooled.at[i], recv_pooled.at[i])

    def first_step(pair, carry):
        at = 2 * pair
        for one in range(2):
            own = HALO + at + one
            fill_rims(
                loader(parts, own), linker(fine_links, at + one, fine_start, own, parts.shape[0]), False, one,
                faces_even, faces_odd, face_edge, rims,
            )
        sums = hidden.at[pl.ds(at, 2)]
        add_rims(sums, 2, False, faces_even, faces_odd, face_edge, shift_down, shift_up, matrix)
        for one in range(2):
            v = sums[one]
            v = silu(v + pltpu.roll(v, 64, 1) + in_both)
            pool(v, small, pooled.at[members + member, at + one])
            sums[one] = v
            start_shared(pooled_copies(at + one))
        return carry

    lax.fori_loop(0, pairs, first_step, 0)
    pack(lambda spot: merged(hidden[0, spot], hidden[1, spot]), hidden_send.at[0])
    pack(lambda spot: merged(hidden[count - 2, spot], hidden[count - 1, spot]), hidden_send.at[1])
    hidden_copies = [
        halo_copies(hidden_send, hidden_halo, send_hidden.at[part], recv_hidden.at[part], at, rows)
        for part, (at, rows) in enumerate(((0, EARLY), (EARLY, SURFACE - EARLY)))
    ]
    start_halo(hidden_copies[0])
    fetches[2].wait()
    coarse_matrix(one_weight, one_matrix)
    fetches[3].wait()
    coarse_matrix(two_weight, two_matrix)
    fetches[4].wait()
    fine_matrix(out_weight, last_matrix)
    to_table.wait()
    to_codes.wait()

    turned_down = down_weight[...]
    down_high = high_of(turned_down)
    down_both = jnp.concatenate([down_high, turned_down - down_high], axis=1)
    down_matrix = jnp.concatenate([down_both, down_both], axis=0).astype(BF16)
    for i in range(count):
        end_near(pooled.at[members + member, i], pooled_at(i), send_pooled.at[i], recv_pooled.at[i])
    for i in range(count):
        end_far(pooled.at[members + member, i], pooled_at(i), send_pooled.at[i], recv_pooled.at[i])

    def base_of(near):
        for slot in range(slots):
            for octant in range(8):
                which = table_scalars[near, slot * 8 + octant]
                there_is = which >= 0
                which = jnp.where(there_is, jnp.minimum(which, 3 * members * count - 1), (members + member) * count)
                keep = jnp.where(there_is, 1.0, 0.0).astype(F32)
                place_piece(pooled[which // count, which % count] * keep, octant, placed.at[slot])
        sums = dot(placed[...].reshape(slots * VOX, 128).astype(BF16), down_matrix)
        sums = sums[:, 0:128] + sums[:, 128:256]
        for slot in range(slots):
            base[near * slots + slot] = swap_halves(sums[slot * VOX : slot * VOX + VOX], True)

    def base_step(t, carry):
        base_of(t)
        return carry

    lax.fori_loop(0, 3, base_step, 0)
    coarse_start = (position - 1) * slots
    wide_scratch = (wide_even, wide_odd, wide_edge, rims, shift_down, shift_up)

    if relayed:
        parity = member % 2
        x_at = (group, member + 1 - 2 * parity)
        relay_group = group + jnp.where(member == 1, -1, 0) + jnp.where(member == 2, 1, 0)
        relays_out = (relay_group >= 0) & (relay_group < groups)
        relays_in = jnp.where(is_first, has_low, True) & jnp.where(is_last, has_high, True)
        relay_at = (jnp.clip(relay_group, 0, groups - 1), (member + 2) % members)

        def direct(i, c):
            at, rows = CHUNKS[c]
            return remote(
                first_send.at[i, pl.ds(at, rows)], first_halo.at[parity, i, pl.ds(at, rows)],
                send_first.at[i, c], recv_first.at[i, c], x_at,
            )

        def came(i, c):
            at, rows = CHUNKS[c]
            return remote(
                first_send.at[i, pl.ds(at, rows)], first_halo.at[1 - parity, i, pl.ds(at, rows)],
                send_first.at[i, c], recv_first.at[i, c], x_at,
            )

        def relay(i, c):
            at, rows = CHUNKS[c]
            return remote(
                first_halo.at[1 - parity, i, pl.ds(at, rows)], first_halo.at[parity, i, pl.ds(at, rows)],
                send_relay.at[i, c], recv_relay.at[i, c], relay_at,
            )

        def start_first(i):
            for c in range(len(CHUNKS)):
                direct(i, c).start()

        arrivals = [(i, c) for i in range(slots) for c in range(len(CHUNKS))]

        def pass_on(at):
            i, c = arrivals[at]
            came(i, c).wait_recv()
            pl.when(relays_out)(relay(i, c).start)

        def end_first(passed):
            for at in range(passed, len(arrivals)):
                pass_on(at)
            for i in range(slots):
                for c in range(len(CHUNKS)):
                    pl.when(relays_in)(relay(i, c).wait_recv)

        def end_first_sends():
            for i in range(slots):
                for c in range(len(CHUNKS)):
                    direct(i, c).wait_send()
                    pl.when(relays_out)(relay(i, c).wait_send)
    else:

        def sides(i):
            to_left = remote(first_send.at[i], first_halo.at[1, i], send_first.at[i, 0], recv_first.at[i, 1], left_at)
            to_right = remote(first_send.at[i], first_halo.at[0, i], send_first.at[i, 1], recv_first.at[i, 0], right_at)
            return to_left, to_right

        def start_first(i):
            start_halo(sides(i))

        def pass_on(at):
            pass

        def end_first(passed):
            for i in range(slots):
                end_halo(sides(i))

        def end_first_sends():
            for i in range(slots):
                end_halo_sends(sides(i))

    def second_step(i, carry):
        v = silu(coarse_conv(base, slots + i, coarse_start, coarse_links, i, wide_scratch, one_matrix) + one_bias[...])
        first[slots + i] = v
        pack(lambda spot: first[slots + i, spot], first_send.at[i])
        start_first(i)
        return carry

    lax.fori_loop(0, slots, second_step, 0)
    turned_up = up_weight[...].T
    up_high = high_of(turned_up)
    up_both = jnp.concatenate([up_high, turned_up - up_high], axis=1)
    up_matrix = jnp.concatenate([up_both, up_both], axis=0).astype(BF16)
    clear_center(wide_even, wide_odd, True)
    passed = 0
    for i in range(slots):
        fill_center(first.at[slots + i], True, wide_even, wide_odd)
        for half in range(2):
            pass_on(passed)
            passed += 1
            spot = slice(256 * half, 256 * half + 256)
            wide_sums[i, spot] = center(
                True, wide_even, wide_odd, shift_down, shift_up, two_matrix, 4 * half, 4 * half + 4
            )
    end_first(passed)
    start_halo(hidden_copies[1])
    for side, at in ((0, 0), (1, 2 * slots)):
        for i in range(slots):
            unpack(first_halo.at[side, i], first.at[at + i])

    def wide_rim_step(i, carry):
        fill_rims(
            loader(first, slots + i), linker(coarse_links, i, coarse_start, slots + i, first.shape[0]), True, i,
            wide_faces_even, wide_faces_odd, wide_face_edge, rims,
        )
        return carry

    lax.fori_loop(0, slots, wide_rim_step, 0)
    add_rims(
        wide_sums, slots, True, wide_faces_even, wide_faces_odd, wide_face_edge, shift_down, shift_up, two_matrix
    )

    def third_step(i, carry):
        v = silu(wide_sums[i] + two_bias[...])
        high = v.astype(BF16)
        low = (v - high.astype(F32)).astype(BF16)
        sums = dot(jnp.concatenate([high, low], axis=1), up_matrix)
        placed[0] = swap_halves(sums + pltpu.roll(sums, 64, 1), False)
        take_pieces(placed.at[0], lifted.at[pl.ds(i * 8, 8)])
        return carry

    lax.fori_loop(0, slots, third_step, 0)
    bricks = members * count
    zeros = jnp.zeros((HALO,) + wanted.shape[1:], F32)
    wanted[0:HALO] = zeros
    wanted[HALO + bricks :] = zeros

    def choose(j, carry):
        code = code_scalars[j // count, j % count, 0] - member * slots * 8
        mine = (code >= 0) & (code < slots * 8)
        keep = jnp.where(mine, 1.0, 0.0).astype(F32)
        wanted[HALO + j] = lifted[jnp.where(mine, code, 0)] * keep
        return carry

    lax.fori_loop(0, bricks, choose, 0)
    parts_of = ((HALO, count, None), (0, HALO, 0), (HALO + count, HALO, members - 1))

    def to_member(k, part):
        other = (member + k) % members
        at, rows, _ = parts_of[part]
        return remote(
            wanted.at[pl.ds(other * count + at, rows)], window.at[member, pl.ds(at, rows)], send_wanted.at[k, part],
            recv_wanted.at[members + member, part], (group, other),
        )

    def from_member(k, part):
        other = (member + k) % members
        at, rows, _ = parts_of[part]
        return remote(
            wanted.at[pl.ds(at, rows)], window.at[other, pl.ds(at, rows)], send_wanted.at[k, part],
            recv_wanted.at[members + other, part], (group, other),
        )

    def when_read(who, part, action):
        none_at = parts_of[part][2]
        if none_at is None:
            action()
        else:
            pl.when(who != none_at)(action)

    to_high = remote(
        wanted.at[pl.ds(bricks, HALO)], low_window.at[member], send_wanted.at[0, 0], recv_wanted.at[member, 0], high_at
    )
    to_low = remote(
        wanted.at[pl.ds(HALO, HALO)], high_window.at[member], send_wanted.at[members, 0],
        recv_wanted.at[2 * members + member, 0], low_at,
    )
    for k in range(1, members):
        to_member(k, 0).start()
    for k in range(1, members):
        for part in (1, 2):
            when_read((member + k) % members, part, to_member(k, part).start)
    pl.when(has_high)(to_high.start)
    pl.when(has_low)(to_low.start)
    window[member] = wanted[pl.ds(member * count, count + 2 * HALO)]
    for copies in hidden_copies:
        end_halo(copies)
    for k in range(1, members):
        from_member(k, 0).wait_recv()

    def total(source, i):
        piece = source[0, i]
        for owner in range(1, members):
            piece = piece + source[owner, i]
        return piece

    def own_blend(i, carry):
        rising = grow(total(window, HALO + i), small)
        parts[HALO + i] = parted(silu(hidden[i] + rising))
        return carry

    lax.fori_loop(0, count, own_blend, 0)
    for k in range(1, members):
        for part in (1, 2):
            when_read(member, part, from_member(k, part).wait_recv)
    for k in range(members):
        spot = wanted.at[pl.ds(0, HALO)]
        from_low = remote(spot, low_window.at[k], send_wanted.at[0, 0], recv_wanted.at[k, 0], low_at)
        from_high = remote(
            spot, high_window.at[k], send_wanted.at[0, 0], recv_wanted.at[2 * members + k, 0], high_at
        )
        pl.when(is_first & has_low)(from_low.wait_recv)
        pl.when(is_last & has_high)(from_high.wait_recv)
    for side, at, edge_window, beyond in (
        (0, 0, low_window, is_first), (1, HALO + count, high_window, is_last),
    ):
        for one in range(HALO):
            piece = jnp.where(beyond, total(edge_window, one), total(window, at + one))
            grown[one] = grow(piece, small)
        pack(lambda spot: merged(grown[0, spot], grown[1, spot]), halves.at[0])
        wire = silu(hidden_halo[side] + halves[0])
        unpack_pair(wire, halves, parts.at[at], parts.at[at + 1])
    out_both = two(out_bias)

    def last_step(i, carry):
        hidden[i] = fine_conv(parts, HALO + i, fine_start, fine_links, i, fine_scratch, last_matrix) + out_both
        return carry

    lax.fori_loop(0, count, last_step, 0)
    for pair in range(pairs):
        flat = merged(hidden[2 * pair], hidden[2 * pair + 1]).T
        out[2 * pair : 2 * pair + 2] = x[2 * pair : 2 * pair + 2] + flat.reshape(2, 64, VOX)

    end_halo_sends(x_copies)
    end_shared_sends(code_copies)
    for i in range(count):
        end_shared_sends(pooled_copies(i))
    for copies in hidden_copies:
        end_halo_sends(copies)
    end_first_sends()
    for k in range(1, members):
        to_member(k, 0).wait_send()
        for part in (1, 2):
            when_read((member + k) % members, part, to_member(k, part).wait_send)
    pl.when(has_high)(to_high.wait_send)
    pl.when(has_low)(to_low.wait_send)


def per_device(
    x, fine_links, parent_codes, coarse_links,
    in_weight, in_bias, down, one_weight, one_bias, two_weight, two_bias, up, out_weight, out_bias,
):
    count, channels = x.shape[0], x.shape[1]
    slots, wide = coarse_links.shape[0], one_bias.shape[0]
    members = lax.axis_size("dev")
    row = lambda bias: bias.reshape(1, -1)
    vmem = pl.BlockSpec(memory_space=pltpu.VMEM)
    smem = pl.BlockSpec(memory_space=pltpu.SMEM)
    anywhere = pl.BlockSpec(memory_space=pl.ANY)
    floats = lambda *shape: pltpu.VMEM(shape, F32)
    halfs = lambda *shape: pltpu.VMEM(shape, BF16)
    ints = lambda *shape: pltpu.VMEM(shape, jnp.int32)
    sems = lambda *shape: pltpu.SemaphoreType.DMA(shape)
    span = count + 2 * HALO
    wire = (32, 128)
    scratch = [
        floats(*x.shape), floats(*in_weight.shape), floats(*one_weight.shape), floats(*two_weight.shape),
        floats(*out_weight.shape), sems(5),
        halfs(1152, 384), halfs(1152, 384), halfs(1152, 768), halfs(1152, 768),
        halfs(1, 10, 80, 128), halfs(1, 10, 64, 128), halfs(3, 10, 16, 128),
        halfs(2, 10, 80, 128), halfs(2, 10, 64, 128), halfs(2, 3, 10, 16, 128),
        floats(2, 10 * LINE, 128), floats(VOX + 16, 128), floats(VOX + 16, 128),
        halfs(1, 4, 2, 80, 128), halfs(1, 4, 2, 64, 128), halfs(1, 3, 2, 10, 16, 128),
        halfs(2, 4, slots, 80, 128), halfs(2, 4, slots, 64, 128), halfs(2, 3, slots, 10, 16, 128),
        floats(slots, VOX, 128),
        floats(span, VOX, 128), floats(count // 2, VOX, 128), floats(count, VOX, 128),
        floats(2, SURFACE, 128), floats(128, 128), floats(HALO, VOX, 128),
        floats(2, SURFACE, 128), floats(2, SURFACE, 128), floats(2, SURFACE, 128), floats(2, SURFACE, 128),
        ints(8, 128), ints(3 * members, 8, 128), ints(members, 8, 128), ints(8, 128),
        pltpu.SMEM((members, 8, 128), jnp.int32), pltpu.SMEM((8, 128), jnp.int32),
        floats(3 * members, count, *wire), floats(slots, VOX, 128), floats(3 * slots, VOX, 128), floats(3 * slots, VOX, 128),
        floats(slots, SURFACE, 128), floats(2, slots, SURFACE, 128), floats(slots * 8, *wire),
        floats(members * count + 2 * HALO, *wire), floats(members, span, *wire), floats(members, HALO, *wire),
        floats(members, HALO, *wire),
        sems(2), sems(2), sems(2), sems(2, 2), sems(2, 2), sems(members + 1), sems(3 * members),
        sems(count, members + 1), sems(count, 3 * members),
        sems(slots, 3), sems(slots, 3), sems(slots, 3), sems(slots, 3), sems(members + 1, 3), sems(3 * members, 3),
    ]
    return pl.pallas_call(
        step_kernel,
        out_shape=jax.ShapeDtypeStruct(x.shape, F32),
        in_specs=[anywhere, smem, smem, smem, anywhere, vmem, vmem, anywhere, vmem, anywhere, vmem, vmem, anywhere, vmem],
        out_specs=vmem,
        scratch_shapes=scratch,
        name="step",
        compiler_params=pltpu.CompilerParams(collective_id=1, has_side_effects=True, vmem_limit_bytes=LIMIT),
    )(
        x, fine_links, parent_codes, coarse_links, in_weight, row(in_bias), down.T, one_weight, row(one_bias),
        two_weight, row(two_bias), up, out_weight, row(out_bias),
    )


def solution(mesh):
    bricks = P(("grp", "dev"), None, None)
    rows = P(("grp", "dev"), None)
    placed = (bricks, rows, P(("grp", "dev")), rows) + (P(),) * 10
    return jax.shard_map(per_device, mesh=mesh, in_specs=placed, out_specs=bricks, check_vma=False)
```

```python
import functools

import jax
import jax.numpy as jnp
from jax import lax
from jax.experimental import pallas as pl
from jax.experimental.pallas import tpu as pltpu
from jax.sharding import PartitionSpec as P

F32 = jnp.float32
BF16 = jnp.bfloat16
MESH = pl.DeviceIdType.MESH
SIDE = 8
VOX = SIDE * SIDE * SIDE
HALO = 2
SURFACE = VOX - 6 * 6 * 6
LINE = 24
LIMIT = 62 * 1024 * 1024
EARLY = 160
CHUNKS = ((0, 120), (120, 96), (216, 80))
STRAIGHT = 1

offsets = [(x, y, z) for x in (-1, 0, 1) for y in (-1, 0, 1) for z in (-1, 0, 1)]
columns = {o: k for k, o in enumerate(o for o in offsets if o != (0, 0, 0))}


def high_of(v):
    return v.astype(BF16).astype(F32)


def silu(v):
    return v / (1.0 + jnp.exp(-v))


def dot(a, b):
    return lax.dot_general(a, b, (((1,), (0,)), ((), ())), preferred_element_type=F32)


def first_half(v):
    return lax.broadcasted_iota(jnp.int32, v.shape, 1) < v.shape[1] // 2


def merged(a, b):
    return jnp.where(first_half(a), a, b)


def doubled(v):
    turned = pltpu.roll(v, v.shape[1] // 2, 1)
    return merged(v, turned), merged(turned, v)


def parted(v):
    high = high_of(v)
    return merged(high, v - high)


def fill(load, link, put, rims, put_rim):
    found = {o: link(o) for o in columns}

    def get(o, start, size=SIDE, stride=1):
        row, keep = found[o]
        return load(row, start, size, stride) * keep

    for px in range(SIDE + 2):
        dx = -1 if px == 0 else (1 if px == SIDE + 1 else 0)
        x = {-1: SIDE - 1, 0: px - 1, 1: 0}[dx]
        low = get((dx, -1, 0), 64 * x + 56)
        high = get((dx, 1, 0), 64 * x)
        middle = get((dx, 0, 0), 64 * x, 64) if dx else load(None, 64 * x, 64, 1)
        put(px, jnp.concatenate([low, middle, high], axis=0))
    fill_edges(get, rims, put_rim)


def fill_edges(get, rims, put_rim):
    for plane, dz in enumerate((-1, 1)):
        z = SIDE - 1 if dz < 0 else 0
        for px in range(SIDE + 2):
            dx = -1 if px == 0 else (1 if px == SIDE + 1 else 0)
            x = {-1: SIDE - 1, 0: px - 1, 1: 0}[dx]
            rims[plane, px * LINE + 8 : px * LINE + 16] = get((dx, 0, dz), 64 * x + z, SIDE, 8)
            if dx:
                for dy in (-1, 1):
                    y = SIDE - 1 if dy < 0 else 0
                    at = px * LINE + (7 if dy < 0 else 16)
                    rims[plane, at : at + 1] = get((dx, dy, dz), 64 * x + 8 * y + z, 1)
        for dy in (-1, 1):
            y = SIDE - 1 if dy < 0 else 0
            at = LINE + (7 if dy < 0 else 16)
            rims[plane, pl.ds(at, SIDE, stride=LINE)] = get((0, dy, dz), 8 * y + z, SIDE, 64)
    for j in range(3):
        for px in range(SIDE + 2):
            at = px * LINE + 7 + j
            put_rim(j, px, jnp.concatenate([rims[0, at : at + 8], rims[1, at : at + 8]], axis=0))


def stacked(even, odd, edge):
    mains, rims = [], []
    for i in range(3):
        for j in range(3):
            main = odd[i : i + 8] if j == 1 else even[i : i + 8, 8 * j : 8 * j + 64]
            mains.append(main.reshape(VOX, 128))
            rims.append(edge[j, i : i + 8].reshape(128, 128))
    return jnp.concatenate(mains, axis=1), jnp.concatenate(rims, axis=1)


def shifted_sum(blocks, edges, down, up):
    before, here, after = blocks
    down[8 : VOX + 8] = before
    up[8 : VOX + 8] = after
    for x in range(SIDE):
        down[pl.ds(7 + 64 * x, SIDE, stride=8)] = edges[16 * x : 16 * x + 8, 0:128]
        up[pl.ds(16 + 64 * x, SIDE, stride=8)] = edges[16 * x + 8 : 16 * x + 16, 128:256]
    return down[7 : VOX + 7] + here + up[9 : VOX + 9]


def fine_matrix(weight, matrix):
    w = weight[...]
    high = high_of(w)
    both = jnp.concatenate([high, w - high], axis=0).T.astype(BF16)
    for tap in range(27):
        rows, cols = tap // 3 * 128, tap % 3 * 128
        block = both[64 * tap : 64 * tap + 64]
        matrix[rows : rows + 64, cols : cols + 128] = block
        matrix[rows + 64 : rows + 128, cols : cols + 128] = block


def coarse_matrix(weight, matrix):
    for tap in range(27):
        rows, cols = tap // 3 * 128, tap % 3 * 128
        block = weight[:, 128 * tap : 128 * tap + 128].T
        high = high_of(block)
        matrix[rows : rows + 128, cols : cols + 128] = high.astype(BF16)
        matrix[rows : rows + 128, 384 + cols : 384 + cols + 128] = (block - high).astype(BF16)


def linker(links, brick, start, own, rows):
    def link(o):
        there = links[brick, columns[o]]
        there_is = there >= 0
        row = jnp.where(there_is, jnp.clip(there - start, 0, rows - 1), own)
        return row, jnp.where(there_is, 1.0, 0.0).astype(F32)

    return link


def loader(parts, own):
    def load(row, start, size, stride):
        row = own if row is None else row
        if stride == 1:
            return parts[row, start : start + size]
        return parts[row, pl.ds(start, size, stride=stride)]

    return load


def fine_conv(parts, own, start, links, brick, scratch, matrix):
    even, odd, edge, rims, down, up = scratch

    def put(px, v):
        even[px] = v.astype(BF16)
        odd[px] = v[8:72].astype(BF16)

    def put_rim(j, px, v):
        edge[j, px] = v.astype(BF16)

    fill(loader(parts, own), linker(links, brick, start, own, parts.shape[0]), put, rims, put_rim)
    main, rim = stacked(even, odd, edge)
    sums = dot(main, matrix[...])
    ends = lambda at: jnp.concatenate([matrix[:, at : at + 128], matrix[:, at + 256 : at + 384]], axis=1)
    edges = dot(rim, ends(0))
    out = shifted_sum([sums[:, 128 * k : 128 * k + 128] for k in range(3)], edges, down, up)
    return out + pltpu.roll(out, 64, 1)


def coarse_conv(parts, own, start, links, brick, scratch, matrix):
    even, odd, edge, rims, down, up = scratch

    def put(px, v):
        high = v.astype(BF16)
        low = (v - high.astype(F32)).astype(BF16)
        for part, value in enumerate((high, low)):
            even[part, px] = value
        middle = v[8:72]
        high = middle.astype(BF16)
        odd[0, px] = high
        odd[1, px] = (middle - high.astype(F32)).astype(BF16)

    def put_rim(j, px, v):
        high = v.astype(BF16)
        edge[0, j, px] = high
        edge[1, j, px] = (v - high.astype(F32)).astype(BF16)

    fill(loader(parts, own), linker(links, brick, start, own, parts.shape[0]), put, rims, put_rim)
    (main_0, rim_0), (main_1, rim_1) = (stacked(even.at[p], odd.at[p], edge.at[p]) for p in range(2))
    tops = dot(main_0, matrix[...])
    rests = dot(main_1, matrix[:, 0:384])
    ends = lambda at: jnp.concatenate([matrix[:, at : at + 128], matrix[:, at + 256 : at + 384]], axis=1)
    edges = dot(rim_0, ends(0)) + dot(rim_0, ends(384)) + dot(rim_1, ends(0))
    cut = lambda v, at: v[:, 128 * at : 128 * at + 128]
    blocks = [cut(tops, k) + cut(tops, 3 + k) + cut(rests, k) for k in range(3)]
    return shifted_sum(blocks, edges, down, up)


def pieces_of(v, wide):
    high = v.astype(BF16)
    return (high, (v - high.astype(F32)).astype(BF16)) if wide else (high,)


def multiplied(lhs, wide, matrix, blocks):
    rows = [matrix.at[pl.ds(128 * at, 128)] for at in blocks]
    take = lambda cols: jnp.concatenate([r[:, cols] for r in rows], axis=0)
    cut = lambda v, at: v[:, 128 * at : 128 * at + 128]
    if not wide:
        sums = dot(lhs[0], take(slice(0, 384)))
        return [cut(sums, k) for k in range(3)]
    tops, rests = dot(lhs[0], take(slice(0, 768))), dot(lhs[1], take(slice(0, 384)))
    return [cut(tops, k) + cut(tops, 3 + k) + cut(rests, k) for k in range(3)]


def line_sum(blocks, down, up):
    rows = blocks[0].shape[0]
    down[8 : rows + 8] = blocks[0]
    up[8 : rows + 8] = blocks[2]
    zeros = jnp.zeros((SIDE, 128), F32)
    for at in range(0, rows, 64):
        down[pl.ds(7 + at, SIDE, stride=8)] = zeros
        up[pl.ds(16 + at, SIDE, stride=8)] = zeros
    return down[7 : rows + 7] + blocks[1] + up[9 : rows + 9]


def clear_center(even, odd, wide):
    for part in range(2 if wide else 1):
        for px in (0, SIDE + 1):
            even[part, px] = jnp.zeros(even.shape[2:], BF16)
            odd[part, px] = jnp.zeros(odd.shape[2:], BF16)


def fill_center(brick, wide, even, odd):
    zeros = jnp.zeros((SIDE, 128), F32)
    for x in range(SIDE):
        middle = brick[64 * x : 64 * x + 64]
        for part, v in enumerate(pieces_of(jnp.concatenate([zeros, middle, zeros], axis=0), wide)):
            even[part, x + 1] = v
        for part, v in enumerate(pieces_of(middle, wide)):
            odd[part, x + 1] = v


def center(wide, even, odd, down, up, matrix, first, last):
    def taps(part):
        windows = []
        for i in range(3):
            for j in range(3):
                xs = slice(first + i, last + i)
                v = odd[part, xs] if j == 1 else even[part, xs, 8 * j : 8 * j + 64]
                windows.append(v.reshape((last - first) * 64, 128))
        return jnp.concatenate(windows, axis=1)

    lhs = [taps(part) for part in range(2 if wide else 1)]
    return line_sum(multiplied(lhs, wide, matrix, range(9)), down, up)


def fill_rims(load, link, wide, at, faces_even, faces_odd, edge, rims):
    found = {o: link(o) for o in columns}
    zeros = jnp.zeros((SIDE, 128), F32)

    def get(o, start, size=SIDE, stride=1):
        row, keep = found[o]
        return load(row, start, size, stride) * keep

    def put_face(face, lines):
        v = jnp.concatenate(lines, axis=0)
        for part, value in enumerate(pieces_of(v, wide)):
            faces_even[part, face, at] = value
        for part, value in enumerate(pieces_of(v[8:72], wide)):
            faces_odd[part, face, at] = value

    def put_rim(j, px, v):
        for part, value in enumerate(pieces_of(v, wide)):
            edge[part, j, at, px] = value

    for face, d in enumerate((-1, 1)):
        spot = SIDE - 1 if d < 0 else 0
        put_face(face, [get((d, -1, 0), 64 * spot + 56), get((d, 0, 0), 64 * spot, 64), get((d, 1, 0), 64 * spot)])
        lines = [get((0, d, 0), 64 * x + 8 * spot) for x in range(SIDE)]
        put_face(2 + face, [zeros] + lines + [zeros])
    fill_edges(get, rims, put_rim)


def add_rims(sums, n, wide, faces_even, faces_odd, edge, down, up, matrix):
    parts = range(2 if wide else 1)
    for face in range(4):
        side = 2 * (face % 2)
        blocks = [3 * side + t for t in range(3)] if face < 2 else [3 * t + side for t in range(3)]
        lhs = []
        for part in parts:
            windows = []
            for t in range(3):
                v = faces_odd[part, face] if t == 1 else faces_even[part, face, :, 8 * t : 8 * t + 64]
                windows.append(v.reshape(n * 64, 128))
            lhs.append(jnp.concatenate(windows, axis=1))
        total = line_sum(multiplied(lhs, wide, matrix, blocks), down, up)
        for b in range(n):
            if face < 2:
                sums[b, 224 * side : 224 * side + 64] += total[64 * b : 64 * b + 64]
            else:
                for x in range(SIDE):
                    at = 64 * x + 28 * side
                    sums[b, at : at + 8] += total[64 * b + 8 * x : 64 * b + 8 * x + 8]
    lhs = []
    for part in parts:
        windows = [edge[part, j, :, i : i + 8].reshape(n * 128, 128) for i in range(3) for j in range(3)]
        lhs.append(jnp.concatenate(windows, axis=1))
    ends = lambda at: jnp.concatenate([matrix[:, at : at + 128], matrix[:, at + 256 : at + 384]], axis=1)
    total = dot(lhs[0], ends(0))
    if wide:
        total = total + dot(lhs[0], ends(384)) + dot(lhs[1], ends(0))
    for b in range(n):
        for x in range(SIDE):
            at = 128 * b + 16 * x
            sums[b, pl.ds(64 * x, SIDE, stride=8)] += total[at : at + 8, 0:128]
            sums[b, pl.ds(64 * x + 7, SIDE, stride=8)] += total[at + 8 : at + 16, 128:256]


def surface_spots():
    spots = [(0, 0, 64, 1), (64, 448, 64, 1)]
    for x in range(1, 7):
        at = 128 + (x - 1) * 16
        spots += [(at, 64 * x, 8, 1), (at + 8, 64 * x + 56, 8, 1)]
    for x in range(1, 7):
        at = 224 + (x - 1) * 12
        spots += [(at, 64 * x + 8, 6, 8), (at + 6, 64 * x + 15, 6, 8)]
    return spots


def pack(get, wire):
    for at, start, size, stride in surface_spots():
        wire[at : at + size] = get(pl.ds(start, size, stride=stride) if stride > 1 else pl.ds(start, size))


def unpack(wire, brick):
    for at, start, size, stride in surface_spots():
        spot = pl.ds(start, size, stride=stride) if stride > 1 else pl.ds(start, size)
        brick[spot] = wire[at : at + size]


def unpack_pair(wire, scratch, first, second):
    a, b = doubled(wire)
    scratch[0] = parted(a)
    scratch[1] = parted(b)
    unpack(scratch.at[0], first)
    unpack(scratch.at[1], second)


def pool(v, scratch, wire):
    lines = v.reshape(4, 2, 4, 2, SIDE, 128)
    sums = (lines[:, 0, :, 0] + lines[:, 0, :, 1]) + (lines[:, 1, :, 0] + lines[:, 1, :, 1])
    scratch[...] = sums.reshape(128, 128)
    for z in range(4):
        halves = [
            scratch[pl.ds(64 * half + 2 * z, 8, stride=8)] + scratch[pl.ds(64 * half + 2 * z + 1, 8, stride=8)]
            for half in range(2)
        ]
        wire[8 * z : 8 * z + 8] = merged(*halves) * 0.125


def split_spot(octant, half, z):
    a, b, c = octant // 4, octant // 2 % 2, octant % 2
    return pl.ds(256 * b + 32 * (4 * a + 2 * half) + 4 * c + z, 8, stride=8)


def place_piece(wire, octant, brick):
    for half, v in enumerate(doubled(wire)):
        v = parted(v)
        for z in range(4):
            brick[split_spot(octant, half, z)] = v[8 * z : 8 * z + 8]


def take_pieces(brick, pieces):
    for octant in range(8):
        for z in range(4):
            halves = [brick[split_spot(octant, half, z)] for half in range(2)]
            pieces[octant, 8 * z : 8 * z + 8] = merged(*halves)


def swap_halves(v, split):
    first, second = (2, SIDE) if split else (SIDE, 2)
    return v.reshape(first, second, 32, 128).swapaxes(0, 1).reshape(VOX, 128)


def grow(piece, scratch):
    for half, v in enumerate(doubled(piece)):
        for z in range(4):
            rows = v[8 * z : 8 * z + 8]
            scratch[pl.ds(64 * half + 2 * z, 8, stride=8)] = rows
            scratch[pl.ds(64 * half + 2 * z + 1, 8, stride=8)] = rows
    lines = scratch[...].reshape(4, 1, 4, 1, SIDE, 128)
    return jnp.broadcast_to(lines, (4, 2, 4, 2, SIDE, 128)).reshape(VOX, 128)


def step_kernel(
    x_any, fine_links, own_codes, coarse_links, in_any, in_bias, down_weight, one_any, one_bias, two_any, two_bias,
    up_weight, out_any, out_bias,
    out,
    x, in_weight, one_weight, two_weight, out_weight, loads,
    matrix, last_matrix, one_matrix, two_matrix,
    even, odd, edge, wide_even, wide_odd, wide_edge, rims, shift_down, shift_up,
    faces_even, faces_odd, face_edge, wide_faces_even, wide_faces_odd, wide_face_edge, wide_sums,
    parts, turned, hidden, halves, small, grown,
    x_send, x_halo, hidden_send, hidden_halo,
    code_block, codes, code_table, table, code_scalars, table_scalars,
    pooled, placed, base, first,
    first_send, first_halo, lifted, wanted, window, low_window, high_window,
    local_sems, send_x, recv_x, send_hidden, recv_hidden, send_codes, recv_codes, send_pooled, recv_pooled,
    send_first, recv_first, send_relay, recv_relay, send_wanted, recv_wanted,
):
    group, member = lax.axis_index("grp"), lax.axis_index("dev")
    groups, members = lax.axis_size("grp"), lax.axis_size("dev")
    position = group * members + member
    whole = groups * members
    count, slots = fine_links.shape[0], coarse_links.shape[0]
    pairs = count // 2
    relayed = members == 4
    has_left, has_right = position > 0, position < whole - 1
    has_low, has_high = group > 0, group < groups - 1
    is_first, is_last = member == 0, member == members - 1
    left_at = (jnp.maximum(position - 1, 0) // members, (position + members - 1) % members)
    right_at = (jnp.minimum(position + 1, whole - 1) // members, (position + 1) % members)
    low_at = (jnp.maximum(group - 1, 0), members - 1)
    high_at = (jnp.minimum(group + 1, groups - 1), 0)
    always = position >= 0

    def fetch(k, source, target):
        return pltpu.make_async_copy(source, target, loads.at[k])

    fetches = [
        fetch(0, x_any, x), fetch(1, in_any, in_weight), fetch(2, one_any, one_weight),
        fetch(3, two_any, two_weight), fetch(4, out_any, out_weight),
    ]
    for copy in fetches:
        copy.start()

    barrier = pltpu.get_barrier_semaphore()

    def greet(where):
        pl.semaphore_signal(barrier, inc=1, device_id=where, device_id_type=MESH)

    pl.when(has_left)(lambda: greet(left_at))
    pl.when(has_right)(lambda: greet(right_at))
    for k in range(1, members):
        greet((group, (member + k) % members))
    for k in range(members):
        pl.when(is_first & has_low)(lambda k=k: greet((low_at[0], k)))
        pl.when(is_last & has_high)(lambda k=k: greet((high_at[0], k)))

    def remote(src, dst, send, recv, where):
        return pltpu.make_async_remote_copy(
            src_ref=src, dst_ref=dst, send_sem=send, recv_sem=recv, device_id=where, device_id_type=MESH
        )

    row = lax.broadcasted_iota(jnp.int32, (SIDE, 128), 0)
    block = jnp.full((SIDE, 128), -1, jnp.int32)
    for i in range(count):
        block = jnp.where(row == i, own_codes[i], block)
    code_block[...] = block
    codes[members + member] = block
    fetches[0].wait()
    for pair in range(pairs):
        turned[pair] = x[2 * pair : 2 * pair + 2].reshape(128, VOX).T
    pack(lambda spot: turned[0, spot], x_send.at[0])
    pack(lambda spot: turned[pairs - 1, spot], x_send.at[1])
    pl.semaphore_wait(
        barrier,
        jnp.where(has_left, 1, 0) + jnp.where(has_right, 1, 0) + (members - 1)
        + jnp.where(has_low, 1, 0) + jnp.where(has_high, 1, 0),
    )

    def halo_copies(source, halo, send, recv, at=0, rows=SURFACE):
        spot = pl.ds(at, rows)
        to_left = remote(source.at[0, spot], halo.at[1, spot], send.at[0], recv.at[1], left_at)
        to_right = remote(source.at[1, spot], halo.at[0, spot], send.at[1], recv.at[0], right_at)
        return to_left, to_right

    def start_halo(copies):
        pl.when(has_left)(copies[0].start)
        pl.when(has_right)(copies[1].start)

    def end_halo(copies):
        pl.when(has_left)(copies[1].wait_recv)
        pl.when(has_right)(copies[0].wait_recv)

    def end_halo_sends(copies):
        pl.when(has_left)(copies[0].wait_send)
        pl.when(has_right)(copies[1].wait_send)

    def shared_copies(source, at, send, recv):
        near = [
            remote(source, at(members + member), send.at[k], recv.at[members + member], (group, (member + k) % members))
            for k in range(1, members)
        ]
        to_high = remote(source, at(member), send.at[0], recv.at[member], high_at)
        to_low = remote(source, at(2 * members + member), send.at[members], recv.at[2 * members + member], low_at)
        return near, to_high, to_low

    def start_shared(copies):
        near, to_high, to_low = copies
        for copy in near:
            copy.start()
        pl.when(has_high)(to_high.start)
        pl.when(has_low)(to_low.start)

    def end_near(source, at, send, recv):
        for k in range(1, members):
            other = (member + k) % members
            remote(source, at(members + other), send.at[k], recv.at[members + other], (group, other)).wait_recv()

    def end_far(source, at, send, recv):
        for k in range(members):
            from_low = remote(source, at(k), send.at[0], recv.at[k], low_at)
            from_high = remote(source, at(2 * members + k), send.at[0], recv.at[2 * members + k], high_at)
            pl.when(is_first & has_low)(from_low.wait_recv)
            pl.when(is_last & has_high)(from_high.wait_recv)

    def end_shared_sends(copies):
        near, to_high, to_low = copies
        for copy in near:
            copy.wait_send()
        pl.when(has_high)(to_high.wait_send)
        pl.when(has_low)(to_low.wait_send)

    x_copies = halo_copies(x_send, x_halo, send_x, recv_x)
    start_halo(x_copies)
    code_at = lambda k: codes.at[k]
    code_copies = shared_copies(code_block, code_at, send_codes, recv_codes)
    start_shared(code_copies)

    fetches[1].wait()
    fine_matrix(in_weight, matrix)
    for pair in range(pairs):
        for one, v in enumerate(doubled(turned[pair])):
            parts[HALO + 2 * pair + one] = parted(v)

    clear_center(even, odd, False)

    def own_step(i, carry):
        fill_center(parts.at[HALO + i], False, even, odd)
        hidden[i] = center(False, even, odd, shift_down, shift_up, matrix, 0, SIDE)
        return carry

    lax.fori_loop(0, count, own_step, 0)
    end_near(code_block, code_at, send_codes, recv_codes)
    end_far(code_block, code_at, send_codes, recv_codes)
    lane = lax.broadcasted_iota(jnp.int32, (SIDE, 128), 1)
    table_rows = jnp.full((SIDE, 128), -1, jnp.int32)
    for near in range(3):
        there = position + near - 1
        valid = (there >= 0) & (there < whole)
        there = jnp.where(valid, there, position)
        there_group = there // members
        there_member = there - there_group * members
        band = there_group - group + 1
        spot = jnp.where(valid, lane, -1000) + there_member * slots * 8
        best = jnp.full((SIDE, 128), -1, jnp.int32)
        for k in range(members):
            match = (codes[band * members + k] == spot) & (row < count) & (lane < slots * 8)
            best = jnp.maximum(best, jnp.where(match, (band * members + k) * count + row, -1))
        top = jnp.max(best, axis=0, keepdims=True)
        table_rows = jnp.where(row == near, top, table_rows)
    code_table[...] = codes[pl.ds(members, members)]
    table[...] = table_rows
    to_table = pltpu.make_async_copy(table, table_scalars, local_sems.at[0])
    to_codes = pltpu.make_async_copy(code_table, code_scalars, local_sems.at[1])
    to_table.start()
    to_codes.start()

    fine_start = position * count - HALO
    end_halo(x_copies)
    for side, at in ((0, 0), (1, HALO + count)):
        unpack_pair(x_halo[side], halves, parts.at[at], parts.at[at + 1])
    fine_scratch = (even.at[0], odd.at[0], edge, rims, shift_down, shift_up)
    two = lambda bias: jnp.concatenate([bias[...], bias[...]], axis=1)
    in_both = two(in_bias)

    def pooled_at(i):
        return lambda k: pooled.at[k, i]

    def pooled_copies(i):
        return shared_copies(pooled.at[members + member, i], pooled_at(i), send_pooled.at[i], recv_pooled.at[i])

    def first_step(pair, carry):
        at = 2 * pair
        for one in range(2):
            own = HALO + at + one
            fill_rims(
                loader(parts, own), linker(fine_links, at + one, fine_start, own, parts.shape[0]), False, one,
                faces_even, faces_odd, face_edge, rims,
            )
        sums = hidden.at[pl.ds(at, 2)]
        add_rims(sums, 2, False, faces_even, faces_odd, face_edge, shift_down, shift_up, matrix)
        for one in range(2):
            v = sums[one]
            v = silu(v + pltpu.roll(v, 64, 1) + in_both)
            pool(v, small, pooled.at[members + member, at + one])
            sums[one] = v
            start_shared(pooled_copies(at + one))
        return carry

    lax.fori_loop(0, pairs, first_step, 0)
    pack(lambda spot: merged(hidden[0, spot], hidden[1, spot]), hidden_send.at[0])
    pack(lambda spot: merged(hidden[count - 2, spot], hidden[count - 1, spot]), hidden_send.at[1])
    hidden_copies = [
        halo_copies(hidden_send, hidden_halo, send_hidden.at[part], recv_hidden.at[part], at, rows)
        for part, (at, rows) in enumerate(((0, EARLY), (EARLY, SURFACE - EARLY)))
    ]
    start_halo(hidden_copies[0])
    fetches[2].wait()
    coarse_matrix(one_weight, one_matrix)
    fetches[3].wait()
    coarse_matrix(two_weight, two_matrix)
    fetches[4].wait()
    fine_matrix(out_weight, last_matrix)
    to_table.wait()
    to_codes.wait()

    turned_down = down_weight[...]
    down_high = high_of(turned_down)
    down_both = jnp.concatenate([down_high, turned_down - down_high], axis=1)
    down_matrix = jnp.concatenate([down_both, down_both], axis=0).astype(BF16)
    for i in range(count):
        end_near(pooled.at[members + member, i], pooled_at(i), send_pooled.at[i], recv_pooled.at[i])
    for i in range(count):
        end_far(pooled.at[members + member, i], pooled_at(i), send_pooled.at[i], recv_pooled.at[i])

    def base_of(near):
        for slot in range(slots):
            for octant in range(8):
                which = table_scalars[near, slot * 8 + octant]
                there_is = which >= 0
                which = jnp.where(there_is, jnp.minimum(which, 3 * members * count - 1), (members + member) * count)
                keep = jnp.where(there_is, 1.0, 0.0).astype(F32)
                place_piece(pooled[which // count, which % count] * keep, octant, placed.at[slot])
        sums = dot(placed[...].reshape(slots * VOX, 128).astype(BF16), down_matrix)
        sums = sums[:, 0:128] + sums[:, 128:256]
        for slot in range(slots):
            base[near * slots + slot] = swap_halves(sums[slot * VOX : slot * VOX + VOX], True)

    def base_step(t, carry):
        base_of(t)
        return carry

    lax.fori_loop(0, 3, base_step, 0)
    coarse_start = (position - 1) * slots
    wide_scratch = (wide_even, wide_odd, wide_edge, rims, shift_down, shift_up)

    if relayed:
        parity = member % 2
        x_at = (group, member + 1 - 2 * parity)
        relay_group = group + jnp.where(member == 1, -1, 0) + jnp.where(member == 2, 1, 0)
        relays_out = (relay_group >= 0) & (relay_group < groups)
        relays_in = jnp.where(is_first, has_low, True) & jnp.where(is_last, has_high, True)
        relay_at = (jnp.clip(relay_group, 0, groups - 1), (member + 2) % members)

        def direct(i, c):
            at, rows = CHUNKS[c]
            return remote(
                first_send.at[i, pl.ds(at, rows)], first_halo.at[parity, i, pl.ds(at, rows)],
                send_first.at[i, c], recv_first.at[i, c], x_at,
            )

        def came(i, c):
            at, rows = CHUNKS[c]
            return remote(
                first_send.at[i, pl.ds(at, rows)], first_halo.at[1 - parity, i, pl.ds(at, rows)],
                send_first.at[i, c], recv_first.at[i, c], x_at,
            )

        def relay(i, c):
            at, rows = CHUNKS[c]
            return remote(
                first_halo.at[1 - parity, i, pl.ds(at, rows)], first_halo.at[parity, i, pl.ds(at, rows)],
                send_relay.at[i, c], recv_relay.at[i, c], relay_at,
            )

        exists = jnp.where(parity == 0, has_left, has_right)
        far_at = tuple(jnp.where(parity == 0, a, b) for a, b in zip(left_at, right_at))

        def far(i, c):
            spot = pl.ds(*CHUNKS[c])
            return remote(
                first_send.at[i, spot], first_halo.at[1 - parity, i, spot],
                send_relay.at[i, c], recv_relay.at[i, c], far_at,
            )

        def start_first(i):
            for c in range(len(CHUNKS)):
                direct(i, c).start()
            for c in range(len(CHUNKS) - STRAIGHT, len(CHUNKS)):
                pl.when((i == slots - 1) & exists)(far(i, c).start)

        arrivals = [(i, c) for i in range(slots) for c in range(len(CHUNKS))]

        def pass_on(at):
            i, c = arrivals[at]
            came(i, c).wait_recv()
            if at < len(arrivals) - STRAIGHT:
                pl.when(relays_out)(relay(i, c).start)

        def end_first(passed):
            for at in range(passed, len(arrivals)):
                pass_on(at)
            for i in range(slots):
                for c in range(len(CHUNKS)):
                    pl.when(relays_in)(relay(i, c).wait_recv)

        def end_first_sends():
            for at, (i, c) in enumerate(arrivals):
                direct(i, c).wait_send()
                if at < len(arrivals) - STRAIGHT:
                    pl.when(relays_out)(relay(i, c).wait_send)
                else:
                    pl.when(exists)(far(i, c).wait_send)
    else:

        def sides(i):
            to_left = remote(first_send.at[i], first_halo.at[1, i], send_first.at[i, 0], recv_first.at[i, 1], left_at)
            to_right = remote(first_send.at[i], first_halo.at[0, i], send_first.at[i, 1], recv_first.at[i, 0], right_at)
            return to_left, to_right

        def start_first(i):
            start_halo(sides(i))

        def pass_on(at):
            pass

        def end_first(passed):
            for i in range(slots):
                end_halo(sides(i))

        def end_first_sends():
            for i in range(slots):
                end_halo_sends(sides(i))

    def second_step(i, carry):
        v = silu(coarse_conv(base, slots + i, coarse_start, coarse_links, i, wide_scratch, one_matrix) + one_bias[...])
        first[slots + i] = v
        pack(lambda spot: first[slots + i, spot], first_send.at[i])
        start_first(i)
        return carry

    lax.fori_loop(0, slots, second_step, 0)
    turned_up = up_weight[...].T
    up_high = high_of(turned_up)
    up_both = jnp.concatenate([up_high, turned_up - up_high], axis=1)
    up_matrix = jnp.concatenate([up_both, up_both], axis=0).astype(BF16)
    clear_center(wide_even, wide_odd, True)
    passed = 0
    for i in range(slots):
        fill_center(first.at[slots + i], True, wide_even, wide_odd)
        for half in range(2):
            pass_on(passed)
            passed += 1
            spot = slice(256 * half, 256 * half + 256)
            wide_sums[i, spot] = center(
                True, wide_even, wide_odd, shift_down, shift_up, two_matrix, 4 * half, 4 * half + 4
            )
    end_first(passed)
    start_halo(hidden_copies[1])
    for side, at in ((0, 0), (1, 2 * slots)):
        for i in range(slots):
            unpack(first_halo.at[side, i], first.at[at + i])

    def wide_rim_step(i, carry):
        fill_rims(
            loader(first, slots + i), linker(coarse_links, i, coarse_start, slots + i, first.shape[0]), True, i,
            wide_faces_even, wide_faces_odd, wide_face_edge, rims,
        )
        return carry

    lax.fori_loop(0, slots, wide_rim_step, 0)
    add_rims(
        wide_sums, slots, True, wide_faces_even, wide_faces_odd, wide_face_edge, shift_down, shift_up, two_matrix
    )

    def third_step(i, carry):
        v = silu(wide_sums[i] + two_bias[...])
        high = v.astype(BF16)
        low = (v - high.astype(F32)).astype(BF16)
        sums = dot(jnp.concatenate([high, low], axis=1), up_matrix)
        placed[0] = swap_halves(sums + pltpu.roll(sums, 64, 1), False)
        take_pieces(placed.at[0], lifted.at[pl.ds(i * 8, 8)])
        return carry

    lax.fori_loop(0, slots, third_step, 0)
    bricks = members * count
    zeros = jnp.zeros((HALO,) + wanted.shape[1:], F32)
    wanted[0:HALO] = zeros
    wanted[HALO + bricks :] = zeros

    def choose(j, carry):
        code = code_scalars[j // count, j % count, 0] - member * slots * 8
        mine = (code >= 0) & (code < slots * 8)
        keep = jnp.where(mine, 1.0, 0.0).astype(F32)
        wanted[HALO + j] = lifted[jnp.where(mine, code, 0)] * keep
        return carry

    lax.fori_loop(0, bricks, choose, 0)
    parts_of = ((HALO, count, None), (0, HALO, 0), (HALO + count, HALO, members - 1))

    def to_member(k, part):
        other = (member + k) % members
        at, rows, _ = parts_of[part]
        return remote(
            wanted.at[pl.ds(other * count + at, rows)], window.at[member, pl.ds(at, rows)], send_wanted.at[k, part],
            recv_wanted.at[members + member, part], (group, other),
        )

    def from_member(k, part):
        other = (member + k) % members
        at, rows, _ = parts_of[part]
        return remote(
            wanted.at[pl.ds(at, rows)], window.at[other, pl.ds(at, rows)], send_wanted.at[k, part],
            recv_wanted.at[members + other, part], (group, other),
        )

    def when_read(who, part, action):
        none_at = parts_of[part][2]
        if none_at is None:
            action()
        else:
            pl.when(who != none_at)(action)

    to_high = remote(
        wanted.at[pl.ds(bricks, HALO)], low_window.at[member], send_wanted.at[0, 0], recv_wanted.at[member, 0], high_at
    )
    to_low = remote(
        wanted.at[pl.ds(HALO, HALO)], high_window.at[member], send_wanted.at[members, 0],
        recv_wanted.at[2 * members + member, 0], low_at,
    )
    for k in range(1, members):
        to_member(k, 0).start()
    for k in range(1, members):
        for part in (1, 2):
            when_read((member + k) % members, part, to_member(k, part).start)
    pl.when(has_high)(to_high.start)
    pl.when(has_low)(to_low.start)
    window[member] = wanted[pl.ds(member * count, count + 2 * HALO)]
    for copies in hidden_copies:
        end_halo(copies)
    for k in range(1, members):
        from_member(k, 0).wait_recv()

    def total(source, i):
        piece = source[0, i]
        for owner in range(1, members):
            piece = piece + source[owner, i]
        return piece

    def own_blend(i, carry):
        rising = grow(total(window, HALO + i), small)
        parts[HALO + i] = parted(silu(hidden[i] + rising))
        return carry

    lax.fori_loop(0, count, own_blend, 0)
    for k in range(1, members):
        for part in (1, 2):
            when_read(member, part, from_member(k, part).wait_recv)
    for k in range(members):
        spot = wanted.at[pl.ds(0, HALO)]
        from_low = remote(spot, low_window.at[k], send_wanted.at[0, 0], recv_wanted.at[k, 0], low_at)
        from_high = remote(
            spot, high_window.at[k], send_wanted.at[0, 0], recv_wanted.at[2 * members + k, 0], high_at
        )
        pl.when(is_first & has_low)(from_low.wait_recv)
        pl.when(is_last & has_high)(from_high.wait_recv)
    for side, at, edge_window, beyond in (
        (0, 0, low_window, is_first), (1, HALO + count, high_window, is_last),
    ):
        for one in range(HALO):
            piece = jnp.where(beyond, total(edge_window, one), total(window, at + one))
            grown[one] = grow(piece, small)
        pack(lambda spot: merged(grown[0, spot], grown[1, spot]), halves.at[0])
        wire = silu(hidden_halo[side] + halves[0])
        unpack_pair(wire, halves, parts.at[at], parts.at[at + 1])
    out_both = two(out_bias)

    def last_step(i, carry):
        hidden[i] = fine_conv(parts, HALO + i, fine_start, fine_links, i, fine_scratch, last_matrix) + out_both
        return carry

    lax.fori_loop(0, count, last_step, 0)
    for pair in range(pairs):
        flat = merged(hidden[2 * pair], hidden[2 * pair + 1]).T
        out[2 * pair : 2 * pair + 2] = x[2 * pair : 2 * pair + 2] + flat.reshape(2, 64, VOX)

    end_halo_sends(x_copies)
    end_shared_sends(code_copies)
    for i in range(count):
        end_shared_sends(pooled_copies(i))
    for copies in hidden_copies:
        end_halo_sends(copies)
    end_first_sends()
    for k in range(1, members):
        to_member(k, 0).wait_send()
        for part in (1, 2):
            when_read((member + k) % members, part, to_member(k, part).wait_send)
    pl.when(has_high)(to_high.wait_send)
    pl.when(has_low)(to_low.wait_send)


def per_device(
    x, fine_links, parent_codes, coarse_links,
    in_weight, in_bias, down, one_weight, one_bias, two_weight, two_bias, up, out_weight, out_bias,
):
    count, channels = x.shape[0], x.shape[1]
    slots, wide = coarse_links.shape[0], one_bias.shape[0]
    members = lax.axis_size("dev")
    row = lambda bias: bias.reshape(1, -1)
    vmem = pl.BlockSpec(memory_space=pltpu.VMEM)
    smem = pl.BlockSpec(memory_space=pltpu.SMEM)
    anywhere = pl.BlockSpec(memory_space=pl.ANY)
    floats = lambda *shape: pltpu.VMEM(shape, F32)
    halfs = lambda *shape: pltpu.VMEM(shape, BF16)
    ints = lambda *shape: pltpu.VMEM(shape, jnp.int32)
    sems = lambda *shape: pltpu.SemaphoreType.DMA(shape)
    span = count + 2 * HALO
    wire = (32, 128)
    scratch = [
        floats(*x.shape), floats(*in_weight.shape), floats(*one_weight.shape), floats(*two_weight.shape),
        floats(*out_weight.shape), sems(5),
        halfs(1152, 384), halfs(1152, 384), halfs(1152, 768), halfs(1152, 768),
        halfs(1, 10, 80, 128), halfs(1, 10, 64, 128), halfs(3, 10, 16, 128),
        halfs(2, 10, 80, 128), halfs(2, 10, 64, 128), halfs(2, 3, 10, 16, 128),
        floats(2, 10 * LINE, 128), floats(VOX + 16, 128), floats(VOX + 16, 128),
        halfs(1, 4, 2, 80, 128), halfs(1, 4, 2, 64, 128), halfs(1, 3, 2, 10, 16, 128),
        halfs(2, 4, slots, 80, 128), halfs(2, 4, slots, 64, 128), halfs(2, 3, slots, 10, 16, 128),
        floats(slots, VOX, 128),
        floats(span, VOX, 128), floats(count // 2, VOX, 128), floats(count, VOX, 128),
        floats(2, SURFACE, 128), floats(128, 128), floats(HALO, VOX, 128),
        floats(2, SURFACE, 128), floats(2, SURFACE, 128), floats(2, SURFACE, 128), floats(2, SURFACE, 128),
        ints(8, 128), ints(3 * members, 8, 128), ints(members, 8, 128), ints(8, 128),
        pltpu.SMEM((members, 8, 128), jnp.int32), pltpu.SMEM((8, 128), jnp.int32),
        floats(3 * members, count, *wire), floats(slots, VOX, 128), floats(3 * slots, VOX, 128), floats(3 * slots, VOX, 128),
        floats(slots, SURFACE, 128), floats(2, slots, SURFACE, 128), floats(slots * 8, *wire),
        floats(members * count + 2 * HALO, *wire), floats(members, span, *wire), floats(members, HALO, *wire),
        floats(members, HALO, *wire),
        sems(2), sems(2), sems(2), sems(2, 2), sems(2, 2), sems(members + 1), sems(3 * members),
        sems(count, members + 1), sems(count, 3 * members),
        sems(slots, 3), sems(slots, 3), sems(slots, 3), sems(slots, 3), sems(members + 1, 3), sems(3 * members, 3),
    ]
    return pl.pallas_call(
        step_kernel,
        out_shape=jax.ShapeDtypeStruct(x.shape, F32),
        in_specs=[anywhere, smem, smem, smem, anywhere, vmem, vmem, anywhere, vmem, anywhere, vmem, vmem, anywhere, vmem],
        out_specs=vmem,
        scratch_shapes=scratch,
        name="step",
        compiler_params=pltpu.CompilerParams(collective_id=1, has_side_effects=True, vmem_limit_bytes=LIMIT),
    )(
        x, fine_links, parent_codes, coarse_links, in_weight, row(in_bias), down.T, one_weight, row(one_bias),
        two_weight, row(two_bias), up, out_weight, row(out_bias),
    )


def solution(mesh):
    bricks = P(("grp", "dev"), None, None)
    rows = P(("grp", "dev"), None)
    placed = (bricks, rows, P(("grp", "dev")), rows) + (P(),) * 10
    return jax.shard_map(per_device, mesh=mesh, in_specs=placed, out_specs=bricks, check_vma=False)
```

```python
import functools

import jax
import jax.numpy as jnp
from jax import lax
from jax.experimental import pallas as pl
from jax.experimental.pallas import tpu as pltpu
from jax.sharding import PartitionSpec as P

F32 = jnp.float32
BF16 = jnp.bfloat16
MESH = pl.DeviceIdType.MESH
SIDE = 8
VOX = SIDE * SIDE * SIDE
HALO = 2
SURFACE = VOX - 6 * 6 * 6
LINE = 24
LIMIT = 62 * 1024 * 1024
EARLY = 160
CHUNKS = ((0, 120), (120, 96), (216, 80))
STRAIGHT = 1

offsets = [(x, y, z) for x in (-1, 0, 1) for y in (-1, 0, 1) for z in (-1, 0, 1)]
columns = {o: k for k, o in enumerate(o for o in offsets if o != (0, 0, 0))}


def high_of(v):
    return v.astype(BF16).astype(F32)


def silu(v):
    return v / (1.0 + jnp.exp(-v))


def dot(a, b):
    return lax.dot_general(a, b, (((1,), (0,)), ((), ())), preferred_element_type=F32)


def first_half(v):
    return lax.broadcasted_iota(jnp.int32, v.shape, 1) < v.shape[1] // 2


def merged(a, b):
    return jnp.where(first_half(a), a, b)


def doubled(v):
    turned = pltpu.roll(v, v.shape[1] // 2, 1)
    return merged(v, turned), merged(turned, v)


def parted(v):
    high = high_of(v)
    return merged(high, v - high)


def fill(load, link, put, rims, put_rim):
    found = {o: link(o) for o in columns}

    def get(o, start, size=SIDE, stride=1):
        row, keep = found[o]
        return load(row, start, size, stride) * keep

    for px in range(SIDE + 2):
        dx = -1 if px == 0 else (1 if px == SIDE + 1 else 0)
        x = {-1: SIDE - 1, 0: px - 1, 1: 0}[dx]
        low = get((dx, -1, 0), 64 * x + 56)
        high = get((dx, 1, 0), 64 * x)
        middle = get((dx, 0, 0), 64 * x, 64) if dx else load(None, 64 * x, 64, 1)
        put(px, jnp.concatenate([low, middle, high], axis=0))
    fill_edges(get, rims, put_rim)


def fill_edges(get, rims, put_rim):
    for plane, dz in enumerate((-1, 1)):
        z = SIDE - 1 if dz < 0 else 0
        for px in range(SIDE + 2):
            dx = -1 if px == 0 else (1 if px == SIDE + 1 else 0)
            x = {-1: SIDE - 1, 0: px - 1, 1: 0}[dx]
            rims[plane, px * LINE + 8 : px * LINE + 16] = get((dx, 0, dz), 64 * x + z, SIDE, 8)
            if dx:
                for dy in (-1, 1):
                    y = SIDE - 1 if dy < 0 else 0
                    at = px * LINE + (7 if dy < 0 else 16)
                    rims[plane, at : at + 1] = get((dx, dy, dz), 64 * x + 8 * y + z, 1)
        for dy in (-1, 1):
            y = SIDE - 1 if dy < 0 else 0
            at = LINE + (7 if dy < 0 else 16)
            rims[plane, pl.ds(at, SIDE, stride=LINE)] = get((0, dy, dz), 8 * y + z, SIDE, 64)
    for j in range(3):
        for px in range(SIDE + 2):
            at = px * LINE + 7 + j
            put_rim(j, px, jnp.concatenate([rims[0, at : at + 8], rims[1, at : at + 8]], axis=0))


def stacked(even, odd, edge):
    mains, rims = [], []
    for i in range(3):
        for j in range(3):
            main = odd[i : i + 8] if j == 1 else even[i : i + 8, 8 * j : 8 * j + 64]
            mains.append(main.reshape(VOX, 128))
            rims.append(edge[j, i : i + 8].reshape(128, 128))
    return jnp.concatenate(mains, axis=1), jnp.concatenate(rims, axis=1)


def shifted_sum(blocks, edges, down, up):
    before, here, after = blocks
    down[8 : VOX + 8] = before
    up[8 : VOX + 8] = after
    for x in range(SIDE):
        down[pl.ds(7 + 64 * x, SIDE, stride=8)] = edges[16 * x : 16 * x + 8, 0:128]
        up[pl.ds(16 + 64 * x, SIDE, stride=8)] = edges[16 * x + 8 : 16 * x + 16, 128:256]
    return down[7 : VOX + 7] + here + up[9 : VOX + 9]


def fine_matrix(weight, matrix):
    w = weight[...]
    high = high_of(w)
    both = jnp.concatenate([high, w - high], axis=0).T.astype(BF16)
    for tap in range(27):
        rows, cols = tap // 3 * 128, tap % 3 * 128
        block = both[64 * tap : 64 * tap + 64]
        matrix[rows : rows + 64, cols : cols + 128] = block
        matrix[rows + 64 : rows + 128, cols : cols + 128] = block


def coarse_matrix(weight, matrix):
    for tap in range(27):
        rows, cols = tap // 3 * 128, tap % 3 * 128
        block = weight[:, 128 * tap : 128 * tap + 128].T
        high = high_of(block)
        matrix[rows : rows + 128, cols : cols + 128] = high.astype(BF16)
        matrix[rows : rows + 128, 384 + cols : 384 + cols + 128] = (block - high).astype(BF16)


def linker(links, brick, start, own, rows):
    def link(o):
        there = links[brick, columns[o]]
        there_is = there >= 0
        row = jnp.where(there_is, jnp.clip(there - start, 0, rows - 1), own)
        return row, jnp.where(there_is, 1.0, 0.0).astype(F32)

    return link


def loader(parts, own):
    def load(row, start, size, stride):
        row = own if row is None else row
        if stride == 1:
            return parts[row, start : start + size]
        return parts[row, pl.ds(start, size, stride=stride)]

    return load


def fine_conv(parts, own, start, links, brick, scratch, matrix):
    even, odd, edge, rims, down, up = scratch

    def put(px, v):
        even[px] = v.astype(BF16)
        odd[px] = v[8:72].astype(BF16)

    def put_rim(j, px, v):
        edge[j, px] = v.astype(BF16)

    fill(loader(parts, own), linker(links, brick, start, own, parts.shape[0]), put, rims, put_rim)
    main, rim = stacked(even, odd, edge)
    sums = dot(main, matrix[...])
    ends = lambda at: jnp.concatenate([matrix[:, at : at + 128], matrix[:, at + 256 : at + 384]], axis=1)
    edges = dot(rim, ends(0))
    out = shifted_sum([sums[:, 128 * k : 128 * k + 128] for k in range(3)], edges, down, up)
    return out + pltpu.roll(out, 64, 1)


def packed_matrix(weight, matrix):
    w = weight[...]
    for ij in range(9):
        ks = [w[:, 64 * (3 * ij + k) : 64 * (3 * ij + k) + 64] for k in (0, 1, 2, 2)]
        block = jnp.concatenate(ks, axis=0).T
        high = high_of(block)
        low = (block - high).astype(BF16)
        high = high.astype(BF16)
        matrix[128 * ij : 128 * ij + 64] = high
        matrix[128 * ij + 64 : 128 * ij + 128] = high
        i, j = ij // 3, ij % 3
        at = 1152 + 128 * j + 64 * i if i < 2 else (1536, 1664, 1600)[j]
        matrix[at : at + 64] = low
    matrix[1728:1792] = jnp.zeros((64, 256), BF16)


def packed_conv(parts, own, start, links, brick, scratch, pair_scratch, matrix, rim_matrix):
    even, odd, edge, rims, down, up = scratch
    next_even, next_odd, over = pair_scratch
    held = []

    def put(px, v):
        even[px] = v.astype(BF16)
        odd[px] = v[8:72].astype(BF16)
        turned = pltpu.roll(v, 64, 1)
        pairs = [(px - 1, merged(held[-1], turned))] if px else []
        if px == SIDE + 1:
            pairs.append((px, merged(v, jnp.zeros_like(v))))
        for at, pair in pairs:
            next_even[at] = pair.astype(BF16)
            next_odd[at] = pair[8:72].astype(BF16)
        if px >= 2:
            over[px] = merged(v[0:64], turned[16:80]).astype(BF16)
        held.append(v)

    def put_rim(j, px, v):
        edge[j, px] = v.astype(BF16)

    fill(loader(parts, own), linker(links, brick, start, own, parts.shape[0]), put, rims, put_rim)
    main, rim = stacked(even, odd, edge)
    flat = lambda v: v.reshape(VOX, 128)
    more = [next_even[0:8, 0:64], next_odd[0:8], next_even[0:8, 16:80], over[2:10], next_odd[2:10]]
    sums = dot(jnp.concatenate([main] + [flat(v) for v in more], axis=1), matrix[...])
    ends = jnp.concatenate([rim_matrix[:, 0:128], rim_matrix[:, 256:384]], axis=1)
    edges = dot(rim, ends)
    low_edge, high_edge = edges[:, 0:128], edges[:, 128:256]
    low_edge = low_edge + pltpu.roll(low_edge, 64, 1)
    high_edge = high_edge + pltpu.roll(high_edge, 64, 1)
    front, back = sums[:, 0:128], sums[:, 128:256]
    out = shifted_sum([front, pltpu.roll(front, 64, 1), back], jnp.concatenate([low_edge, high_edge], axis=1), down, up)
    return out


def coarse_conv(parts, own, start, links, brick, scratch, matrix):
    even, odd, edge, rims, down, up = scratch

    def put(px, v):
        high = v.astype(BF16)
        low = (v - high.astype(F32)).astype(BF16)
        for part, value in enumerate((high, low)):
            even[part, px] = value
        middle = v[8:72]
        high = middle.astype(BF16)
        odd[0, px] = high
        odd[1, px] = (middle - high.astype(F32)).astype(BF16)

    def put_rim(j, px, v):
        high = v.astype(BF16)
        edge[0, j, px] = high
        edge[1, j, px] = (v - high.astype(F32)).astype(BF16)

    fill(loader(parts, own), linker(links, brick, start, own, parts.shape[0]), put, rims, put_rim)
    (main_0, rim_0), (main_1, rim_1) = (stacked(even.at[p], odd.at[p], edge.at[p]) for p in range(2))
    tops = dot(main_0, matrix[...])
    rests = dot(main_1, matrix[:, 0:384])
    ends = lambda at: jnp.concatenate([matrix[:, at : at + 128], matrix[:, at + 256 : at + 384]], axis=1)
    edges = dot(rim_0, ends(0)) + dot(rim_0, ends(384)) + dot(rim_1, ends(0))
    cut = lambda v, at: v[:, 128 * at : 128 * at + 128]
    blocks = [cut(tops, k) + cut(tops, 3 + k) + cut(rests, k) for k in range(3)]
    return shifted_sum(blocks, edges, down, up)


def pieces_of(v, wide):
    high = v.astype(BF16)
    return (high, (v - high.astype(F32)).astype(BF16)) if wide else (high,)


def multiplied(lhs, wide, matrix, blocks):
    rows = [matrix.at[pl.ds(128 * at, 128)] for at in blocks]
    take = lambda cols: jnp.concatenate([r[:, cols] for r in rows], axis=0)
    cut = lambda v, at: v[:, 128 * at : 128 * at + 128]
    if not wide:
        sums = dot(lhs[0], take(slice(0, 384)))
        return [cut(sums, k) for k in range(3)]
    tops, rests = dot(lhs[0], take(slice(0, 768))), dot(lhs[1], take(slice(0, 384)))
    return [cut(tops, k) + cut(tops, 3 + k) + cut(rests, k) for k in range(3)]


def line_sum(blocks, down, up):
    rows = blocks[0].shape[0]
    down[8 : rows + 8] = blocks[0]
    up[8 : rows + 8] = blocks[2]
    zeros = jnp.zeros((SIDE, 128), F32)
    for at in range(0, rows, 64):
        down[pl.ds(7 + at, SIDE, stride=8)] = zeros
        up[pl.ds(16 + at, SIDE, stride=8)] = zeros
    return down[7 : rows + 7] + blocks[1] + up[9 : rows + 9]


def clear_center(even, odd, wide):
    for part in range(2 if wide else 1):
        for px in (0, SIDE + 1):
            even[part, px] = jnp.zeros(even.shape[2:], BF16)
            odd[part, px] = jnp.zeros(odd.shape[2:], BF16)


def fill_center(brick, wide, even, odd):
    zeros = jnp.zeros((SIDE, 128), F32)
    for x in range(SIDE):
        middle = brick[64 * x : 64 * x + 64]
        for part, v in enumerate(pieces_of(jnp.concatenate([zeros, middle, zeros], axis=0), wide)):
            even[part, x + 1] = v
        for part, v in enumerate(pieces_of(middle, wide)):
            odd[part, x + 1] = v


def center(wide, even, odd, down, up, matrix, first, last):
    def taps(part):
        windows = []
        for i in range(3):
            for j in range(3):
                xs = slice(first + i, last + i)
                v = odd[part, xs] if j == 1 else even[part, xs, 8 * j : 8 * j + 64]
                windows.append(v.reshape((last - first) * 64, 128))
        return jnp.concatenate(windows, axis=1)

    lhs = [taps(part) for part in range(2 if wide else 1)]
    return line_sum(multiplied(lhs, wide, matrix, range(9)), down, up)


def fill_rims(load, link, wide, at, faces_even, faces_odd, edge, rims):
    found = {o: link(o) for o in columns}
    zeros = jnp.zeros((SIDE, 128), F32)

    def get(o, start, size=SIDE, stride=1):
        row, keep = found[o]
        return load(row, start, size, stride) * keep

    def put_face(face, lines):
        v = jnp.concatenate(lines, axis=0)
        for part, value in enumerate(pieces_of(v, wide)):
            faces_even[part, face, at] = value
        for part, value in enumerate(pieces_of(v[8:72], wide)):
            faces_odd[part, face, at] = value

    def put_rim(j, px, v):
        for part, value in enumerate(pieces_of(v, wide)):
            edge[part, j, at, px] = value

    for face, d in enumerate((-1, 1)):
        spot = SIDE - 1 if d < 0 else 0
        put_face(face, [get((d, -1, 0), 64 * spot + 56), get((d, 0, 0), 64 * spot, 64), get((d, 1, 0), 64 * spot)])
        lines = [get((0, d, 0), 64 * x + 8 * spot) for x in range(SIDE)]
        put_face(2 + face, [zeros] + lines + [zeros])
    fill_edges(get, rims, put_rim)


def add_rims(sums, n, wide, faces_even, faces_odd, edge, down, up, matrix):
    parts = range(2 if wide else 1)
    for face in range(4):
        side = 2 * (face % 2)
        blocks = [3 * side + t for t in range(3)] if face < 2 else [3 * t + side for t in range(3)]
        lhs = []
        for part in parts:
            windows = []
            for t in range(3):
                v = faces_odd[part, face] if t == 1 else faces_even[part, face, :, 8 * t : 8 * t + 64]
                windows.append(v.reshape(n * 64, 128))
            lhs.append(jnp.concatenate(windows, axis=1))
        total = line_sum(multiplied(lhs, wide, matrix, blocks), down, up)
        for b in range(n):
            if face < 2:
                sums[b, 224 * side : 224 * side + 64] += total[64 * b : 64 * b + 64]
            else:
                for x in range(SIDE):
                    at = 64 * x + 28 * side
                    sums[b, at : at + 8] += total[64 * b + 8 * x : 64 * b + 8 * x + 8]
    lhs = []
    for part in parts:
        windows = [edge[part, j, :, i : i + 8].reshape(n * 128, 128) for i in range(3) for j in range(3)]
        lhs.append(jnp.concatenate(windows, axis=1))
    ends = lambda at: jnp.concatenate([matrix[:, at : at + 128], matrix[:, at + 256 : at + 384]], axis=1)
    total = dot(lhs[0], ends(0))
    if wide:
        total = total + dot(lhs[0], ends(384)) + dot(lhs[1], ends(0))
    for b in range(n):
        for x in range(SIDE):
            at = 128 * b + 16 * x
            sums[b, pl.ds(64 * x, SIDE, stride=8)] += total[at : at + 8, 0:128]
            sums[b, pl.ds(64 * x + 7, SIDE, stride=8)] += total[at + 8 : at + 16, 128:256]


def surface_spots():
    spots = [(0, 0, 64, 1), (64, 448, 64, 1)]
    for x in range(1, 7):
        at = 128 + (x - 1) * 16
        spots += [(at, 64 * x, 8, 1), (at + 8, 64 * x + 56, 8, 1)]
    for x in range(1, 7):
        at = 224 + (x - 1) * 12
        spots += [(at, 64 * x + 8, 6, 8), (at + 6, 64 * x + 15, 6, 8)]
    return spots


def pack(get, wire):
    for at, start, size, stride in surface_spots():
        wire[at : at + size] = get(pl.ds(start, size, stride=stride) if stride > 1 else pl.ds(start, size))


def unpack(wire, brick):
    for at, start, size, stride in surface_spots():
        spot = pl.ds(start, size, stride=stride) if stride > 1 else pl.ds(start, size)
        brick[spot] = wire[at : at + size]


def unpack_pair(wire, scratch, first, second):
    a, b = doubled(wire)
    scratch[0] = parted(a)
    scratch[1] = parted(b)
    unpack(scratch.at[0], first)
    unpack(scratch.at[1], second)


def pool(v, scratch, wire):
    lines = v.reshape(4, 2, 4, 2, SIDE, 128)
    sums = (lines[:, 0, :, 0] + lines[:, 0, :, 1]) + (lines[:, 1, :, 0] + lines[:, 1, :, 1])
    scratch[...] = sums.reshape(128, 128)
    for z in range(4):
        halves = [
            scratch[pl.ds(64 * half + 2 * z, 8, stride=8)] + scratch[pl.ds(64 * half + 2 * z + 1, 8, stride=8)]
            for half in range(2)
        ]
        wire[8 * z : 8 * z + 8] = merged(*halves) * 0.125


def split_spot(octant, half, z):
    a, b, c = octant // 4, octant // 2 % 2, octant % 2
    return pl.ds(256 * b + 32 * (4 * a + 2 * half) + 4 * c + z, 8, stride=8)


def place_piece(wire, octant, brick):
    for half, v in enumerate(doubled(wire)):
        v = parted(v)
        for z in range(4):
            brick[split_spot(octant, half, z)] = v[8 * z : 8 * z + 8]


def take_pieces(brick, pieces):
    for octant in range(8):
        for z in range(4):
            halves = [brick[split_spot(octant, half, z)] for half in range(2)]
            pieces[octant, 8 * z : 8 * z + 8] = merged(*halves)


def swap_halves(v, split):
    first, second = (2, SIDE) if split else (SIDE, 2)
    return v.reshape(first, second, 32, 128).swapaxes(0, 1).reshape(VOX, 128)


def grow(piece, scratch):
    for half, v in enumerate(doubled(piece)):
        for z in range(4):
            rows = v[8 * z : 8 * z + 8]
            scratch[pl.ds(64 * half + 2 * z, 8, stride=8)] = rows
            scratch[pl.ds(64 * half + 2 * z + 1, 8, stride=8)] = rows
    lines = scratch[...].reshape(4, 1, 4, 1, SIDE, 128)
    return jnp.broadcast_to(lines, (4, 2, 4, 2, SIDE, 128)).reshape(VOX, 128)


def step_kernel(
    x_any, fine_links, own_codes, coarse_links, in_any, in_bias, down_weight, one_any, one_bias, two_any, two_bias,
    up_weight, out_any, out_bias,
    out,
    x, in_weight, one_weight, two_weight, out_weight, loads,
    matrix, last_matrix, one_matrix, two_matrix,
    even, odd, edge, wide_even, wide_odd, wide_edge, rims, shift_down, shift_up,
    faces_even, faces_odd, face_edge, wide_faces_even, wide_faces_odd, wide_face_edge, wide_sums,
    next_even, next_odd, over, tri_matrix, even_2, odd_2, edge_2, rims_2, down_2, up_2,
    parts, turned, hidden, halves, small, grown,
    x_send, x_halo, hidden_send, hidden_halo,
    code_block, codes, code_table, table, code_scalars, table_scalars,
    pooled, placed, base, first,
    first_send, first_halo, lifted, wanted, window, low_window, high_window,
    local_sems, send_x, recv_x, send_hidden, recv_hidden, send_codes, recv_codes, send_pooled, recv_pooled,
    send_first, recv_first, send_relay, recv_relay, send_wanted, recv_wanted,
):
    group, member = lax.axis_index("grp"), lax.axis_index("dev")
    groups, members = lax.axis_size("grp"), lax.axis_size("dev")
    position = group * members + member
    whole = groups * members
    count, slots = fine_links.shape[0], coarse_links.shape[0]
    pairs = count // 2
    relayed = members == 4
    has_left, has_right = position > 0, position < whole - 1
    has_low, has_high = group > 0, group < groups - 1
    is_first, is_last = member == 0, member == members - 1
    left_at = (jnp.maximum(position - 1, 0) // members, (position + members - 1) % members)
    right_at = (jnp.minimum(position + 1, whole - 1) // members, (position + 1) % members)
    low_at = (jnp.maximum(group - 1, 0), members - 1)
    high_at = (jnp.minimum(group + 1, groups - 1), 0)
    always = position >= 0

    def fetch(k, source, target):
        return pltpu.make_async_copy(source, target, loads.at[k])

    fetches = [
        fetch(0, x_any, x), fetch(1, in_any, in_weight), fetch(2, one_any, one_weight),
        fetch(3, two_any, two_weight), fetch(4, out_any, out_weight),
    ]
    for copy in fetches:
        copy.start()

    barrier = pltpu.get_barrier_semaphore()

    def greet(where):
        pl.semaphore_signal(barrier, inc=1, device_id=where, device_id_type=MESH)

    pl.when(has_left)(lambda: greet(left_at))
    pl.when(has_right)(lambda: greet(right_at))
    for k in range(1, members):
        greet((group, (member + k) % members))
    for k in range(members):
        pl.when(is_first & has_low)(lambda k=k: greet((low_at[0], k)))
        pl.when(is_last & has_high)(lambda k=k: greet((high_at[0], k)))

    def remote(src, dst, send, recv, where):
        return pltpu.make_async_remote_copy(
            src_ref=src, dst_ref=dst, send_sem=send, recv_sem=recv, device_id=where, device_id_type=MESH
        )

    row = lax.broadcasted_iota(jnp.int32, (SIDE, 128), 0)
    block = jnp.full((SIDE, 128), -1, jnp.int32)
    for i in range(count):
        block = jnp.where(row == i, own_codes[i], block)
    code_block[...] = block
    codes[members + member] = block
    fetches[0].wait()
    for pair in range(pairs):
        turned[pair] = x[2 * pair : 2 * pair + 2].reshape(128, VOX).T
    pack(lambda spot: turned[0, spot], x_send.at[0])
    pack(lambda spot: turned[pairs - 1, spot], x_send.at[1])
    pl.semaphore_wait(
        barrier,
        jnp.where(has_left, 1, 0) + jnp.where(has_right, 1, 0) + (members - 1)
        + jnp.where(has_low, 1, 0) + jnp.where(has_high, 1, 0),
    )

    def halo_copies(source, halo, send, recv, at=0, rows=SURFACE):
        spot = pl.ds(at, rows)
        to_left = remote(source.at[0, spot], halo.at[1, spot], send.at[0], recv.at[1], left_at)
        to_right = remote(source.at[1, spot], halo.at[0, spot], send.at[1], recv.at[0], right_at)
        return to_left, to_right

    def start_halo(copies):
        pl.when(has_left)(copies[0].start)
        pl.when(has_right)(copies[1].start)

    def end_halo(copies):
        pl.when(has_left)(copies[1].wait_recv)
        pl.when(has_right)(copies[0].wait_recv)

    def end_halo_sends(copies):
        pl.when(has_left)(copies[0].wait_send)
        pl.when(has_right)(copies[1].wait_send)

    def shared_copies(source, at, send, recv):
        near = [
            remote(source, at(members + member), send.at[k], recv.at[members + member], (group, (member + k) % members))
            for k in range(1, members)
        ]
        to_high = remote(source, at(member), send.at[0], recv.at[member], high_at)
        to_low = remote(source, at(2 * members + member), send.at[members], recv.at[2 * members + member], low_at)
        return near, to_high, to_low

    def start_shared(copies):
        near, to_high, to_low = copies
        for copy in near:
            copy.start()
        pl.when(has_high)(to_high.start)
        pl.when(has_low)(to_low.start)

    def end_near(source, at, send, recv):
        for k in range(1, members):
            other = (member + k) % members
            remote(source, at(members + other), send.at[k], recv.at[members + other], (group, other)).wait_recv()

    def end_far(source, at, send, recv):
        for k in range(members):
            from_low = remote(source, at(k), send.at[0], recv.at[k], low_at)
            from_high = remote(source, at(2 * members + k), send.at[0], recv.at[2 * members + k], high_at)
            pl.when(is_first & has_low)(from_low.wait_recv)
            pl.when(is_last & has_high)(from_high.wait_recv)

    def end_shared_sends(copies):
        near, to_high, to_low = copies
        for copy in near:
            copy.wait_send()
        pl.when(has_high)(to_high.wait_send)
        pl.when(has_low)(to_low.wait_send)

    x_copies = halo_copies(x_send, x_halo, send_x, recv_x)
    start_halo(x_copies)
    code_at = lambda k: codes.at[k]
    code_copies = shared_copies(code_block, code_at, send_codes, recv_codes)
    start_shared(code_copies)

    fetches[1].wait()
    fine_matrix(in_weight, matrix)
    for pair in range(pairs):
        for one, v in enumerate(doubled(turned[pair])):
            parts[HALO + 2 * pair + one] = parted(v)

    clear_center(even, odd, False)

    def own_step(i, carry):
        fill_center(parts.at[HALO + i], False, even, odd)
        hidden[i] = center(False, even, odd, shift_down, shift_up, matrix, 0, SIDE)
        return carry

    lax.fori_loop(0, count, own_step, 0)
    end_near(code_block, code_at, send_codes, recv_codes)
    end_far(code_block, code_at, send_codes, recv_codes)
    lane = lax.broadcasted_iota(jnp.int32, (SIDE, 128), 1)
    table_rows = jnp.full((SIDE, 128), -1, jnp.int32)
    for near in range(3):
        there = position + near - 1
        valid = (there >= 0) & (there < whole)
        there = jnp.where(valid, there, position)
        there_group = there // members
        there_member = there - there_group * members
        band = there_group - group + 1
        spot = jnp.where(valid, lane, -1000) + there_member * slots * 8
        best = jnp.full((SIDE, 128), -1, jnp.int32)
        for k in range(members):
            match = (codes[band * members + k] == spot) & (row < count) & (lane < slots * 8)
            best = jnp.maximum(best, jnp.where(match, (band * members + k) * count + row, -1))
        top = jnp.max(best, axis=0, keepdims=True)
        table_rows = jnp.where(row == near, top, table_rows)
    code_table[...] = codes[pl.ds(members, members)]
    table[...] = table_rows
    to_table = pltpu.make_async_copy(table, table_scalars, local_sems.at[0])
    to_codes = pltpu.make_async_copy(code_table, code_scalars, local_sems.at[1])
    to_table.start()
    to_codes.start()

    fine_start = position * count - HALO
    end_halo(x_copies)
    for side, at in ((0, 0), (1, HALO + count)):
        unpack_pair(x_halo[side], halves, parts.at[at], parts.at[at + 1])
    fine_scratch = (even.at[0], odd.at[0], edge, rims, shift_down, shift_up)
    two = lambda bias: jnp.concatenate([bias[...], bias[...]], axis=1)
    in_both = two(in_bias)

    def pooled_at(i):
        return lambda k: pooled.at[k, i]

    def pooled_copies(i):
        return shared_copies(pooled.at[members + member, i], pooled_at(i), send_pooled.at[i], recv_pooled.at[i])

    def first_step(pair, carry):
        at = 2 * pair
        for one in range(2):
            own = HALO + at + one
            fill_rims(
                loader(parts, own), linker(fine_links, at + one, fine_start, own, parts.shape[0]), False, one,
                faces_even, faces_odd, face_edge, rims,
            )
        sums = hidden.at[pl.ds(at, 2)]
        add_rims(sums, 2, False, faces_even, faces_odd, face_edge, shift_down, shift_up, matrix)
        for one in range(2):
            v = sums[one]
            v = silu(v + pltpu.roll(v, 64, 1) + in_both)
            pool(v, small, pooled.at[members + member, at + one])
            sums[one] = v
            start_shared(pooled_copies(at + one))
        return carry

    lax.fori_loop(0, pairs, first_step, 0)
    pack(lambda spot: merged(hidden[0, spot], hidden[1, spot]), hidden_send.at[0])
    pack(lambda spot: merged(hidden[count - 2, spot], hidden[count - 1, spot]), hidden_send.at[1])
    hidden_copies = [
        halo_copies(hidden_send, hidden_halo, send_hidden.at[part], recv_hidden.at[part], at, rows)
        for part, (at, rows) in enumerate(((0, EARLY), (EARLY, SURFACE - EARLY)))
    ]
    start_halo(hidden_copies[0])
    fetches[2].wait()
    coarse_matrix(one_weight, one_matrix)
    fetches[3].wait()
    coarse_matrix(two_weight, two_matrix)
    fetches[4].wait()
    fine_matrix(out_weight, last_matrix)
    packed_matrix(out_weight, tri_matrix)
    to_table.wait()
    to_codes.wait()

    turned_down = down_weight[...]
    down_high = high_of(turned_down)
    down_both = jnp.concatenate([down_high, turned_down - down_high], axis=1)
    down_matrix = jnp.concatenate([down_both, down_both], axis=0).astype(BF16)
    for i in range(count):
        end_near(pooled.at[members + member, i], pooled_at(i), send_pooled.at[i], recv_pooled.at[i])
    for i in range(count):
        end_far(pooled.at[members + member, i], pooled_at(i), send_pooled.at[i], recv_pooled.at[i])

    def base_of(near):
        for slot in range(slots):
            for octant in range(8):
                which = table_scalars[near, slot * 8 + octant]
                there_is = which >= 0
                which = jnp.where(there_is, jnp.minimum(which, 3 * members * count - 1), (members + member) * count)
                keep = jnp.where(there_is, 1.0, 0.0).astype(F32)
                place_piece(pooled[which // count, which % count] * keep, octant, placed.at[slot])
        sums = dot(placed[...].reshape(slots * VOX, 128).astype(BF16), down_matrix)
        sums = sums[:, 0:128] + sums[:, 128:256]
        for slot in range(slots):
            base[near * slots + slot] = swap_halves(sums[slot * VOX : slot * VOX + VOX], True)

    def base_step(t, carry):
        base_of(t)
        return carry

    lax.fori_loop(0, 3, base_step, 0)
    coarse_start = (position - 1) * slots
    wide_scratch = (wide_even, wide_odd, wide_edge, rims, shift_down, shift_up)

    if relayed:
        parity = member % 2
        x_at = (group, member + 1 - 2 * parity)
        relay_group = group + jnp.where(member == 1, -1, 0) + jnp.where(member == 2, 1, 0)
        relays_out = (relay_group >= 0) & (relay_group < groups)
        relays_in = jnp.where(is_first, has_low, True) & jnp.where(is_last, has_high, True)
        relay_at = (jnp.clip(relay_group, 0, groups - 1), (member + 2) % members)

        def direct(i, c):
            at, rows = CHUNKS[c]
            return remote(
                first_send.at[i, pl.ds(at, rows)], first_halo.at[parity, i, pl.ds(at, rows)],
                send_first.at[i, c], recv_first.at[i, c], x_at,
            )

        def came(i, c):
            at, rows = CHUNKS[c]
            return remote(
                first_send.at[i, pl.ds(at, rows)], first_halo.at[1 - parity, i, pl.ds(at, rows)],
                send_first.at[i, c], recv_first.at[i, c], x_at,
            )

        def relay(i, c):
            at, rows = CHUNKS[c]
            return remote(
                first_halo.at[1 - parity, i, pl.ds(at, rows)], first_halo.at[parity, i, pl.ds(at, rows)],
                send_relay.at[i, c], recv_relay.at[i, c], relay_at,
            )

        exists = jnp.where(parity == 0, has_left, has_right)
        far_at = tuple(jnp.where(parity == 0, a, b) for a, b in zip(left_at, right_at))

        def far(i, c):
            spot = pl.ds(*CHUNKS[c])
            return remote(
                first_send.at[i, spot], first_halo.at[1 - parity, i, spot],
                send_relay.at[i, c], recv_relay.at[i, c], far_at,
            )

        def start_first(i):
            for c in range(len(CHUNKS)):
                direct(i, c).start()
            for c in range(len(CHUNKS) - STRAIGHT, len(CHUNKS)):
                pl.when((i == slots - 1) & exists)(far(i, c).start)

        arrivals = [(i, c) for i in range(slots) for c in range(len(CHUNKS))]

        def pass_on(at):
            i, c = arrivals[at]
            came(i, c).wait_recv()
            if at < len(arrivals) - STRAIGHT:
                pl.when(relays_out)(relay(i, c).start)

        def end_first(passed):
            for at in range(passed, len(arrivals)):
                pass_on(at)
            for i in range(slots):
                for c in range(len(CHUNKS)):
                    pl.when(relays_in)(relay(i, c).wait_recv)

        def end_first_sends():
            for at, (i, c) in enumerate(arrivals):
                direct(i, c).wait_send()
                if at < len(arrivals) - STRAIGHT:
                    pl.when(relays_out)(relay(i, c).wait_send)
                else:
                    pl.when(exists)(far(i, c).wait_send)
    else:

        def sides(i):
            to_left = remote(first_send.at[i], first_halo.at[1, i], send_first.at[i, 0], recv_first.at[i, 1], left_at)
            to_right = remote(first_send.at[i], first_halo.at[0, i], send_first.at[i, 1], recv_first.at[i, 0], right_at)
            return to_left, to_right

        def start_first(i):
            start_halo(sides(i))

        def pass_on(at):
            pass

        def end_first(passed):
            for i in range(slots):
                end_halo(sides(i))

        def end_first_sends():
            for i in range(slots):
                end_halo_sends(sides(i))

    def second_step(i, carry):
        v = silu(coarse_conv(base, slots + i, coarse_start, coarse_links, i, wide_scratch, one_matrix) + one_bias[...])
        first[slots + i] = v
        pack(lambda spot: first[slots + i, spot], first_send.at[i])
        start_first(i)
        return carry

    lax.fori_loop(0, slots, second_step, 0)
    turned_up = up_weight[...].T
    up_high = high_of(turned_up)
    up_both = jnp.concatenate([up_high, turned_up - up_high], axis=1)
    up_matrix = jnp.concatenate([up_both, up_both], axis=0).astype(BF16)
    clear_center(wide_even, wide_odd, True)
    passed = 0
    for i in range(slots):
        fill_center(first.at[slots + i], True, wide_even, wide_odd)
        for half in range(2):
            pass_on(passed)
            passed += 1
            spot = slice(256 * half, 256 * half + 256)
            wide_sums[i, spot] = center(
                True, wide_even, wide_odd, shift_down, shift_up, two_matrix, 4 * half, 4 * half + 4
            )
    end_first(passed)
    start_halo(hidden_copies[1])
    for side, at in ((0, 0), (1, 2 * slots)):
        for i in range(slots):
            unpack(first_halo.at[side, i], first.at[at + i])

    def wide_rim_step(i, carry):
        fill_rims(
            loader(first, slots + i), linker(coarse_links, i, coarse_start, slots + i, first.shape[0]), True, i,
            wide_faces_even, wide_faces_odd, wide_face_edge, rims,
        )
        return carry

    lax.fori_loop(0, slots, wide_rim_step, 0)
    add_rims(
        wide_sums, slots, True, wide_faces_even, wide_faces_odd, wide_face_edge, shift_down, shift_up, two_matrix
    )

    def third_step(i, carry):
        v = silu(wide_sums[i] + two_bias[...])
        high = v.astype(BF16)
        low = (v - high.astype(F32)).astype(BF16)
        sums = dot(jnp.concatenate([high, low], axis=1), up_matrix)
        placed[0] = swap_halves(sums + pltpu.roll(sums, 64, 1), False)
        take_pieces(placed.at[0], lifted.at[pl.ds(i * 8, 8)])
        return carry

    lax.fori_loop(0, slots, third_step, 0)
    bricks = members * count
    zeros = jnp.zeros((HALO,) + wanted.shape[1:], F32)
    wanted[0:HALO] = zeros
    wanted[HALO + bricks :] = zeros

    def choose(j, carry):
        code = code_scalars[j // count, j % count, 0] - member * slots * 8
        mine = (code >= 0) & (code < slots * 8)
        keep = jnp.where(mine, 1.0, 0.0).astype(F32)
        wanted[HALO + j] = lifted[jnp.where(mine, code, 0)] * keep
        return carry

    lax.fori_loop(0, bricks, choose, 0)
    parts_of = ((HALO, count, None), (0, HALO, 0), (HALO + count, HALO, members - 1))

    def to_member(k, part):
        other = (member + k) % members
        at, rows, _ = parts_of[part]
        return remote(
            wanted.at[pl.ds(other * count + at, rows)], window.at[member, pl.ds(at, rows)], send_wanted.at[k, part],
            recv_wanted.at[members + member, part], (group, other),
        )

    def from_member(k, part):
        other = (member + k) % members
        at, rows, _ = parts_of[part]
        return remote(
            wanted.at[pl.ds(at, rows)], window.at[other, pl.ds(at, rows)], send_wanted.at[k, part],
            recv_wanted.at[members + other, part], (group, other),
        )

    def when_read(who, part, action):
        none_at = parts_of[part][2]
        if none_at is None:
            action()
        else:
            pl.when(who != none_at)(action)

    to_high = remote(
        wanted.at[pl.ds(bricks, HALO)], low_window.at[member], send_wanted.at[0, 0], recv_wanted.at[member, 0], high_at
    )
    to_low = remote(
        wanted.at[pl.ds(HALO, HALO)], high_window.at[member], send_wanted.at[members, 0],
        recv_wanted.at[2 * members + member, 0], low_at,
    )
    for k in range(1, members):
        to_member(k, 0).start()
    for k in range(1, members):
        for part in (1, 2):
            when_read((member + k) % members, part, to_member(k, part).start)
    pl.when(has_high)(to_high.start)
    pl.when(has_low)(to_low.start)
    window[member] = wanted[pl.ds(member * count, count + 2 * HALO)]
    for copies in hidden_copies:
        end_halo(copies)
    for k in range(1, members):
        from_member(k, 0).wait_recv()

    def total(source, i):
        piece = source[0, i]
        for owner in range(1, members):
            piece = piece + source[owner, i]
        return piece

    def own_blend(i, carry):
        rising = grow(total(window, HALO + i), small)
        parts[HALO + i] = parted(silu(hidden[i] + rising))
        return carry

    lax.fori_loop(0, count, own_blend, 0)
    for k in range(1, members):
        for part in (1, 2):
            when_read(member, part, from_member(k, part).wait_recv)
    for k in range(members):
        spot = wanted.at[pl.ds(0, HALO)]
        from_low = remote(spot, low_window.at[k], send_wanted.at[0, 0], recv_wanted.at[k, 0], low_at)
        from_high = remote(
            spot, high_window.at[k], send_wanted.at[0, 0], recv_wanted.at[2 * members + k, 0], high_at
        )
        pl.when(is_first & has_low)(from_low.wait_recv)
        pl.when(is_last & has_high)(from_high.wait_recv)
    for side, at, edge_window, beyond in (
        (0, 0, low_window, is_first), (1, HALO + count, high_window, is_last),
    ):
        for one in range(HALO):
            piece = jnp.where(beyond, total(edge_window, one), total(window, at + one))
            grown[one] = grow(piece, small)
        pack(lambda spot: merged(grown[0, spot], grown[1, spot]), halves.at[0])
        wire = silu(hidden_halo[side] + halves[0])
        unpack_pair(wire, halves, parts.at[at], parts.at[at + 1])
    out_both = two(out_bias)

    def last_step(pair, carry):
        at = 2 * pair
        first_sums, second_sums = (
            packed_conv(
                parts, HALO + at + one, fine_start, fine_links, at + one,
                (even_2.at[one], odd_2.at[one], edge_2.at[one], rims_2.at[one], down_2.at[one], up_2.at[one]),
                (next_even.at[one], next_odd.at[one], over.at[one]), tri_matrix, last_matrix,
            )
            for one in range(2)
        )
        flat = (merged(first_sums, pltpu.roll(second_sums, 64, 1)) + out_both).T
        out[pl.ds(at, 2)] = x[pl.ds(at, 2)] + flat.reshape(2, 64, VOX)
        return carry

    lax.fori_loop(0, pairs, last_step, 0)

    end_halo_sends(x_copies)
    end_shared_sends(code_copies)
    for i in range(count):
        end_shared_sends(pooled_copies(i))
    for copies in hidden_copies:
        end_halo_sends(copies)
    end_first_sends()
    for k in range(1, members):
        to_member(k, 0).wait_send()
        for part in (1, 2):
            when_read((member + k) % members, part, to_member(k, part).wait_send)
    pl.when(has_high)(to_high.wait_send)
    pl.when(has_low)(to_low.wait_send)


def per_device(
    x, fine_links, parent_codes, coarse_links,
    in_weight, in_bias, down, one_weight, one_bias, two_weight, two_bias, up, out_weight, out_bias,
):
    count, channels = x.shape[0], x.shape[1]
    slots, wide = coarse_links.shape[0], one_bias.shape[0]
    members = lax.axis_size("dev")
    row = lambda bias: bias.reshape(1, -1)
    vmem = pl.BlockSpec(memory_space=pltpu.VMEM)
    smem = pl.BlockSpec(memory_space=pltpu.SMEM)
    anywhere = pl.BlockSpec(memory_space=pl.ANY)
    floats = lambda *shape: pltpu.VMEM(shape, F32)
    halfs = lambda *shape: pltpu.VMEM(shape, BF16)
    ints = lambda *shape: pltpu.VMEM(shape, jnp.int32)
    sems = lambda *shape: pltpu.SemaphoreType.DMA(shape)
    span = count + 2 * HALO
    wire = (32, 128)
    scratch = [
        floats(*x.shape), floats(*in_weight.shape), floats(*one_weight.shape), floats(*two_weight.shape),
        floats(*out_weight.shape), sems(5),
        halfs(1152, 384), halfs(1152, 384), halfs(1152, 768), halfs(1152, 768),
        halfs(1, 10, 80, 128), halfs(1, 10, 64, 128), halfs(3, 10, 16, 128),
        halfs(2, 10, 80, 128), halfs(2, 10, 64, 128), halfs(2, 3, 10, 16, 128),
        floats(2, 10 * LINE, 128), floats(VOX + 16, 128), floats(VOX + 16, 128),
        halfs(1, 4, 2, 80, 128), halfs(1, 4, 2, 64, 128), halfs(1, 3, 2, 10, 16, 128),
        halfs(2, 4, slots, 80, 128), halfs(2, 4, slots, 64, 128), halfs(2, 3, slots, 10, 16, 128),
        floats(slots, VOX, 128),
        halfs(2, 10, 80, 128), halfs(2, 10, 64, 128), halfs(2, 10, 64, 128), halfs(1792, 256),
        halfs(2, 10, 80, 128), halfs(2, 10, 64, 128), halfs(2, 3, 10, 16, 128),
        floats(2, 2, 10 * LINE, 128), floats(2, VOX + 16, 128), floats(2, VOX + 16, 128),
        floats(span, VOX, 128), floats(count // 2, VOX, 128), floats(count, VOX, 128),
        floats(2, SURFACE, 128), floats(128, 128), floats(HALO, VOX, 128),
        floats(2, SURFACE, 128), floats(2, SURFACE, 128), floats(2, SURFACE, 128), floats(2, SURFACE, 128),
        ints(8, 128), ints(3 * members, 8, 128), ints(members, 8, 128), ints(8, 128),
        pltpu.SMEM((members, 8, 128), jnp.int32), pltpu.SMEM((8, 128), jnp.int32),
        floats(3 * members, count, *wire), floats(slots, VOX, 128), floats(3 * slots, VOX, 128), floats(3 * slots, VOX, 128),
        floats(slots, SURFACE, 128), floats(2, slots, SURFACE, 128), floats(slots * 8, *wire),
        floats(members * count + 2 * HALO, *wire), floats(members, span, *wire), floats(members, HALO, *wire),
        floats(members, HALO, *wire),
        sems(2), sems(2), sems(2), sems(2, 2), sems(2, 2), sems(members + 1), sems(3 * members),
        sems(count, members + 1), sems(count, 3 * members),
        sems(slots, 3), sems(slots, 3), sems(slots, 3), sems(slots, 3), sems(members + 1, 3), sems(3 * members, 3),
    ]
    return pl.pallas_call(
        step_kernel,
        out_shape=jax.ShapeDtypeStruct(x.shape, F32),
        in_specs=[anywhere, smem, smem, smem, anywhere, vmem, vmem, anywhere, vmem, anywhere, vmem, vmem, anywhere, vmem],
        out_specs=vmem,
        scratch_shapes=scratch,
        name="step",
        compiler_params=pltpu.CompilerParams(collective_id=1, has_side_effects=True, vmem_limit_bytes=LIMIT),
    )(
        x, fine_links, parent_codes, coarse_links, in_weight, row(in_bias), down.T, one_weight, row(one_bias),
        two_weight, row(two_bias), up, out_weight, row(out_bias),
    )


def solution(mesh):
    bricks = P(("grp", "dev"), None, None)
    rows = P(("grp", "dev"), None)
    placed = (bricks, rows, P(("grp", "dev")), rows) + (P(),) * 10
    return jax.shard_map(per_device, mesh=mesh, in_specs=placed, out_specs=bricks, check_vma=False)
```
